32 devices in a mesh: head: 4 (over y, x), seq: 8 (over z, core).
Axes of the slice: x: 2, y: 2, z: 4, core: 2. Of those that a mesh axis runs over, the one named last changes fastest.
Arguments:
- tokens: bfloat16 [4, 2048, 1024], P('head', 'seq'), may hold values from -6 to 6
- doc_ids: int32 [4, 2048], P('head', 'seq'), may hold values from 0 to 7, never falling along the last dimension, each value on 1 to 512 neighbouring positions
- query_weight: bfloat16 [1024, 256], P('seq', 'head'), may hold values from -0.1875 to 0.1875
- key_weight: bfloat16 [1024, 256], P('seq', 'head'), may hold values from -0.1875 to 0.1875
- value_weight: bfloat16 [1024, 1024], P('seq', 'head'), may hold values from -0.1875 to 0.1875
- out_weight: bfloat16 [1024, 1024], P('head', 'seq'), may hold values from -2 to 2
- gate_weight: bfloat16 [1024, 2752], P('seq', 'head'), may hold values from -0.1875 to 0.1875
- up_weight: bfloat16 [1024, 2752], P('seq', 'head'), may hold values from -0.1875 to 0.1875
- down_weight: bfloat16 [2752, 1024], P('head', 'seq'), may hold values from -0.109375 to 0.109375
- mix_gain: bfloat16 [1024], P(('head', 'seq')), may hold values from 0.25 to 1.75
- mlp_gain: bfloat16 [1024], P(('head', 'seq')), may hold values from 0.25 to 1.75
- cotangent: bfloat16 [4, 2048, 1024], P('head', 'seq'), may hold values from -6 to 6
Outputs:
- output: bfloat16 [4, 2048, 1024], P('head', 'seq')
- grad_tokens: float32 [4, 2048, 1024], P('head', 'seq')
- grad_query: float32 [1024, 256], P('seq', 'head')
- grad_key: float32 [1024, 256], P('seq', 'head')
- grad_value: float32 [1024, 1024], P('seq', 'head')
- grad_out: float32 [1024, 1024], P('head', 'seq')
- grad_gate: float32 [1024, 2752], P('seq', 'head')
- grad_up: float32 [1024, 2752], P('seq', 'head')
- grad_down: float32 [2752, 1024], P('head', 'seq')
- grad_mixgain: float32 [1024], P(('head', 'seq'))
- grad_mlpgain: float32 [1024], P(('head', 'seq'))
The draws below stay inside these ranges and needn't reach their ends.
Inputs may be any that keep to these rules, and one draw needn't show every extreme that they name: `doc_ids`: within each sequence the document numbers never fall; no document is longer than 512 positions, and in each sequence one is exactly that long.
All inputs are finite; a program needn't handle non-finite values.
Results may differ from the reference program's by a relative error of at most 0.019.
Values may be sent and summed in bfloat16 or wider, within the bound.
No kernel may reach another device: no remote copies, remote signals or barrier semaphores. Data moves between devices by JAX's collectives and lax.ppermute only.
A program may use at most 320 MiB of HBM per device.

```python
import math
import jax
import jax.numpy as jnp
import numpy as np
from jax import lax

D = 1024
HEADS = 16
FDIM = 16
VDIM = 64
FF = 2752
SPAN = 256
DOCS = 8
SEQS = 4
LENGTH = 2048


def with_spikes(values, own_key, source, target, blocks, factor):
    owner, partner = [(jnp.arange(values.shape[dim]) // (values.shape[dim] // blocks)).reshape([-1 if axis == dim else 1 for axis in range(values.ndim)]) for dim in (source, target)]
    chosen = jax.random.permutation(own_key, blocks)[partner]
    strong = (owner == chosen) | (owner == (partner + blocks // 2) % blocks)
    return jnp.where(strong, factor * values, values)


def steps_of(rng, dims, shards, least, top_value):
    def one(dim, blocks):
        heights = jax.random.uniform(jax.random.fold_in(jax.random.fold_in(rng, 6), dim), (blocks,), jnp.float32, least / len(shards), top_value / len(shards))
        return jnp.repeat(jnp.exp(heights), dims[dim] // blocks).reshape((-1,) + (1,) * (len(dims) - dim - 1))

    loudness = one(*shards[0])
    for cut in shards[1:]:
        loudness = loudness * one(*cut)
    return loudness


def split_up(amount, total, most, lean):
    loads = [(1 << 20) // math.isqrt(grade ** lean) + 1 for grade in range(2, amount + 1)]
    surplus, holding = total - most - (amount - 1), [1] * (amount - 1)
    while surplus > 0:
        movable = [i for i in range(amount - 1) if holding[i] < most]
        whole, remaining = sum([loads[i] for i in movable]), surplus
        for i in movable:
            addition = min(most - holding[i], max(1, remaining * loads[i] // whole), surplus)
            holding[i] = holding[i] + addition
            surplus = surplus - addition
    return np.array([most] + holding)


def uneven_parts(own_key, amount, total, reach, slope):
    if amount == 2:
        one = jax.random.randint(own_key, (), max(1, total - reach), min(reach, total - 1) + 1)
        return jnp.stack([one, total - one])
    tallies = jnp.asarray(split_up(amount, total, reach, slope), jnp.int32)
    twos = (amount - 1) // 2
    giver, receiver = tallies[1:1 + 2 * twos:2], tallies[2:2 + 2 * twos:2]
    room = jnp.minimum(giver - 1, reach - receiver)
    shifted = jax.random.randint(jax.random.fold_in(own_key, 1), (twos,), 0, 1 << 20) % (room + 1)
    tallies = tallies.at[1:1 + 2 * twos:2].set(giver - shifted).at[2:2 + 2 * twos:2].set(receiver + shifted)
    return tallies[jax.random.permutation(jax.random.fold_in(own_key, 2), amount)]


def noise(own_key, extent, scale, limit, shards=(), kind=jnp.bfloat16):
    values = jax.random.normal(own_key, extent, jnp.float32) * scale
    if len(shards) > 0:
        values = steps_of(own_key, extent, shards, -0.22, 0.18) * values
    return jnp.clip(values, min=-limit, max=limit).astype(kind)


def gaussian_with(rng, shape, width, reach, split, heavy, kind=jnp.bfloat16):
    array = width * jax.random.normal(rng, shape, jnp.float32)
    if split:
        array = array * steps_of(rng, shape, split, -0.22, 0.18)
    return jnp.clip(with_spikes(array, jax.random.fold_in(rng, 3), *heavy), -reach, reach).astype(kind)


def setup_inputs(seed: int = 0) -> dict:
    key_of = jax.random.split(jax.random.key(seed), 13)
    return {
        "tokens": noise(key_of[0], (SEQS, LENGTH, D), 1.0, 6.0, ((0, 4), (1, 8))),
        "doc_ids": jax.vmap(lambda own: jnp.searchsorted(jnp.cumsum(uneven_parts(own, DOCS, LENGTH, LENGTH // 4, 0)), jnp.arange(LENGTH), side="right"))(jax.random.split(key_of[1], SEQS)).reshape((SEQS, LENGTH)).astype(jnp.int32),
        "query_weight": noise(key_of[2], (D, HEADS * FDIM), D ** -0.5, 0.1875, ((0, 8), (1, 4))),
        "key_weight": noise(key_of[3], (D, HEADS * FDIM), D ** -0.5, 0.1875, ((0, 8), (1, 4))),
        "value_weight": noise(key_of[4], (D, HEADS * VDIM), D ** -0.5, 0.1875, ((0, 8), (1, 4))),
        "out_weight": noise(key_of[5], (HEADS * VDIM, D), (D // 128) ** -0.5, 2.0, ((0, 4), (1, 8))),
        "gate_weight": noise(key_of[6], (D, FF), D ** -0.5, 0.1875, ((0, 8), (1, 4))),
        "up_weight": noise(key_of[7], (D, FF), D ** -0.5, 0.1875, ((0, 8), (1, 4))),
        "down_weight": noise(key_of[8], (FF, D), FF ** -0.5, 0.109375, ((0, 4), (1, 8))),
        "mix_gain": jnp.clip(1.0 + 0.15 * jax.random.normal(key_of[9], (D,), jnp.float32), 0.25, 1.75).astype(jnp.bfloat16),
        "mlp_gain": jnp.clip(1.0 + 0.15 * jax.random.normal(key_of[10], (D,), jnp.float32), 0.25, 1.75).astype(jnp.bfloat16),
        "cotangent": gaussian_with(key_of[11], (SEQS, LENGTH, D), 1.0, 6.0, ((0, 4), (1, 8)), (1, 2, 8, 2.0)),
    }


@jax.custom_vjp
def low(v):
    return lax.optimization_barrier(v.astype(jnp.bfloat16)).astype(jnp.float32)

@jax.custom_vjp
def low_back(v):
    return v

def low_keep(v):
    return (low(v), None)

def low_pass(kept, grad):
    return (grad,)

def back_keep(v):
    return (v, None)

def back_low(kept, grad):
    return (low(grad),)
low.defvjp(low_keep, low_pass)
low_back.defvjp(back_keep, back_low)
EPS = 1e-06
ROOT_HALF = 0.7071067811865476
HIGH = lax.Precision.HIGHEST

def features(values):
    half = values * 0.5
    lead = values.shape[:-1]
    square = (half[..., :, None] * half[..., None, :]).reshape(lead + (FDIM * FDIM,)) * ROOT_HALF
    return jnp.concatenate([jnp.ones(lead + (1,), values.dtype), half, square], axis=-1)

def rms_scale(values):
    return lax.rsqrt(lax.optimization_barrier(jnp.mean(values * values, axis=-1, keepdims=True)) + EPS)

def attend(queries, keys, values, segment):
    blocks = LENGTH // SPAN
    ftype = queries.dtype
    qblock = queries.reshape(blocks, SPAN, HEADS, FDIM)
    kblock = keys.reshape(blocks, SPAN, HEADS, FDIM)
    vblock = values.reshape(blocks, SPAN, HEADS, VDIM)
    sblock = segment.reshape(blocks, SPAN)
    scores = low_back(jnp.einsum('bihf,bjhf->bhij', qblock, kblock, precision=HIGH) * 0.25)
    place = jnp.arange(SPAN)
    causal = place[:, None] >= place[None, :]
    same = sblock[:, :, None] == sblock[:, None, :]
    mask = (causal[None] & same)[:, None].astype(ftype)
    weights = low((1.0 + scores + 0.5 * scores * scores) * mask)
    final = sblock[:, -1]
    tail = (sblock == final[:, None]).astype(ftype)
    phik = features(kblock)
    phiq = features(qblock)
    tail_state = jnp.einsum('bjhf,bjhe->bhfe', phik * tail[:, :, None, None], vblock, precision=HIGH)
    tail_norm = jnp.einsum('bjhf,bj->bhf', phik, tail, precision=HIGH)
    label = jnp.concatenate([jnp.full((1,), -1, jnp.int32), final[:-1].astype(jnp.int32)])
    index = jnp.arange(blocks)
    joined = ((index[None, :] < index[:, None]) & (final[None, :] == label[:, None])).astype(ftype)
    carry_state = jnp.einsum('cb,bhfe->chfe', joined, tail_state, precision=HIGH)
    carry_norm = jnp.einsum('cb,bhf->chf', joined, tail_norm, precision=HIGH)
    live = (sblock == label[:, None]).astype(ftype)
    numer = jnp.einsum('bhij,bjhe->bihe', weights, vblock, precision=HIGH)
    numer = numer + live[:, :, None, None] * jnp.einsum('bihf,bhfe->bihe', phiq, carry_state, precision=HIGH)
    denom = jnp.swapaxes(lax.optimization_barrier(jnp.sum(weights, axis=-1)), 1, 2)
    denom = denom + live[:, :, None] * jnp.einsum('bihf,bhf->bih', phiq, carry_norm, precision=HIGH)
    numer = low_back(numer)
    mixed = low_back(low(numer / denom[..., None]))
    return mixed.reshape(LENGTH, HEADS * VDIM)

def forward(inputs, segment, params):
    query_full, key_full, value_full, out_full, gate_full, up_full, down_full, gain_first, gain_second = params
    normed = inputs * rms_scale(inputs)
    inner = low(normed * gain_first)
    queries = low_back(low(jnp.dot(inner, query_full, precision=HIGH, preferred_element_type=jnp.float32)))
    keys = low_back(low(jnp.dot(inner, key_full, precision=HIGH, preferred_element_type=jnp.float32)))
    values = low_back(low(jnp.dot(inner, value_full, precision=HIGH, preferred_element_type=jnp.float32)))
    mixed = attend(queries, keys, values, segment)
    middle = inputs + low_back(jnp.dot(mixed, out_full, precision=HIGH, preferred_element_type=jnp.float32))
    normed_two = middle * rms_scale(middle)
    inner_two = low(normed_two * gain_second)
    gate = low_back(jnp.dot(inner_two, gate_full, precision=HIGH, preferred_element_type=jnp.float32))
    up = low_back(jnp.dot(inner_two, up_full, precision=HIGH, preferred_element_type=jnp.float32))
    hidden = low(jax.nn.silu(gate) * up)
    return middle + low_back(jnp.dot(hidden, down_full, precision=HIGH, preferred_element_type=jnp.float32))

def reference(tokens, doc_ids, query_weight, key_weight, value_weight, out_weight, gate_weight, up_weight, down_weight, mix_gain, mlp_gain, cotangent):
    params = tuple((w.astype(jnp.float32) for w in (query_weight, key_weight, value_weight, out_weight, gate_weight, up_weight, down_weight, mix_gain, mlp_gain)))

    def step(totals, item):
        seq_tokens, seq_ids, seq_cot = item

        def run(inputs, *weights_in):
            return forward(inputs, seq_ids, weights_in)
        result, pull = jax.vjp(run, seq_tokens.astype(jnp.float32), *params)
        grads = pull(seq_cot.astype(jnp.float32))
        totals = tuple((a + g for a, g in zip(totals, grads[1:])))
        return (totals, (result.astype(jnp.bfloat16), grads[0]))
    start = tuple((jnp.zeros(w.shape, jnp.float32) for w in params))
    totals, stacked = lax.scan(step, start, (tokens, doc_ids, cotangent))
    return (stacked[0], stacked[1], totals[0], totals[1], totals[2], totals[3], totals[4], totals[5], totals[6], totals[7], totals[8])
```

```python
import functools

import jax
import jax.numpy as jnp
from jax import lax
from jax.experimental import pallas as pl
from jax.experimental.pallas import tpu as pltpu
from jax.sharding import PartitionSpec as P

FDIM = 16
VDIM = 64
EPS = 1e-06
ROOT_HALF = 0.7071067811865476
FROWS = 11 * FDIM
F32 = jnp.float32
BF16 = jnp.bfloat16
VMEM_BYTES = 56 * 1024 * 1024

NN = (((1,), (0,)), ((), ()))
NT = (((1,), (1,)), ((), ()))
TN = (((0,), (0,)), ((), ()))


def mm(a, b, dims=NN):
    return lax.dot_general(a, b, dims, preferred_element_type=F32)


def call(body, outs, ins, grid=None, in_specs=None, out_specs=None, scratch=(), flops=0):
    nbytes = sum(x.size * x.dtype.itemsize for x in jax.tree.leaves((ins, outs)))
    kwargs = {}
    if grid is not None:
        kwargs = dict(grid=grid, in_specs=in_specs, out_specs=out_specs)
    return pl.pallas_call(
        body,
        out_shape=outs,
        scratch_shapes=list(scratch),
        compiler_params=pltpu.CompilerParams(vmem_limit_bytes=VMEM_BYTES),
        cost_estimate=pl.CostEstimate(flops=flops, bytes_accessed=nbytes, transcendentals=0),
        **kwargs,
    )(*ins)


def sds(shape, dtype):
    return jax.ShapeDtypeStruct(shape, dtype)


def whole(shape):
    return pl.BlockSpec(shape, lambda r: (0,) * len(shape))


def by_row(shape):
    return pl.BlockSpec((1,) + tuple(shape), lambda r: (r,) + (0,) * len(shape))


def coef(d):
    return ROOT_HALF if d in (0, FDIM // 2) else 1.0


def features(w):
    half = w * 0.5
    rows = [half]
    for d in range(FDIM // 2 + 1):
        other = half if d == 0 else pltpu.roll(half, FDIM - d, 0)
        rows.append(half * other * coef(d))
    first = lax.broadcasted_iota(jnp.int32, half.shape, 0) == 0
    rows.append(jnp.where(first, 1.0, 0.0))
    return jnp.concatenate(rows, axis=0)


def features_back(w, grad):
    half = w * 0.5
    total = grad[:FDIM]
    for d in range(FDIM // 2 + 1):
        part = grad[FDIM * (d + 1) : FDIM * (d + 2)]
        if d == 0:
            total = total + part * half * (2.0 * coef(0))
        else:
            near = part * pltpu.roll(half, FDIM - d, 0)
            far = pltpu.roll(part * half, d, 0)
            total = total + (near + far) * coef(d)
    return total * 0.5


def lanes(shape):
    return lax.broadcasted_iota(jnp.int32, shape, len(shape) - 1)


def one_hot_lanes(rows, index):
    lane = lanes((rows, 128))
    return jnp.where(lane == index, 1.0, 0.0).astype(BF16)


def own_half(x, j, other=None):
    left = lanes(x.shape) < VDIM
    keep = left if j == 0 else jnp.logical_not(left)
    return jnp.where(keep, x, jnp.zeros_like(x) if other is None else other)


def pick_columns(z, column, spots):
    row = lax.broadcasted_iota(jnp.int32, (128, 128), 0)
    hot = jnp.where(column(row), 1.0, 0.0) * jnp.where(spots(lanes((128, 128))), 1.0, 0.0)
    return mm(z, hot.astype(BF16))


def doc_mask(masks, rows):
    seg = masks[0:1, :]
    col = jnp.transpose(masks)[:, 0:1]
    causal = lax.broadcasted_iota(jnp.int32, (rows, rows), 0) >= lax.broadcasted_iota(
        jnp.int32, (rows, rows), 1
    )
    return jnp.logical_and(causal, col == seg)


def with_pair(z, j):
    lane = lanes(z.shape)
    base = VDIM if j == 0 else 0
    high = z.astype(BF16)
    low = (z - high.astype(F32)).astype(BF16)
    zero = jnp.zeros_like(high)
    return jnp.where(lane == base, high, jnp.where(lane == base + 1, low, zero))


def with_ones(x, j):
    lane = lanes(x.shape)
    base = VDIM if j == 0 else 0
    hot = jnp.where(jnp.logical_or(lane == base, lane == base + 1), 1.0, 0.0).astype(x.dtype)
    return own_half(x, j, hot)


def project_body(x_ref, gain_ref, w_ref, masks_ref, h1_ref, qk_ref, v_ref, p_ref, z_ref, wt_ref):
    r = pl.program_id(0)
    heads = qk_ref.shape[1] // (2 * FDIM)
    nb, _, wb = w_ref.shape

    @pl.when(r == 0)
    def _():
        for s in range(nb):
            wt_ref[:, s * wb : (s + 1) * wb] = w_ref[s]
        z_ref[...] = jnp.zeros_like(z_ref)

    x = x_ref[0].astype(F32)
    normed = x * lax.rsqrt(jnp.mean(x * x, axis=-1, keepdims=True) + EPS)
    h1 = (normed * gain_ref[0:1, :]).astype(BF16)
    h1_ref[0] = h1
    nqk = qk_ref.shape[1]
    qk = mm(wt_ref[:nqk, :], h1, NT).astype(BF16)
    qk_ref[0] = qk
    v = mm(h1, wt_ref[nqk:, :], NT).astype(BF16)
    v_ref[0] = v
    tail = masks_ref[0, 1:2, :]
    rows = v.shape[0]
    for pair in range(heads // 2):
        v_pair = v[:, pair * 128 : (pair + 1) * 128]
        both = []
        for j in range(2):
            i = 2 * pair + j
            k = qk[nqk // 2 + i * FDIM : nqk // 2 + (i + 1) * FDIM].astype(F32)
            phi = (features(k) * tail).astype(BF16)
            rhs = jnp.concatenate([v_pair, one_hot_lanes(rows, r * heads + i)], axis=1)
            res = mm(phi, rhs)
            both.append(res[:, :128])
            z_ref[...] += res[:, 128:]
        p_ref[r * (heads // 2) + pair] = own_half(both[0], 0, both[1]).astype(BF16)

    @pl.when(r == pl.num_programs(0) - 1)
    def _():
        p_ref[p_ref.shape[0] - 1] = z_ref[...].astype(BF16)


def project(x, gain, w, masks, heads):
    n, rows, d = x.shape
    nb, total, wb = w.shape
    nqk, nv = 2 * heads * FDIM, heads * VDIM
    pieces = n * heads // 2 + 1
    return call(
        project_body,
        (
            sds((n, rows, d), BF16),
            sds((n, nqk, rows), BF16),
            sds((n, rows, nv), BF16),
            sds((pieces, FROWS, 128), BF16),
        ),
        (x, gain, w, masks),
        grid=(n,),
        in_specs=[by_row((rows, d)), whole(gain.shape), whole(w.shape), by_row(masks.shape[1:])],
        out_specs=[
            by_row((rows, d)),
            by_row((nqk, rows)),
            by_row((rows, nv)),
            whole((pieces, FROWS, 128)),
        ],
        scratch=[pltpu.VMEM((FROWS, 128), F32), pltpu.VMEM((nqk + nv, d), BF16)],
        flops=2 * n * rows * d * (nqk + nv),
    )


def local_body(qk_ref, v_ref, masks_ref, nd_ref):
    nqk = qk_ref.shape[1]
    heads = nqk // (2 * FDIM)
    rows = v_ref.shape[1]
    mask = doc_mask(masks_ref[0], rows)
    for pair in range(heads // 2):
        v_pair = v_ref[0, :, pair * 128 : (pair + 1) * 128]
        acc = None
        for j in range(2):
            i = 2 * pair + j
            q = qk_ref[0, i * FDIM : (i + 1) * FDIM, :]
            k = qk_ref[0, nqk // 2 + i * FDIM : nqk // 2 + (i + 1) * FDIM, :]
            s1 = mm(q, k, TN) * 0.25 + 1.0
            a = jnp.where(mask, 0.5 * s1 * s1 + 0.5, 0.0).astype(BF16)
            ones = own_half(jnp.ones((rows, 128), BF16), j)
            part = mm(a, jnp.concatenate([own_half(v_pair, j), ones], axis=1))
            acc = part if acc is None else acc + part
        nd_ref[0, pair] = acc


def local(qk, v, masks):
    n, nqk, rows = qk.shape
    heads = nqk // (2 * FDIM)
    return call(
        local_body,
        sds((n, heads // 2, rows, 256), F32),
        (qk, v, masks),
        grid=(n,),
        in_specs=[by_row(qk.shape[1:]), by_row(v.shape[1:]), by_row(masks.shape[1:])],
        out_specs=by_row((heads // 2, rows, 256)),
        flops=n * heads * rows * rows * 600,
    )


def joined(first, second, flag):
    return first.astype(F32) + second.astype(F32) * flag


def lane_flags(masks_ref, row, n, heads):
    lane = lanes((1, 128)) % (n * heads) // heads
    flag = jnp.zeros((1, 128), F32)
    for r in range(n):
        flag = jnp.where(lane == r, masks_ref[r, row : row + 1, 0:128], flag)
    return flag


def carry_body(nd_ref, qk_ref, masks_ref, one_ref, two_ref, o_ref, on_ref, inv_ref, c_ref):
    r = pl.program_id(0)
    n = pl.num_programs(0)
    nqk = qk_ref.shape[1]
    heads = nqk // (2 * FDIM)
    last = one_ref.shape[0] - 1

    @pl.when(r == 0)
    def _():
        flag = lane_flags(masks_ref, 3, masks_ref.shape[0], heads)
        c_ref[last] = joined(one_ref[last], two_ref[last], flag).astype(BF16)

    flag = masks_ref[r, 3:4, 0:128]
    live = masks_ref[r, 2:3, :]
    for pair in range(heads // 2):
        at = r * (heads // 2) + pair
        c = joined(one_ref[at], two_ref[at], flag).astype(BF16)
        c_ref[at] = c
        acc = nd_ref[0, pair]
        for j in range(2):
            i = 2 * pair + j
            q = qk_ref[0, i * FDIM : (i + 1) * FDIM, :].astype(F32)
            phi = (features(q) * live).astype(BF16)
            z = pick_columns(
                c_ref[last],
                lambda row: row == r * heads + i,
                lambda lane: (lane < VDIM) if j == 0 else (lane >= VDIM),
            ).astype(BF16)
            acc = acc + mm(phi, jnp.concatenate([own_half(c, j), z], axis=1), TN)
        inv = 1.0 / acc[:, 128:]
        on = acc[:, :128] * inv
        cols = slice(pair * 128, (pair + 1) * 128)
        o_ref[0, :, cols] = on.astype(BF16)
        on_ref[0, :, cols] = on
        inv_ref[0, :, cols] = inv


def carry(nd, qk, masks, one, two):
    n, nqk, rows = qk.shape
    heads = nqk // (2 * FDIM)
    nv = heads * VDIM
    return call(
        carry_body,
        (sds((n, rows, nv), BF16), sds((n, rows, nv), F32), sds((n, rows, nv), F32), sds(one.shape, BF16)),
        (nd, qk, masks, one, two),
        grid=(n,),
        in_specs=[
            by_row(nd.shape[1:]),
            by_row(qk.shape[1:]),
            whole(masks.shape),
            whole(one.shape),
            whole(two.shape),
        ],
        out_specs=[by_row((rows, nv)), by_row((rows, nv)), by_row((rows, nv)), whole(one.shape)],
        flops=n * heads * rows * 1000 * 256,
    )


def middle_body(x_ref, o_ref, wo_ref, gain_ref, y1_ref, h2_ref, wide_ref):
    n, nb, _, wb = wo_ref.shape
    acc = x_ref[...].astype(F32)
    for r in range(n):
        for s in range(nb):
            wide_ref[:, s * wb : (s + 1) * wb] = wo_ref[r, s]
        acc = acc + mm(o_ref[r], wide_ref[...])
    y1_ref[...] = acc
    scale = lax.rsqrt(jnp.mean(acc * acc, axis=-1, keepdims=True) + EPS)
    h2_ref[...] = (acc * scale * gain_ref[0:1, :]).astype(BF16)


def middle(x, o, wo, gain):
    rows, d = x.shape
    return call(
        middle_body,
        (sds((rows, d), F32), sds((rows, d), BF16)),
        (x, o, wo, gain),
        scratch=[pltpu.VMEM((wo.shape[2], d), BF16)],
        flops=2 * rows * d * d,
    )


def widen_body(w_ref, o_ref):
    o_ref[...] = w_ref[0]


def widen(w):
    nb, rows, wb = w.shape
    return pl.pallas_call(
        widen_body,
        out_shape=sds((rows, nb * wb), BF16),
        grid=(nb,),
        in_specs=[pl.BlockSpec((1, rows, wb), lambda s: (s, 0, 0))],
        out_specs=pl.BlockSpec((rows, wb), lambda s: (0, s)),
        compiler_params=pltpu.CompilerParams(vmem_limit_bytes=VMEM_BYTES),
        cost_estimate=pl.CostEstimate(flops=0, bytes_accessed=4 * w.size, transcendentals=0),
    )(w)


def mlp_body(h2_ref, cot_ref, w_ref, dh_ref, out_ref, hid_ref, dg_ref, du_ref):
    ff = hid_ref.shape[1]
    h2 = h2_ref[...]
    gate_w, up_w, down_w = w_ref[0:ff, :], w_ref[ff : 2 * ff, :], w_ref[2 * ff : 3 * ff, :]
    dhid = mm(cot_ref[...], down_w, NT)
    g = mm(h2, gate_w, NT)
    u = mm(h2, up_w, NT)
    sig = jax.nn.sigmoid(g)
    act = g * sig
    hid = (act * u).astype(BF16)
    dg = (dhid * u * sig * (1.0 + g * (1.0 - sig))).astype(BF16)
    du = (dhid * act).astype(BF16)
    hid_ref[...] = hid
    dg_ref[...] = dg
    du_ref[...] = du
    dh_ref[...] = (mm(dg, gate_w) + mm(du, up_w)).astype(BF16)
    out_ref[...] = mm(hid, down_w).astype(BF16)


def mlp(h2, cot, w):
    rows, d = h2.shape
    ff = w.shape[0] // 3
    return call(
        mlp_body,
        (
            sds((rows, d), BF16),
            sds((rows, d), BF16),
            sds((rows, ff), BF16),
            sds((rows, ff), BF16),
            sds((rows, ff), BF16),
        ),
        (h2, cot, w),
        flops=12 * rows * d * ff,
    )


def mlp_grads_body(n, *refs):
    h2, cot, hid, dg, du = (refs[k * n : (k + 1) * n] for k in range(5))
    o_ref = refs[5 * n]
    nb, total, wb = o_ref.shape
    ff = total // 3
    for k, (left, right) in enumerate(((dg, h2), (du, h2), (hid, cot))):
        acc = None
        for r in range(n):
            part = mm(left[r][...], right[r][...], TN)
            acc = part if acc is None else acc + part
        acc = acc.astype(BF16)
        for s in range(nb):
            o_ref[s, k * ff : (k + 1) * ff, :] = acc[:, s * wb : (s + 1) * wb]


def mlp_grads(h2, cot, hid, dg, du, nb):
    n = len(h2)
    d, ff = h2[0].shape[1], hid[0].shape[1]
    return call(
        functools.partial(mlp_grads_body, n),
        sds((nb, 3 * ff, d // nb), BF16),
        (*h2, *cot, *hid, *dg, *du),
        flops=6 * n * h2[0].shape[0] * d * ff,
    )


def turn_body(n, *refs):
    parts, (y1_ref, cot_ref, gain_ref, wo_ref) = refs[:n], refs[n : n + 4]
    dy1_ref, f_ref, do_ref, dgain_ref, wide_ref = refs[n + 4 :]
    dh2 = parts[0][...].astype(F32)
    for r in range(1, n):
        dh2 = dh2 + parts[r][...].astype(F32)
    y1 = y1_ref[...]
    scale = lax.rsqrt(jnp.mean(y1 * y1, axis=-1, keepdims=True) + EPS)
    normed = y1 * scale
    dgain_ref[...] = jnp.sum(dh2 * normed, axis=0, keepdims=True)
    dn = dh2 * gain_ref[0:1, :]
    inner = jnp.mean(dn * normed, axis=-1, keepdims=True)
    dy1 = cot_ref[...].astype(F32) + scale * (dn - normed * inner)
    dy1_ref[...] = dy1
    f = dy1.astype(BF16)
    f_ref[...] = f
    nb, wb = wo_ref.shape[1], wo_ref.shape[3]
    for r in range(n):
        for s in range(nb):
            wide_ref[:, s * wb : (s + 1) * wb] = wo_ref[r, s]
        do_ref[r] = mm(f, wide_ref[...], NT).astype(BF16)


def turn(parts, y1, cot, gain, wo):
    n = len(parts)
    rows, d = y1.shape
    nv = wo.shape[2]
    return call(
        functools.partial(turn_body, n),
        (sds((rows, d), F32), sds((rows, d), BF16), sds((n, rows, nv), BF16), sds((1, d), F32)),
        (*parts, y1, cot, gain, wo),
        scratch=[pltpu.VMEM((nv, d), BF16)],
        flops=2 * rows * d * d,
    )


def back_first_body(do_ref, on_ref, inv_ref, qk_ref, masks_ref, d_ref, p_ref, z_ref):
    r = pl.program_id(0)
    n = pl.num_programs(0)
    nqk = qk_ref.shape[1]
    heads = nqk // (2 * FDIM)
    rows = do_ref.shape[1]

    @pl.when(r == 0)
    def _():
        z_ref[...] = jnp.zeros_like(z_ref)

    live = masks_ref[0, 2:3, :]
    lane = lanes((rows, 128))
    for pair in range(heads // 2):
        cols = slice(pair * 128, (pair + 1) * 128)
        wide = do_ref[0, :, cols].astype(F32) * inv_ref[0, :, cols]
        dnum = wide.astype(BF16)
        prod = -(wide * on_ref[0, :, cols])
        high = prod.astype(BF16)
        low = (prod - high.astype(F32)).astype(BF16)
        both = []
        for j in range(2):
            i = 2 * pair + j
            row = lax.broadcasted_iota(jnp.int32, (128, 128), 0)
            hot = jnp.where((row < VDIM) if j == 0 else (row >= VDIM), 1.0, 0.0).astype(BF16)
            dden = mm(high, hot) + mm(low, hot)
            d_ref[0, i] = own_half(dnum, j, with_pair(dden, j))
            dh = dden.astype(BF16)
            dl = (dden - dh.astype(F32)).astype(BF16)
            zero = jnp.zeros_like(dh)
            spot = r * heads + i
            zext = jnp.where(lane == spot, dh, jnp.where(lane == spot + n * heads, dl, zero))
            q = qk_ref[0, i * FDIM : (i + 1) * FDIM, :].astype(F32)
            phi = (features(q) * live).astype(BF16)
            res = mm(phi, jnp.concatenate([dnum, zext], axis=1))
            both.append(res[:, :128])
            z_ref[...] += res[:, 128:]
        p_ref[r * (heads // 2) + pair] = own_half(both[0], 0, both[1]).astype(BF16)

    @pl.when(r == n - 1)
    def _():
        p_ref[p_ref.shape[0] - 1] = z_ref[...].astype(BF16)


def back_first(do, on, inv, qk, masks):
    n, nqk, rows = qk.shape
    heads = nqk // (2 * FDIM)
    pieces = n * heads // 2 + 1
    return call(
        back_first_body,
        (sds((n, heads, rows, 128), BF16), sds((pieces, FROWS, 128), BF16)),
        (do, on, inv, qk, masks),
        grid=(n,),
        in_specs=[by_row(x.shape[1:]) for x in (do, on, inv, qk, masks)],
        out_specs=[by_row((heads, rows, 128)), whole((pieces, FROWS, 128))],
        scratch=[pltpu.VMEM((FROWS, 128), F32)],
        flops=n * heads * rows * 256 * 600,
    )


def back_local_body(d_ref, qk_ref, v_ref, masks_ref, c_ref, dq_ref, dk_ref, dv_ref):
    r = pl.program_id(0)
    nqk = qk_ref.shape[1]
    heads = nqk // (2 * FDIM)
    rows = v_ref.shape[1]
    masks = masks_ref[0]
    mask = doc_mask(masks, rows)
    live = masks[2:3, :]
    last = c_ref.shape[0] - 1
    for pair in range(heads // 2):
        cols = slice(pair * 128, (pair + 1) * 128)
        v_pair = v_ref[0, :, cols]
        c = c_ref[r * (heads // 2) + pair]
        dv = None
        for j in range(2):
            i = 2 * pair + j
            q = qk_ref[0, i * FDIM : (i + 1) * FDIM, :]
            k = qk_ref[0, nqk // 2 + i * FDIM : nqk // 2 + (i + 1) * FDIM, :]
            s1 = mm(q, k, TN) * 0.25 + 1.0
            a = jnp.where(mask, 0.5 * s1 * s1 + 0.5, 0.0).astype(BF16)
            d = d_ref[0, i]
            da = mm(d, with_ones(v_pair, j), NT)
            ds = jnp.where(mask, da * s1, 0.0).astype(BF16)
            z = pick_columns(
                c_ref[last], lambda row: row == r * heads + i, lambda lane: lane >= 0
            )
            dphi = mm(own_half(c, j, with_pair(z, j)), d, NT) * live
            back = features_back(q.astype(F32), dphi)
            dq_ref[0, i * FDIM : (i + 1) * FDIM, :] = (mm(k, ds, NT) * 0.25 + back).astype(BF16)
            dk_ref[0, i * FDIM : (i + 1) * FDIM, :] = mm(q, ds) * 0.25
            part = mm(own_half(d, j), a, TN)
            dv = part if dv is None else dv + part
        dv_ref[0, cols, :] = dv


def back_local(d, qk, v, masks, c):
    n, nqk, rows = qk.shape
    heads = nqk // (2 * FDIM)
    nv = heads * VDIM
    return call(
        back_local_body,
        (sds((n, nqk // 2, rows), BF16), sds((n, nqk // 2, rows), F32), sds((n, nv, rows), F32)),
        (d, qk, v, masks, c),
        grid=(n,),
        in_specs=[by_row(x.shape[1:]) for x in (d, qk, v, masks)] + [whole(c.shape)],
        out_specs=[by_row((nqk // 2, rows)), by_row((nqk // 2, rows)), by_row((nv, rows))],
        flops=n * heads * rows * rows * 1500,
    )


def back_last_body(
    dq_ref, dk_ref, dv_ref, qk_ref, v_ref, masks_ref, one_ref, two_ref, h1_ref, x_ref, w_ref,
    dh1_ref, dw_ref, dgain_ref, z_ref, wt_ref, acc_ref,
):
    r = pl.program_id(0)
    n = pl.num_programs(0)
    nqk = qk_ref.shape[1]
    heads = nqk // (2 * FDIM)
    nb, _, wb = w_ref.shape
    last = one_ref.shape[0] - 1

    @pl.when(r == 0)
    def _():
        for s in range(nb):
            wt_ref[:, s * wb : (s + 1) * wb] = w_ref[s]
        flag = lane_flags(masks_ref, 4, masks_ref.shape[0], heads)
        z_ref[...] = joined(one_ref[last], two_ref[last], flag).astype(BF16)
        dgain_ref[...] = jnp.zeros_like(dgain_ref)
        acc_ref[...] = jnp.zeros_like(acc_ref)

    flag = masks_ref[r, 4:5, 0:128]
    tail = masks_ref[r, 1:2, :]
    dks, dvs = [], []
    for pair in range(heads // 2):
        cols = slice(pair * 128, (pair + 1) * 128)
        at = r * (heads // 2) + pair
        dp = joined(one_ref[at], two_ref[at], flag).astype(BF16)
        v_pair = v_ref[0, :, cols]
        dv = dv_ref[0, cols, :]
        for j in range(2):
            i = 2 * pair + j
            k = qk_ref[0, nqk // 2 + i * FDIM : nqk // 2 + (i + 1) * FDIM, :].astype(F32)
            spot = r * heads + i
            z = pick_columns(
                z_ref[...],
                lambda row: jnp.logical_or(row == spot, row == spot + n * heads),
                lambda lane: lane >= 0,
            )
            dphi = mm(own_half(dp, j, with_pair(z, j)), with_ones(v_pair, j), NT) * tail
            dk = dk_ref[0, i * FDIM : (i + 1) * FDIM, :] + features_back(k, dphi)
            dks.append(dk.astype(BF16))
            phi = (features(k) * tail).astype(BF16)
            dv = dv + mm(own_half(dp, j), phi, TN)
        dvs.append(dv.astype(BF16))
    d = jnp.concatenate([dq_ref[0]] + dks + dvs, axis=0)
    acc_ref[...] += mm(d, h1_ref[0])
    dh1 = mm(d, wt_ref[...], TN)
    dh1_ref[0] = dh1.astype(BF16)
    x = x_ref[0].astype(F32)
    normed = x * lax.rsqrt(jnp.mean(x * x, axis=-1, keepdims=True) + EPS)
    dgain_ref[...] += jnp.sum(dh1 * normed, axis=0, keepdims=True)

    @pl.when(r == n - 1)
    def _():
        for s in range(nb):
            dw_ref[s] = acc_ref[:, s * wb : (s + 1) * wb].astype(BF16)


def back_last(dq, dk, dv, qk, v, masks, one, two, h1, x, w):
    n, nqk, rows = qk.shape
    nb, total, wb = w.shape
    d = nb * wb
    return call(
        back_last_body,
        (sds((n, rows, d), BF16), sds(w.shape, BF16), sds((1, d), F32)),
        (dq, dk, dv, qk, v, masks, one, two, h1, x, w),
        grid=(n,),
        in_specs=[by_row(y.shape[1:]) for y in (dq, dk, dv, qk, v)]
        + [whole(masks.shape), whole(one.shape), whole(two.shape)]
        + [by_row(h1.shape[1:]), by_row(x.shape[1:]), whole(w.shape)],
        out_specs=[by_row((rows, d)), whole(w.shape), whole((1, d))],
        scratch=[
            pltpu.VMEM((FROWS, 128), BF16),
            pltpu.VMEM((total, d), BF16),
            pltpu.VMEM((total, d), F32),
        ],
        flops=4 * n * rows * d * total,
    )


def out_grads_body(n, o_ref, *refs):
    fs, out_ref = refs[:n], refs[n]
    nb, _, wb = out_ref.shape
    acc = None
    for r in range(n):
        part = mm(o_ref[r], fs[r][...], TN)
        acc = part if acc is None else acc + part
    for s in range(nb):
        out_ref[s] = acc[:, s * wb : (s + 1) * wb].astype(BF16)


def out_grads(o, fs, nb):
    n, rows, nv = o.shape
    d = fs[0].shape[1]
    return call(
        functools.partial(out_grads_body, n),
        sds((nb, nv, d // nb), BF16),
        (o, *fs),
        flops=2 * n * rows * nv * d,
    )


def final_body(n, *refs):
    parts, (x_ref, dy1_ref, gain_ref, o_ref) = refs[:n], refs[n:]
    dh1 = parts[0][...].astype(F32)
    for r in range(1, n):
        dh1 = dh1 + parts[r][...].astype(F32)
    x = x_ref[...].astype(F32)
    scale = lax.rsqrt(jnp.mean(x * x, axis=-1, keepdims=True) + EPS)
    normed = x * scale
    dn = dh1 * gain_ref[0:1, :]
    inner = jnp.mean(dn * normed, axis=-1, keepdims=True)
    o_ref[...] = dy1_ref[...] + scale * (dn - normed * inner)


def final(parts, x, dy1, gain):
    return call(
        functools.partial(final_body, len(parts)), sds(x.shape, F32), (*parts, x, dy1, gain)
    )


def xor_pairs(size, r):
    return [(i, i ^ r) for i in range(size)]


def swap(parts):
    size = lax.axis_size("head")
    return [parts[0]] + [lax.ppermute(parts[r], "head", xor_pairs(size, r)) for r in range(1, size)]


def spread(x):
    return swap([x] * lax.axis_size("head"))


def shifted(x, step):
    size = lax.axis_size("seq")
    return lax.ppermute(x, "seq", [(i, i + step) for i in range(size) if 0 <= i + step < size])


def halved(x):
    size, me = lax.axis_size("seq"), lax.axis_index("seq")
    if size & (size - 1):
        return lax.psum_scatter(x, "seq", tiled=True)
    k = 1
    while k < size:
        x = x.reshape((x.shape[0] // 2, 2) + x.shape[1:])
        bit = (me // k) % 2
        keep = lax.dynamic_index_in_dim(x, bit, 1, keepdims=False)
        send = lax.dynamic_index_in_dim(x, 1 - bit, 1, keepdims=False)
        got = lax.ppermute(send, "seq", xor_pairs(size, k))
        x = (keep.astype(F32) + got.astype(F32)).astype(x.dtype)
        k *= 2
    return x


def carried(x, labels, step, keep):
    size, me = lax.axis_size("seq"), lax.axis_index("seq")
    reach = max(size // 4, 1)
    mine = jnp.take(labels, me, axis=1)
    k = 1
    while 2 * k < reach:
        other = jnp.take(labels, jnp.clip(me - step * k, 0, size - 1), axis=1)
        flag = (other == mine).astype(F32)
        x = keep(x, shifted(x, step * k), flag)
        k *= 2
    near = jnp.take(labels, jnp.clip(me - step, 0, size - 1), axis=1)
    far = jnp.take(labels, jnp.clip(me - step * (1 + k), 0, size - 1), axis=1)
    return shifted(x, step), shifted(x, step * (1 + k)), (near == far).astype(F32)


def on_device(
    tokens, doc_ids, query_weight, key_weight, value_weight, out_weight,
    gate_weight, up_weight, down_weight, mix_gain, mlp_gain, cotangent,
):
    n, blocks = lax.axis_size("head"), lax.axis_size("seq")
    here, me = lax.axis_index("head"), lax.axis_index("seq")
    rows, d = tokens.shape[1:]
    wb = d // blocks
    nb = blocks if wb % 128 == 0 else 1
    heads = query_weight.shape[1] // FDIM
    nqkv = 2 * heads * FDIM + heads * VDIM
    nv = heads * VDIM
    ff = gate_weight.shape[1]
    x, cot = tokens[0], cotangent[0]

    xs = jnp.stack(spread(x))
    small = jnp.concatenate([mix_gain, mlp_gain, doc_ids[0].astype(BF16)])
    small = lax.all_gather(small, "head")
    width = small.shape[1]
    extra = -(-n * width // (16 * wb)) * 16
    small = jnp.pad(small.reshape(-1), (0, extra * wb - n * width)).reshape(extra, wb)
    pack = jnp.concatenate(
        [query_weight.T, key_weight.T, value_weight.T, out_weight, small], axis=0
    )
    pack = lax.all_gather(pack, "seq")
    small = pack[:, nqkv + nv :].reshape(blocks, -1)[:, : n * width].reshape(blocks, n, width)
    piece = mix_gain.shape[0]
    gain_mix = jnp.transpose(small[:, :, :piece], (1, 0, 2)).reshape(1, d).astype(F32)
    gain_mlp = jnp.transpose(small[:, :, piece : 2 * piece], (1, 0, 2)).reshape(1, d).astype(F32)
    docs = jnp.take(small[:, :, 2 * piece :].astype(F32), here ^ jnp.arange(n), axis=1)
    segs = jnp.take(docs, me, axis=0)
    lasts = jnp.transpose(docs[:, :, -1])

    def blocked(w):
        return w if nb == blocks else jnp.transpose(w, (1, 0, 2)).reshape(1, w.shape[1], d)

    def unblocked(w):
        return w if nb == blocks else jnp.transpose(w.reshape(w.shape[1], blocks, wb), (1, 0, 2))

    w_qkv = blocked(pack[:, :nqkv])
    w_out = jnp.stack(spread(blocked(pack[:, nqkv : nqkv + nv])))
    cots = spread(cot)
    mlp_pack = jnp.concatenate([gate_weight.T, up_weight.T, down_weight], axis=0)
    mlp_pack = lax.all_gather(mlp_pack, "seq")
    w_mlp = widen(blocked(mlp_pack))

    before = jnp.where(me > 0, jnp.take(lasts, jnp.maximum(me - 1, 0), axis=1), -1.0)
    final_label = jnp.take(lasts, me, axis=1)
    labels_back = jnp.concatenate([jnp.full((n, 1), -1.0), lasts[:, :-1]], axis=1)

    def join(a, b, flag):
        each = jnp.repeat(flag, heads // 2)[:, None, None]
        lane = jnp.arange(128) % (n * heads) // heads
        both = a[:-1].astype(F32) + b[:-1].astype(F32) * each
        norm = a[-1].astype(F32) + b[-1].astype(F32) * jnp.take(flag, lane)[None]
        return jnp.concatenate([both, norm[None]], axis=0).astype(BF16)

    def flags_of(labels, step):
        reach = max(blocks // 4, 1)
        k = 1
        while 2 * k < reach:
            k *= 2
        near = jnp.take(labels, jnp.clip(me - step, 0, blocks - 1), axis=1)
        far = jnp.take(labels, jnp.clip(me - step * (1 + k), 0, blocks - 1), axis=1)
        return (near == far).astype(F32)

    flat = jnp.ones((1, rows), F32)
    masks = jnp.stack(
        [
            segs,
            (segs == final_label[:, None]).astype(F32),
            (segs == before[:, None]).astype(F32),
            flags_of(lasts, 1)[:, None] * flat,
            flags_of(labels_back, -1)[:, None] * flat,
        ]
        + [jnp.zeros_like(segs)] * 3,
        axis=1,
    )

    h1, qk, v, sums = project(xs, gain_mix, w_qkv, masks, heads)
    one, two, _ = carried(sums, lasts, 1, join)
    nd = local(qk, v, masks)
    o, on, inv, c = carry(nd, qk, masks, one, two)
    o_all = jnp.stack(swap([o[r] for r in range(n)]))
    y1, h2 = middle(x, o_all, w_out, gain_mlp)
    h2s = spread(h2)
    res = [mlp(h2s[r], cots[r], w_mlp) for r in range(n)]
    dparts, oparts, hid, dg, du = ([t[k] for t in res] for k in range(5))
    dparts = swap(dparts)
    dy1, f, do, dgain_mlp = turn(dparts, y1, cot, gain_mlp, w_out)
    do = jnp.stack(swap([do[r] for r in range(n)]))
    dext, dsums = back_first(do, on, inv, qk, masks)
    back_one, back_two, _ = carried(dsums, labels_back, -1, join)
    dq, dk, dv = back_local(dext, qk, v, masks, c)
    dmlp = unblocked(mlp_grads(h2s, cots, hid, dg, du, nb))
    dmlp = lax.psum_scatter(dmlp, "seq", tiled=True)[0].astype(F32)
    oparts = swap(oparts)
    output = y1
    for part in oparts:
        output = output + part.astype(F32)
    fs = spread(f)
    dout = halved(unblocked(out_grads(o, fs, nb)))[0].astype(F32)
    dh1, dqkv, dgain_mix = back_last(dq, dk, dv, qk, v, masks, back_one, back_two, h1, xs, w_qkv)
    dqkv = halved(unblocked(dqkv))[0].astype(F32)
    dh1 = swap([dh1[r] for r in range(n)])
    grad_tokens = final(dh1, x, dy1, gain_mix)

    gains = jnp.stack([dgain_mix[0], dgain_mlp[0]])
    gains = jnp.transpose(gains.reshape(2, n, blocks, piece), (1, 2, 0, 3))
    gains = jnp.take(gains, here ^ jnp.arange(n), axis=0)
    got = swap([gains[r] for r in range(n)])
    total = got[0]
    for part in got[1:]:
        total = total + part
    total = halved(total)[0]

    kq = heads * FDIM
    return (
        output.astype(BF16)[None],
        grad_tokens[None],
        dqkv[:kq].T,
        dqkv[kq : 2 * kq].T,
        dqkv[2 * kq :].T,
        dout,
        dmlp[:ff].T,
        dmlp[ff : 2 * ff].T,
        dmlp[2 * ff :],
        total[0],
        total[1],
    )


def solution(mesh):
    placed = (
        P("head", "seq", None),
        P("head", "seq"),
        P("seq", "head"),
        P("seq", "head"),
        P("seq", "head"),
        P("head", "seq"),
        P("seq", "head"),
        P("seq", "head"),
        P("head", "seq"),
        P(("head", "seq")),
        P(("head", "seq")),
        P("head", "seq", None),
    )
    return jax.shard_map(
        on_device,
        mesh=mesh,
        in_specs=placed,
        out_specs=(
            P("head", "seq", None),
            P("head", "seq", None),
            P("seq", "head"),
            P("seq", "head"),
            P("seq", "head"),
            P("head", "seq"),
            P("seq", "head"),
            P("seq", "head"),
            P("head", "seq"),
            P(("head", "seq")),
            P(("head", "seq")),
        ),
        check_vma=False,
    )
```

```python
import functools

import jax
import jax.numpy as jnp
from jax import lax
from jax.experimental import pallas as pl
from jax.experimental.pallas import tpu as pltpu
from jax.sharding import PartitionSpec as P

FDIM = 16
VDIM = 64
EPS = 1e-06
ROOT_HALF = 0.7071067811865476
FROWS = 11 * FDIM
F32 = jnp.float32
BF16 = jnp.bfloat16
VMEM_BYTES = 24 * 1024 * 1024
VMEM_MOST = 56 * 1024 * 1024

NN = (((1,), (0,)), ((), ()))
NT = (((1,), (1,)), ((), ()))
TN = (((0,), (0,)), ((), ()))


def mm(a, b, dims=NN):
    return lax.dot_general(a, b, dims, preferred_element_type=F32)


def call(body, outs, ins, grid=None, in_specs=None, out_specs=None, scratch=(), smem=0, us=5, most=False):
    kwargs = {}
    if smem:
        spaces = [pltpu.SMEM] * smem + [pltpu.VMEM] * (len(ins) - smem)
        kwargs = dict(in_specs=[pl.BlockSpec(memory_space=space) for space in spaces])
    if grid is not None:
        kwargs = dict(grid=grid, in_specs=in_specs, out_specs=out_specs)
    return pl.pallas_call(
        body,
        out_shape=outs,
        scratch_shapes=list(scratch),
        compiler_params=pltpu.CompilerParams(vmem_limit_bytes=VMEM_MOST if most else VMEM_BYTES),
        cost_estimate=pl.CostEstimate(flops=0, bytes_accessed=us * 600000, transcendentals=0),
        **kwargs,
    )(*ins)


def sds(shape, dtype):
    return jax.ShapeDtypeStruct(shape, dtype)


def whole(shape):
    return pl.BlockSpec(shape, lambda r: (0,) * len(shape))


def by_row(shape):
    return pl.BlockSpec((1,) + tuple(shape), lambda r: (r,) + (0,) * len(shape))


def coef(d):
    return ROOT_HALF if d in (0, FDIM // 2) else 1.0


def features(w):
    half = w * 0.5
    rows = [half]
    for d in range(FDIM // 2 + 1):
        other = half if d == 0 else pltpu.roll(half, FDIM - d, 0)
        rows.append(half * other * coef(d))
    first = lax.broadcasted_iota(jnp.int32, half.shape, 0) == 0
    rows.append(jnp.where(first, 1.0, 0.0))
    return jnp.concatenate(rows, axis=0)


def features_back(w, grad):
    half = w * 0.5
    total = grad[:FDIM]
    for d in range(FDIM // 2 + 1):
        part = grad[FDIM * (d + 1) : FDIM * (d + 2)]
        if d == 0:
            total = total + part * half * (2.0 * coef(0))
        else:
            near = part * pltpu.roll(half, FDIM - d, 0)
            far = pltpu.roll(part * half, d, 0)
            total = total + (near + far) * coef(d)
    return total * 0.5


def lanes(shape):
    return lax.broadcasted_iota(jnp.int32, shape, len(shape) - 1)


def one_hot_lanes(rows, index):
    lane = lanes((rows, 128))
    return jnp.where(lane == index, 1.0, 0.0).astype(BF16)


def own_half(x, j, other=None):
    left = lanes(x.shape) < VDIM
    keep = left if j == 0 else jnp.logical_not(left)
    return jnp.where(keep, x, jnp.zeros_like(x) if other is None else other)


def pick_columns(z, column, spots):
    row = lax.broadcasted_iota(jnp.int32, (128, 128), 0)
    hot = jnp.where(column(row), 1.0, 0.0) * jnp.where(spots(lanes((128, 128))), 1.0, 0.0)
    return mm(z, hot.astype(BF16))


def doc_mask(masks, rows):
    seg = masks[0:1, :]
    col = jnp.transpose(masks)[:, 0:1]
    causal = lax.broadcasted_iota(jnp.int32, (rows, rows), 0) >= lax.broadcasted_iota(
        jnp.int32, (rows, rows), 1
    )
    return jnp.logical_and(causal, col == seg)


def with_pair(z, j):
    lane = lanes(z.shape)
    base = VDIM if j == 0 else 0
    high = z.astype(BF16)
    low = (z - high.astype(F32)).astype(BF16)
    zero = jnp.zeros_like(high)
    return jnp.where(lane == base, high, jnp.where(lane == base + 1, low, zero))


def with_ones(x, j):
    lane = lanes(x.shape)
    base = VDIM if j == 0 else 0
    hot = jnp.where(jnp.logical_or(lane == base, lane == base + 1), 1.0, 0.0).astype(x.dtype)
    return own_half(x, j, hot)


def join_rows(refs):
    return refs[0][...] if len(refs) == 1 else jnp.concatenate([one[...] for one in refs], axis=0)


def grouped(refs, n):
    k = len(refs) // n
    return [refs[i * k : (i + 1) * k] for i in range(n)]


def flat(lists):
    return [x for one in lists for x in one]


def take_row(r, groups, ref):
    for index, one in enumerate(groups):
        @pl.when(r == index)
        def _():
            ref[...] = join_rows(one)


def give_row(r, refs, value):
    for index, one in enumerate(refs):
        @pl.when(r == index)
        def _():
            one[...] = value


def pack_body(q_ref, k_ref, v_ref, mix_ref, mlp_ref, docs_ref, pack_ref):
    at = 0
    for one in (q_ref, k_ref):
        pack_ref[at : at + one.shape[0], :] = one[...]
        at += one.shape[0]
    pack_ref[at : at + v_ref.shape[1], :] = v_ref[...].T
    at += v_ref.shape[1]
    wb = pack_ref.shape[1]
    extra = pack_ref.shape[0] - at
    rows = []
    for one in (mix_ref, mlp_ref):
        fill = jnp.zeros((1, wb - one.shape[1]), F32)
        rows.append(jnp.concatenate([one[...].astype(F32), fill], axis=1))
    rows.append(docs_ref[...].astype(F32))
    rows.append(jnp.zeros((extra - 2 - docs_ref.shape[0], wb), F32))
    pack_ref[at:, :] = jnp.concatenate(rows, axis=0).astype(BF16)


def pack_two_body(gate_ref, up_ref, pack_ref):
    ff = gate_ref.shape[0]
    pack_ref[:ff, :] = gate_ref[...]
    pack_ref[ff:, :] = up_ref[...]


def project_body(n, core_ref, x_ref, gain_ref, masks_ref, *refs):
    blocks = grouped(refs[:-6], n)
    h1_ref, qk_ref, v_ref, p_ref, wt_ref, z_ref = refs[-6:]
    r = pl.program_id(0)
    heads = qk_ref.shape[1] // (2 * FDIM)
    total = wt_ref.shape[1]

    @pl.when(r == 0)
    def _():
        x = x_ref[...].astype(F32)
        normed = x * lax.rsqrt(jnp.mean(x * x, axis=-1, keepdims=True) + EPS)
        h1_ref[...] = (normed * gain_ref[0:1, :]).astype(BF16)
        z_ref[...] = jnp.zeros_like(z_ref)

    for index, halves in enumerate(blocks):

        @pl.when(r == index)
        def _():
            for other, half in enumerate(halves):
                count, _, wb = half.shape
                side = core_ref[0] if other == 0 else 1 - core_ref[0]
                for j in range(count):
                    at = j * wb if count * wb == wt_ref.shape[2] else (side * count + j) * wb
                    if not isinstance(at, int):
                        at = pl.multiple_of(at, wb)
                    wt_ref[0, :, pl.ds(at, wb)] = half[j, :total, :]

    h1 = h1_ref[...]
    nqk = qk_ref.shape[1]
    qk = mm(wt_ref[0, :nqk, :], h1, NT).astype(BF16)
    qk_ref[0] = qk
    v = mm(h1, wt_ref[0, nqk:, :], NT).astype(BF16)
    v_ref[0] = v
    tail = masks_ref[1:2, :]
    rows = v.shape[0]
    for pair in range(heads // 2):
        v_pair = v[:, pair * 128 : (pair + 1) * 128]
        both = []
        for j in range(2):
            i = 2 * pair + j
            k = qk[nqk // 2 + i * FDIM : nqk // 2 + (i + 1) * FDIM].astype(F32)
            phi = (features(k) * tail).astype(BF16)
            rhs = jnp.concatenate([v_pair, one_hot_lanes(rows, r * heads + i)], axis=1)
            res = mm(phi, rhs)
            both.append(res[:, :128])
            z_ref[...] += res[:, 128:]
        p_ref[r * (heads // 2) + pair] = own_half(both[0], 0, both[1]).astype(BF16)

    @pl.when(r == pl.num_programs(0) - 1)
    def _():
        p_ref[p_ref.shape[0] - 1] = z_ref[...].astype(BF16)


def project(core, x, gain, masks, blocks, heads):
    n = len(blocks)
    rows, d = x.shape
    nqk, nv = 2 * heads * FDIM, heads * VDIM
    sums = n * heads // 2 + 1
    ins = (core, x, gain, masks, *flat(blocks))
    return call(
        functools.partial(project_body, n),
        (
            sds((rows, d), BF16),
            sds((n, nqk, rows), BF16),
            sds((n, rows, nv), BF16),
            sds((sums, FROWS, 128), BF16),
            sds((n, nqk + nv, d), BF16),
        ),
        ins,
        grid=(n,),
        in_specs=[pl.BlockSpec(memory_space=pltpu.SMEM)] + [whole(x.shape) for x in ins[1:]],
        out_specs=[
            whole((rows, d)),
            by_row((nqk, rows)),
            by_row((rows, nv)),
            whole((sums, FROWS, 128)),
            by_row((nqk + nv, d)),
        ],
        scratch=[pltpu.VMEM((FROWS, 128), F32)],
        us=7,
        most=True,
    )


def local_body(qk_ref, v_ref, masks_ref, nd_ref):
    nqk = qk_ref.shape[1]
    heads = nqk // (2 * FDIM)
    rows = v_ref.shape[1]
    mask = doc_mask(masks_ref[...], rows)
    for pair in range(heads // 2):
        v_pair = v_ref[0, :, pair * 128 : (pair + 1) * 128]
        acc = None
        for j in range(2):
            i = 2 * pair + j
            q = qk_ref[0, i * FDIM : (i + 1) * FDIM, :]
            k = qk_ref[0, nqk // 2 + i * FDIM : nqk // 2 + (i + 1) * FDIM, :]
            s1 = mm(q, k, TN) * 0.25 + 1.0
            a = jnp.where(mask, 0.5 * s1 * s1 + 0.5, 0.0).astype(BF16)
            ones = own_half(jnp.ones((rows, 128), BF16), j)
            part = mm(a, jnp.concatenate([own_half(v_pair, j), ones], axis=1))
            acc = part if acc is None else acc + part
        nd_ref[0, pair] = acc


def local(qk, v, masks):
    n, nqk, rows = qk.shape
    heads = nqk // (2 * FDIM)
    return call(
        local_body,
        sds((n, heads // 2, rows, 256), F32),
        (qk, v, masks),
        grid=(n,),
        in_specs=[by_row(qk.shape[1:]), by_row(v.shape[1:]), whole(masks.shape)],
        out_specs=by_row((heads // 2, rows, 256)),
    )


def joined(first, second, flag):
    return first.astype(F32) + second.astype(F32) * flag


def carry_body(nd_ref, qk_ref, masks_ref, one_ref, two_ref, o_ref, on_ref, inv_ref, c_ref):
    r = pl.program_id(0)
    n = pl.num_programs(0)
    nqk = qk_ref.shape[1]
    heads = nqk // (2 * FDIM)
    last = one_ref.shape[0] - 1

    @pl.when(r == 0)
    def _():
        c_ref[last] = joined(one_ref[last], two_ref[last], masks_ref[3:4, 0:128]).astype(BF16)

    flag = masks_ref[3:4, 0:128]
    live = masks_ref[2:3, :]
    for pair in range(heads // 2):
        at = r * (heads // 2) + pair
        c = joined(one_ref[at], two_ref[at], flag).astype(BF16)
        c_ref[at] = c
        acc = nd_ref[0, pair]
        for j in range(2):
            i = 2 * pair + j
            q = qk_ref[0, i * FDIM : (i + 1) * FDIM, :].astype(F32)
            phi = (features(q) * live).astype(BF16)
            z = pick_columns(
                c_ref[last],
                lambda row: row == r * heads + i,
                lambda lane: (lane < VDIM) if j == 0 else (lane >= VDIM),
            ).astype(BF16)
            acc = acc + mm(phi, jnp.concatenate([own_half(c, j), z], axis=1), TN)
        inv = 1.0 / acc[:, 128:]
        on = acc[:, :128] * inv
        cols = slice(pair * 128, (pair + 1) * 128)
        o_ref[0, :, cols] = on.astype(BF16)
        on_ref[0, :, cols] = on
        inv_ref[0, :, cols] = inv


def carry(nd, qk, masks, one, two):
    n, nqk, rows = qk.shape
    heads = nqk // (2 * FDIM)
    nv = heads * VDIM
    return call(
        carry_body,
        (
            sds((n, rows, nv), BF16),
            sds((n, rows, nv), F32),
            sds((n, rows, nv), F32),
            sds(one.shape, BF16),
        ),
        (nd, qk, masks, one, two),
        grid=(n,),
        in_specs=[
            by_row(nd.shape[1:]),
            by_row(qk.shape[1:]),
            whole(masks.shape),
            whole(one.shape),
            whole(two.shape),
        ],
        out_specs=[by_row((rows, nv))] * 3 + [whole(one.shape)],
        most=True,
    )


def middle_body(x_ref, gain_ref, o_ref, w_ref, y1_ref, *h2_refs):
    n, _, width = o_ref.shape
    acc = x_ref[...].astype(F32)
    for r in range(n):
        acc = acc + mm(o_ref[r], w_ref[r * width : (r + 1) * width, :])
    y1_ref[...] = acc
    scale = lax.rsqrt(jnp.mean(acc * acc, axis=-1, keepdims=True) + EPS)
    give_rows(h2_refs, (acc * scale * gain_ref[0:1, :]).astype(BF16))


def give_rows(refs, value):
    at = 0
    for one in refs:
        one[...] = value[at : at + one.shape[0]]
        at += one.shape[0]


def middle(x, o, wo, gain):
    rows, d = x.shape
    res = call(
        middle_body,
        (sds((rows, d), F32), *[sds((rows // 2, d), BF16)] * 2),
        (x, gain, o, wo),
        us=4,
    )
    return res[0], res[1:]


def spread_out_body(w_ref, out_ref, down_ref):
    nb, _, wb = w_ref.shape
    split = out_ref.shape[0]
    for s in range(nb):
        out_ref[:, s * wb : (s + 1) * wb] = w_ref[s, :split, :]
        down_ref[:, s * wb : (s + 1) * wb] = w_ref[s, split:, :]


def spread_out(w, ff):
    nb, total, wb = w.shape
    d = nb * wb
    return call(spread_out_body, (sds((total - ff, d), BF16), sds((ff, d), BF16)), (w,), us=4)


def prepare_body(n, down_ref, *refs):
    cots, out_ref = refs[:n], refs[n]
    for r in range(n):
        out_ref[r] = mm(cots[r][...], down_ref[...], NT).astype(BF16)


def prepare(down, cots):
    n = len(cots)
    return call(
        functools.partial(prepare_body, n),
        sds((n, cots[0].shape[0], down.shape[0]), BF16),
        (down, *cots),
    )


def widen_body(w_ref, wide_ref):
    nb, _, wb = w_ref.shape
    for s in range(nb):
        wide_ref[:, s * wb : (s + 1) * wb] = w_ref[s]


def widen(w):
    nb, total, wb = w.shape
    return call(widen_body, sds((total, nb * wb), BF16), (w,))


def mlp_body(first_ref, second_ref, dhid_ref, w_ref, dh_ref, hid_ref, dg_ref, du_ref):
    ff = hid_ref.shape[1]
    h2 = join_rows((first_ref, second_ref))
    gate_w, up_w = w_ref[0:ff, :], w_ref[ff : 2 * ff, :]
    dhid = dhid_ref[0].astype(F32)
    g = mm(h2, gate_w, NT)
    u = mm(h2, up_w, NT)
    sig = jax.nn.sigmoid(g)
    act = g * sig
    hid_ref[...] = (act * u).astype(BF16)
    dg = (dhid * u * sig * (1.0 + g * (1.0 - sig))).astype(BF16)
    du = (dhid * act).astype(BF16)
    dg_ref[...] = dg
    du_ref[...] = du
    dh_ref[...] = (mm(dg, gate_w) + mm(du, up_w)).astype(BF16)


def mlp(index, h2, dhid, w):
    half, d = h2[0].shape
    rows = 2 * half
    ff = w.shape[0] // 2
    return call(
        mlp_body,
        (sds((rows, d), BF16), *[sds((rows, ff), BF16)] * 3),
        (*h2, dhid, w),
        grid=(1,),
        in_specs=[whole((half, d))] * 2
        + [pl.BlockSpec((1, rows, ff), lambda r: (index, 0, 0)), whole((2 * ff, d))],
        out_specs=[whole((rows, d))] + [whole((rows, ff))] * 3,
    )


def mlp_out_body(n, w_ref, *refs):
    for r in range(n):
        refs[n + r][...] = mm(refs[r][...], w_ref[...]).astype(BF16)


def mlp_out(hid, w):
    n = len(hid)
    return call(
        functools.partial(mlp_out_body, n),
        [sds((hid[0].shape[0], w.shape[1]), BF16)] * n,
        (w, *hid),
    )


def mlp_grads_body(n, *refs):
    h2, cot = grouped(refs[: 2 * n], n), grouped(refs[2 * n : 3 * n], n)
    hid, dg, du = (refs[(3 + k) * n : (4 + k) * n] for k in range(3))
    o_ref, ff = refs[6 * n], hid[0].shape[1]
    nb, _, wb = o_ref.shape
    for k, (left, right) in enumerate(((dg, h2), (du, h2), (hid, cot))):
        acc = None
        for r in range(n):
            part = mm(left[r][...], join_rows(right[r]), TN)
            acc = part if acc is None else acc + part
        acc = acc.astype(BF16)
        for s in range(nb):
            o_ref[s, k * ff : (k + 1) * ff, :] = acc[:, s * wb : (s + 1) * wb]


def mlp_grads(h2, cot, hid, dg, du, nb):
    n = len(h2)
    d, ff = h2[0][0].shape[1], hid[0].shape[1]
    ins = (*flat(h2), *cot, *hid, *dg, *du)
    return call(
        functools.partial(mlp_grads_body, n),
        sds((nb, 3 * ff, d // nb), BF16),
        ins,
        grid=(1,),
        in_specs=[whole(x.shape) for x in ins],
        out_specs=whole((nb, 3 * ff, d // nb)),
        us=9,
    )


def turn_body(n, y1_ref, cot_ref, gain_ref, *refs):
    parts, w_ref = refs[:n], refs[n]
    dy1_ref, dgain_ref, *f_refs = refs[n + 1 : n + 4]
    do_ref = refs[n + 4]
    rows_of = do_ref.shape[2]
    dh2 = parts[0][...].astype(F32)
    for r in range(1, n):
        dh2 = dh2 + parts[r][...].astype(F32)
    y1 = y1_ref[...]
    scale = lax.rsqrt(jnp.mean(y1 * y1, axis=-1, keepdims=True) + EPS)
    normed = y1 * scale
    dgain_ref[...] = jnp.sum(dh2 * normed, axis=0, keepdims=True)
    dn = dh2 * gain_ref[0:1, :]
    inner = jnp.mean(dn * normed, axis=-1, keepdims=True)
    dy1 = cot_ref[...].astype(F32) + scale * (dn - normed * inner)
    dy1_ref[...] = dy1
    f = dy1.astype(BF16)
    give_rows(f_refs, f)
    for r in range(n):
        do_ref[r] = mm(f, w_ref[r * rows_of : (r + 1) * rows_of, :], NT).astype(BF16)


def turn(parts, y1, cot, gain, wo):
    n = len(parts)
    rows, d = y1.shape
    nv = wo.shape[0] // n
    res = call(
        functools.partial(turn_body, n),
        (
            sds((rows, d), F32),
            sds((1, d), F32),
            sds((rows, d), BF16),
            sds((n, rows, nv), BF16),
        ),
        (y1, cot, gain, *parts, wo),
    )
    return res


def back_first_body(do_ref, on_ref, inv_ref, qk_ref, masks_ref, d_ref, p_ref, z_ref):
    r = pl.program_id(0)
    n = pl.num_programs(0)
    nqk = qk_ref.shape[1]
    heads = nqk // (2 * FDIM)
    rows = do_ref.shape[1]

    @pl.when(r == 0)
    def _():
        z_ref[...] = jnp.zeros_like(z_ref)

    live = masks_ref[2:3, :]
    lane = lanes((rows, 128))
    for pair in range(heads // 2):
        cols = slice(pair * 128, (pair + 1) * 128)
        wide = do_ref[0, :, cols].astype(F32) * inv_ref[0, :, cols]
        dnum = wide.astype(BF16)
        prod = -(wide * on_ref[0, :, cols])
        high = prod.astype(BF16)
        low = (prod - high.astype(F32)).astype(BF16)
        both = []
        for j in range(2):
            i = 2 * pair + j
            row = lax.broadcasted_iota(jnp.int32, (128, 128), 0)
            hot = jnp.where((row < VDIM) if j == 0 else (row >= VDIM), 1.0, 0.0).astype(BF16)
            dden = mm(high, hot) + mm(low, hot)
            d_ref[0, i] = own_half(dnum, j, with_pair(dden, j))
            dh = dden.astype(BF16)
            dl = (dden - dh.astype(F32)).astype(BF16)
            zero = jnp.zeros_like(dh)
            spot = r * heads + i
            zext = jnp.where(lane == spot, dh, jnp.where(lane == spot + n * heads, dl, zero))
            q = qk_ref[0, i * FDIM : (i + 1) * FDIM, :].astype(F32)
            phi = (features(q) * live).astype(BF16)
            res = mm(phi, jnp.concatenate([dnum, zext], axis=1))
            both.append(res[:, :128])
            z_ref[...] += res[:, 128:]
        p_ref[r * (heads // 2) + pair] = own_half(both[0], 0, both[1]).astype(BF16)

    @pl.when(r == n - 1)
    def _():
        p_ref[p_ref.shape[0] - 1] = z_ref[...].astype(BF16)


def back_first(do, on, inv, qk, masks):
    n, nqk, rows = qk.shape
    heads = nqk // (2 * FDIM)
    pieces = n * heads // 2 + 1
    return call(
        back_first_body,
        (sds((n, heads, rows, 128), BF16), sds((pieces, FROWS, 128), BF16)),
        (do, on, inv, qk, masks),
        grid=(n,),
        in_specs=[by_row(x.shape[1:]) for x in (do, on, inv, qk)] + [whole(masks.shape)],
        out_specs=[by_row((heads, rows, 128)), whole((pieces, FROWS, 128))],
        scratch=[pltpu.VMEM((FROWS, 128), F32)],
    )


def back_local_body(d_ref, qk_ref, v_ref, masks_ref, c_ref, dq_ref, dk_ref, dv_ref):
    r = pl.program_id(0)
    nqk = qk_ref.shape[1]
    heads = nqk // (2 * FDIM)
    rows = v_ref.shape[1]
    masks = masks_ref[...]
    mask = doc_mask(masks, rows)
    live = masks[2:3, :]
    last = c_ref.shape[0] - 1
    for pair in range(heads // 2):
        cols = slice(pair * 128, (pair + 1) * 128)
        v_pair = v_ref[0, :, cols]
        c = c_ref[r * (heads // 2) + pair]
        dv = None
        for j in range(2):
            i = 2 * pair + j
            q = qk_ref[0, i * FDIM : (i + 1) * FDIM, :]
            k = qk_ref[0, nqk // 2 + i * FDIM : nqk // 2 + (i + 1) * FDIM, :]
            s1 = mm(q, k, TN) * 0.25 + 1.0
            a = jnp.where(mask, 0.5 * s1 * s1 + 0.5, 0.0).astype(BF16)
            d = d_ref[0, i]
            da = mm(d, with_ones(v_pair, j), NT)
            ds = jnp.where(mask, da * s1, 0.0).astype(BF16)
            z = pick_columns(
                c_ref[last], lambda row: row == r * heads + i, lambda lane: lane >= 0
            )
            dphi = mm(own_half(c, j, with_pair(z, j)), d, NT) * live
            back = features_back(q.astype(F32), dphi)
            dq_ref[0, i * FDIM : (i + 1) * FDIM, :] = (mm(k, ds, NT) * 0.25 + back).astype(BF16)
            dk_ref[0, i * FDIM : (i + 1) * FDIM, :] = mm(q, ds) * 0.25
            part = mm(own_half(d, j), a, TN)
            dv = part if dv is None else dv + part
        dv_ref[0, cols, :] = dv


def back_local(d, qk, v, masks, c):
    n, nqk, rows = qk.shape
    heads = nqk // (2 * FDIM)
    nv = heads * VDIM
    return call(
        back_local_body,
        (sds((n, nqk // 2, rows), BF16), sds((n, nqk // 2, rows), F32), sds((n, nv, rows), F32)),
        (d, qk, v, masks, c),
        grid=(n,),
        in_specs=[by_row(x.shape[1:]) for x in (d, qk, v)] + [whole(masks.shape), whole(c.shape)],
        out_specs=[by_row((nqk // 2, rows)), by_row((nqk // 2, rows)), by_row((nv, rows))],
    )


def back_last_body(
    where_ref, dq_ref, dk_ref, dv_ref, qk_ref, v_ref, masks_ref, one_ref, two_ref, h1_ref, wt_ref,
    gain_ref, x_ref, dy1_ref, dgain_mlp_ref, grad_ref, *refs,
):
    *dw_refs, dgain_ref, z_ref, acc_ref, wide_ref = refs
    r = pl.program_id(0)
    n = pl.num_programs(0)
    nqk = qk_ref.shape[1]
    heads = nqk // (2 * FDIM)
    nb, wb = dw_refs[0].shape[1] * len(dw_refs), dw_refs[0].shape[3]
    last = one_ref.shape[0] - 1
    flag = masks_ref[4:5, 0:128]
    tail = masks_ref[1:2, :]

    @pl.when(r == 0)
    def _():
        z_ref[...] = joined(one_ref[last], two_ref[last], flag).astype(BF16)
        acc_ref[...] = jnp.zeros_like(acc_ref)

    dks, dvs = [], []
    for pair in range(heads // 2):
        cols = slice(pair * 128, (pair + 1) * 128)
        at = r * (heads // 2) + pair
        dp = joined(one_ref[at], two_ref[at], flag).astype(BF16)
        v_pair = v_ref[0, :, cols]
        dv = dv_ref[0, cols, :]
        for j in range(2):
            i = 2 * pair + j
            k = qk_ref[0, nqk // 2 + i * FDIM : nqk // 2 + (i + 1) * FDIM, :].astype(F32)
            spot = r * heads + i
            z = pick_columns(
                z_ref[...],
                lambda row: jnp.logical_or(row == spot, row == spot + n * heads),
                lambda lane: lane >= 0,
            )
            dphi = mm(own_half(dp, j, with_pair(z, j)), with_ones(v_pair, j), NT) * tail
            dk = dk_ref[0, i * FDIM : (i + 1) * FDIM, :] + features_back(k, dphi)
            dks.append(dk.astype(BF16))
            phi = (features(k) * tail).astype(BF16)
            dv = dv + mm(own_half(dp, j), phi, TN)
        dvs.append(dv.astype(BF16))
    d = jnp.concatenate([dq_ref[0]] + dks + dvs, axis=0)
    total = d.shape[0]
    wide_ref[...] = mm(d, h1_ref[...]).astype(BF16)
    give_blocks(where_ref[where_ref.shape[0] - 1], wide_ref, [one.at[r, :, 0:total, :] for one in dw_refs])
    acc_ref[...] += mm(d, wt_ref[0], TN)

    @pl.when(r == n - 1)
    def _():
        dh1 = acc_ref[...]
        x = x_ref[...].astype(F32)
        scale = lax.rsqrt(jnp.mean(x * x, axis=-1, keepdims=True) + EPS)
        normed = x * scale
        dgain_ref[0:1, :] = jnp.sum(dh1 * normed, axis=0, keepdims=True)
        dgain_ref[1:2, :] = dgain_mlp_ref[...]
        dn = dh1 * gain_ref[0:1, :]
        inner = jnp.mean(dn * normed, axis=-1, keepdims=True)
        grad_ref[...] = dy1_ref[...] + scale * (dn - normed * inner)
        if nb > 1:
            groups = dw_refs[0].shape[0]
            across = groups * nb * wb // dgain_ref.shape[1]
            for q in range(groups):
                for tile in range(nb // across):
                    at = where_ref[q] * (nb // across) + tile
                    both = dgain_ref[:, pl.ds(pl.multiple_of(at * wb, wb), wb)]
                    high = both.astype(BF16).astype(F32)
                    fill = jnp.zeros((dw_refs[0].shape[2] - total - 4, wb), F32)
                    block = jnp.concatenate([high, both - high, fill], axis=0).astype(BF16)
                    for one in dw_refs:
                        for s in range(tile * across // 2, (tile + 1) * across // 2):
                            one[q, s, total:, :] = block


def give_blocks(core, wide_ref, refs):
    count, _, wb = refs[0].shape
    for index, one in enumerate(refs):
        for z in range(count):
            at = (2 * z + jnp.where(index == 0, core, 1 - core)) * wb if len(refs) == 2 else 0
            if len(refs) == 2:
                at = pl.multiple_of(at, wb)
            one[z] = wide_ref[:, pl.ds(at, wb)]


def back_last(where, dq, dk, dv, qk, v, masks, one, two, h1, w, gain, x, dy1, dgain_mlp, nb):
    n, nqk, rows = qk.shape
    _, total, d = w.shape
    shapes = [(n, 1, total + 16, d)] if nb == 1 else [(n, nb // 2, total + 16, d // nb)] * 2
    ins = (where, dq, dk, dv, qk, v, masks, one, two, h1, w, gain, x, dy1, dgain_mlp)
    return call(
        back_last_body,
        (sds((rows, d), F32), *[sds(shape, BF16) for shape in shapes], sds((2, d), F32)),
        ins,
        grid=(n,),
        in_specs=[pl.BlockSpec(memory_space=pltpu.SMEM)]
        + [by_row(y.shape[1:]) for y in (dq, dk, dv, qk, v)]
        + [whole(y.shape) for y in (masks, one, two, h1)]
        + [by_row(w.shape[1:])]
        + [whole(y.shape) for y in (gain, x, dy1, dgain_mlp)],
        out_specs=[whole((rows, d)), *[whole(shape) for shape in shapes], whole((2, d))],
        scratch=[
            pltpu.VMEM((FROWS, 128), BF16),
            pltpu.VMEM((rows, d), F32),
            pltpu.VMEM((total, d), BF16),
        ],
        us=10,
        most=True,
    )


def out_grads_body(n, core_ref, f_ref, *refs):
    o_ref, outs, wide_ref = refs[0], refs[1:-1], refs[-1]
    for r in range(n):
        wide_ref[...] = mm(o_ref[r], f_ref[...], TN).astype(BF16)
        give_blocks(core_ref[0], wide_ref, [one.at[r] for one in outs])


def out_grads(core, o, f, nb):
    n, _, nv = o.shape
    d = f.shape[1]
    shapes = [(n, 1, nv, d)] if nb == 1 else [(n, nb // 2, nv, d // nb)] * 2
    return call(
        functools.partial(out_grads_body, n),
        [sds(shape, BF16) for shape in shapes],
        (core, f, o),
        scratch=[pltpu.VMEM((nv, d), BF16)],
        smem=1,
        us=3,
    )


def xor_pairs(size, r):
    return [(i, i ^ r) for i in range(size)]


def swap(parts):
    size = lax.axis_size("head")
    return [parts[0]] + [lax.ppermute(parts[r], "head", xor_pairs(size, r)) for r in range(1, size)]


def halves(x):
    return [x[: x.shape[0] // 2], x[x.shape[0] // 2 :]]


def sum_parts(parts):
    total = parts[0].astype(F32)
    for part in parts[1:]:
        total = total + part.astype(F32)
    return total.astype(parts[0].dtype)


def spread(x):
    return [[one] for one in swap([x] * lax.axis_size("head"))]


def spread_halves(pair):
    size = lax.axis_size("head")
    a, b = pair

    def send(x, r):
        return lax.ppermute(x, "head", xor_pairs(size, r))

    if size != 4:
        return [[a, b]] + [[send(a, r), send(b, r)] for r in range(1, size)]
    ax, by = send(a, 1), send(b, 2)
    ay, bx = send(a, 2), send(b, 1)
    return [[a, b], [ax, bx], [ay, by], [send(ax, 2), send(by, 1)]]


def shifted(x, step):
    size = lax.axis_size("seq")
    return lax.ppermute(x, "seq", [(i, i + step) for i in range(size) if 0 <= i + step < size])


def halved(x, first=1, stop=None):
    size, me = lax.axis_size("seq"), lax.axis_index("seq")
    k = first
    while k < (stop or size):
        x = x.reshape((x.shape[0] // 2, 2) + x.shape[1:])
        bit = (me // k) % 2
        keep = lax.dynamic_index_in_dim(x, bit, 1, keepdims=False)
        send = lax.dynamic_index_in_dim(x, 1 - bit, 1, keepdims=False)
        got = lax.ppermute(send, "seq", xor_pairs(size, k))
        x = (keep.astype(F32) + got.astype(F32)).astype(x.dtype)
        k *= 2
    return x


def carried(x, labels, step, join, before):
    size, me = lax.axis_size("seq"), lax.axis_index("seq")
    reach = max(size // 4, 1)
    k = 1
    while 2 * k < reach:
        other = jnp.take(labels, jnp.clip(me - step * k, 0, size - 1))
        flag = (other == jnp.take(labels, me)).astype(F32)
        x = join(x, shifted(x, step * k), flag)
        k *= 2
    one = shifted(x, step)
    one, before = lax.optimization_barrier((one, before))
    return one, shifted(one, step * k)


def on_device(
    tokens, doc_ids, query_weight, key_weight, value_weight, out_weight,
    gate_weight, up_weight, down_weight, mix_gain, mlp_gain, cotangent,
):
    n, blocks = lax.axis_size("head"), lax.axis_size("seq")
    here, me = lax.axis_index("head"), lax.axis_index("seq")
    rows, d = tokens.shape[1:]
    wb = d // blocks
    nb = blocks if wb % 128 == 0 else 1
    heads = query_weight.shape[1] // FDIM
    nqkv = 2 * heads * FDIM + heads * VDIM
    nv = heads * VDIM
    ff = gate_weight.shape[1]
    x, cot = tokens[0], cotangent[0]

    piece = mix_gain.shape[0]
    doc_rows = rows // wb
    extra = -(-(2 + doc_rows) // 16) * 16
    pack = call(
        pack_body,
        sds((nqkv + extra, wb), BF16),
        (
            query_weight.T, key_weight.T, value_weight, mix_gain.reshape(1, -1), mlp_gain.reshape(1, -1),
            doc_ids.reshape(doc_rows, wb),
        ),
        us=2,
        most=True,
    )
    out_slices = swap([out_weight] * n)
    pack = lax.all_gather(pack, "seq")
    down_late, pack = lax.optimization_barrier((down_weight, pack))
    second = lax.all_gather(jnp.concatenate([*out_slices, down_late], axis=0), "seq")

    def gathered(w):
        return w if nb == blocks else jnp.transpose(w, (1, 0, 2)).reshape(1, w.shape[1], d)

    def unblocked(w):
        if nb == blocks:
            return w
        w = w.reshape(w.shape[1:-1] + (blocks, wb))
        return jnp.moveaxis(w, -2, 0)

    core = (me % 2).reshape(1)
    half = blocks // 2
    mine = lax.dynamic_slice_in_dim(pack, core[0] * half, half)
    other = lax.dynamic_slice_in_dim(pack, (1 - core[0]) * half, half)
    mine = swap([mine] * n)
    pairs = [[mine[0], other]]
    pairs += [[one, lax.ppermute(one, "seq", xor_pairs(blocks, 1))] for one in mine[1:]]
    small = jnp.stack([jnp.stack([one[:, nqkv : nqkv + 2, :piece] for one in pair]) for pair in pairs])
    small = jnp.take(jnp.take(small, here ^ jnp.arange(n), axis=0), core[0] ^ jnp.arange(2), axis=1)
    gains = jnp.transpose(small.reshape(n, blocks, 2, piece), (2, 0, 1, 3)).reshape(2, 1, d)
    gain_mix, gain_mlp = gains[0].astype(F32), gains[1].astype(F32)
    docs = pack[:, nqkv + 2 : nqkv + 2 + doc_rows].reshape(blocks, rows).astype(F32)
    segs = jnp.take(docs, me, axis=0)
    lasts = docs[:, -1]
    if nb != blocks:
        pairs = [
            [gathered(jnp.where(core[0] == 0, jnp.concatenate(p), jnp.concatenate(p[::-1])))] for p in pairs
        ]
    cot_late, pairs[1:] = lax.optimization_barrier((cot, pairs[1:]))
    wide = call(pack_two_body, sds((2 * ff, wb), BF16), (gate_weight.T, up_weight.T), us=2)

    before = jnp.where(me > 0, jnp.take(lasts, jnp.maximum(me - 1, 0)), -1.0)
    final_label = jnp.take(lasts, me)
    labels_back = jnp.concatenate([jnp.full((1,), -1.0), lasts[:-1]])

    def join(a, b, flag):
        return (a.astype(F32) + b.astype(F32) * flag).astype(BF16)

    def flag_of(labels, step):
        reach = max(blocks // 4, 1)
        k = 1
        while 2 * k < reach:
            k *= 2
        near = jnp.take(labels, jnp.clip(me - step, 0, blocks - 1))
        far = jnp.take(labels, jnp.clip(me - step * (1 + k), 0, blocks - 1))
        return (near == far).astype(F32)

    masks = jnp.stack(
        [
            segs,
            (segs == final_label).astype(F32),
            (segs == before).astype(F32),
            jnp.full((rows,), 1.0) * flag_of(lasts, 1),
            jnp.full((rows,), 1.0) * flag_of(labels_back, -1),
        ]
        + [jnp.zeros_like(segs)] * 3
    )

    h1, qk, v, sums, w_qkv = project(core, x, gain_mix, masks, pairs, heads)
    cots = swap([cot_late] * n)
    nd = local(qk, v, masks)
    one, two = carried(sums, lasts, 1, join, nd)
    wide, two = lax.optimization_barrier((wide, two))
    w_mlp = widen(gathered(lax.all_gather(wide, "seq")))
    w_out, w_down = spread_out(gathered(second), ff)
    dhid = prepare(w_down, cots)
    two, w_out = lax.optimization_barrier((two, w_out))
    o, on, inv, c = carry(nd, qk, masks, one, two)
    y1, h2 = middle(x, o, w_out, gain_mlp)
    h2s = spread_halves(h2)
    res = [mlp(r, h2s[r], dhid, w_mlp) for r in range(n)]
    dparts, hid, dg, du = ([t[k] for t in res] for k in range(4))
    dparts = swap(dparts)
    oparts = mlp_out(hid, w_down)
    dmlp = mlp_grads(h2s, cots, hid, dg, du, nb)
    dparts, oparts, dmlp = lax.optimization_barrier((dparts, oparts, dmlp))
    dy1, dgain_mlp, f, do = turn(dparts, y1, cot, gain_mlp, w_out)
    oparts, f = lax.optimization_barrier((oparts, f))
    oparts = swap(oparts)
    dext, dsums = back_first(do, on, inv, qk, masks)
    dq, dk, dv = back_local(dext, qk, v, masks, c)
    back_one, back_two = carried(dsums, labels_back, -1, join, (dq, dk, dv))

    def split(w):
        if nb == blocks:
            return w
        w = unblocked(w[0][:, 0][None])
        w = jnp.moveaxis(w.reshape((half, 2) + w.shape[1:]), 2, 0)
        return [lax.dynamic_index_in_dim(w, bit, 2, keepdims=False) for bit in (core[0], 1 - core[0])]

    def reduced(keep, give):
        got = lax.ppermute(give, "seq", xor_pairs(blocks, 1))
        w = (keep.astype(F32) + got.astype(F32)).astype(BF16)
        w = sum_parts(swap([w[r] for r in range(n)]))
        return halved(w, 2)

    dout = reduced(*split(out_grads(core, o, f, nb)))
    dmlp, back_two, oparts = lax.optimization_barrier((dmlp, back_two, oparts))
    dmlp = lax.psum_scatter(unblocked(dmlp), "seq", tiled=True)[0].astype(F32)
    where = jnp.concatenate([here ^ jnp.arange(n, dtype=jnp.int32), core])
    grad_tokens, *dqkv, dgains = back_last(
        where, dq, dk, dv, qk, v, masks, back_one, back_two, h1, w_qkv, gain_mix, x, dy1, dgain_mlp, nb
    )
    dqkv = reduced(*split(dqkv))[0].astype(F32)
    dout = dout[0].astype(F32)
    if nb == blocks:
        parts = dqkv[nqkv : nqkv + 2] + dqkv[nqkv + 2 : nqkv + 4]
        total = lax.dynamic_slice_in_dim(parts, me % (wb // piece) * piece, piece, axis=1)
    else:
        total = lax.psum_scatter(dgains, ("head", "seq"), scatter_dimension=1, tiled=True)
    output = y1
    for part in oparts:
        output = output + part.astype(F32)

    kq = heads * FDIM
    return (
        output.astype(BF16)[None],
        grad_tokens[None],
        dqkv[:kq].T,
        dqkv[kq : 2 * kq].T,
        dqkv[2 * kq : nqkv].T,
        dout,
        dmlp[:ff].T,
        dmlp[ff : 2 * ff].T,
        dmlp[2 * ff :],
        total[0],
        total[1],
    )


def solution(mesh):
    placed = (
        P("head", "seq", None),
        P("head", "seq"),
        P("seq", "head"),
        P("seq", "head"),
        P("seq", "head"),
        P("head", "seq"),
        P("seq", "head"),
        P("seq", "head"),
        P("head", "seq"),
        P(("head", "seq")),
        P(("head", "seq")),
        P("head", "seq", None),
    )
    return jax.shard_map(
        on_device,
        mesh=mesh,
        in_specs=placed,
        out_specs=(
            P("head", "seq", None),
            P("head", "seq", None),
            P("seq", "head"),
            P("seq", "head"),
            P("seq", "head"),
            P("head", "seq"),
            P("seq", "head"),
            P("seq", "head"),
            P("head", "seq"),
            P(("head", "seq")),
            P(("head", "seq")),
        ),
        check_vma=False,
    )
```

```python
import functools

import jax
import jax.numpy as jnp
from jax import lax
from jax.experimental import pallas as pl
from jax.experimental.pallas import tpu as pltpu
from jax.sharding import PartitionSpec as P

FDIM = 16
VDIM = 64
EPS = 1e-06
ROOT_HALF = 0.7071067811865476
FROWS = 11 * FDIM
F32 = jnp.float32
BF16 = jnp.bfloat16
VMEM_BYTES = 24 * 1024 * 1024
VMEM_MOST = 56 * 1024 * 1024
K1MOST = True
FAR = False

NN = (((1,), (0,)), ((), ()))
NT = (((1,), (1,)), ((), ()))
TN = (((0,), (0,)), ((), ()))


def mm(a, b, dims=NN):
    return lax.dot_general(a, b, dims, preferred_element_type=F32)


def call(body, outs, ins, grid=None, in_specs=None, out_specs=None, scratch=(), smem=0, us=5, most=False):
    kwargs = {}
    if smem:
        spaces = [pltpu.SMEM] * smem + [pltpu.VMEM] * (len(ins) - smem)
        kwargs = dict(in_specs=[pl.BlockSpec(memory_space=space) for space in spaces])
    if grid is not None:
        kwargs = dict(grid=grid, in_specs=in_specs, out_specs=out_specs)
    return pl.pallas_call(
        body,
        out_shape=outs,
        scratch_shapes=list(scratch),
        compiler_params=pltpu.CompilerParams(vmem_limit_bytes=VMEM_MOST if most else VMEM_BYTES),
        cost_estimate=pl.CostEstimate(flops=0, bytes_accessed=us * 600000, transcendentals=0),
        **kwargs,
    )(*ins)


def sds(shape, dtype):
    return jax.ShapeDtypeStruct(shape, dtype)


def whole(shape):
    return pl.BlockSpec(shape, lambda r: (0,) * len(shape))


def by_row(shape):
    return pl.BlockSpec((1,) + tuple(shape), lambda r: (r,) + (0,) * len(shape))


def coef(d):
    return ROOT_HALF if d in (0, FDIM // 2) else 1.0


def features(w):
    half = w * 0.5
    rows = [half]
    for d in range(FDIM // 2 + 1):
        other = half if d == 0 else pltpu.roll(half, FDIM - d, 0)
        rows.append(half * other * coef(d))
    first = lax.broadcasted_iota(jnp.int32, half.shape, 0) == 0
    rows.append(jnp.where(first, 1.0, 0.0))
    return jnp.concatenate(rows, axis=0)


def features_back(w, grad):
    half = w * 0.5
    total = grad[:FDIM]
    for d in range(FDIM // 2 + 1):
        part = grad[FDIM * (d + 1) : FDIM * (d + 2)]
        if d == 0:
            total = total + part * half * (2.0 * coef(0))
        else:
            near = part * pltpu.roll(half, FDIM - d, 0)
            far = pltpu.roll(part * half, d, 0)
            total = total + (near + far) * coef(d)
    return total * 0.5


def lanes(shape):
    return lax.broadcasted_iota(jnp.int32, shape, len(shape) - 1)


def one_hot_lanes(rows, index):
    lane = lanes((rows, 128))
    hot = jnp.logical_or(lane == index, lane == index + FDIM)
    return jnp.where(hot, 1.0, 0.0).astype(BF16)


def own_half(x, j, other=None):
    left = lanes(x.shape) < VDIM
    keep = left if j == 0 else jnp.logical_not(left)
    return jnp.where(keep, x, jnp.zeros_like(x) if other is None else other)


def pick_columns(z, column, spots):
    row = lax.broadcasted_iota(jnp.int32, (128, 128), 0)
    hot = jnp.where(column(row), 1.0, 0.0) * jnp.where(spots(lanes((128, 128))), 1.0, 0.0)
    return mm(z, hot.astype(BF16))


def doc_mask(masks, rows):
    seg = masks[0:1, :]
    col = jnp.transpose(masks)[:, 0:1]
    causal = lax.broadcasted_iota(jnp.int32, (rows, rows), 0) >= lax.broadcasted_iota(
        jnp.int32, (rows, rows), 1
    )
    return jnp.logical_and(causal, col == seg)


def with_pair(z, j):
    lane = lanes(z.shape)
    base = VDIM if j == 0 else 0
    high = z.astype(BF16)
    low = (z - high.astype(F32)).astype(BF16)
    zero = jnp.zeros_like(high)
    return jnp.where(lane == base, high, jnp.where(lane == base + FDIM, low, zero))


def moved_pair(z, spot, j):
    base = VDIM if j == 0 else 0
    z = pltpu.roll(z, lax.rem(base - spot + 128, 128), 1)
    lane = lanes(z.shape)
    keep = jnp.logical_or(lane == base, lane == base + FDIM)
    return jnp.where(keep, z, 0.0).astype(BF16)


def with_ones(x, j):
    lane = lanes(x.shape)
    base = VDIM if j == 0 else 0
    hot = jnp.where(jnp.logical_or(lane == base, lane == base + FDIM), 1.0, 0.0).astype(x.dtype)
    return own_half(x, j, hot)


def join_rows(refs):
    return refs[0][...] if len(refs) == 1 else jnp.concatenate([one[...] for one in refs], axis=0)


def grouped(refs, n):
    k = len(refs) // n
    return [refs[i * k : (i + 1) * k] for i in range(n)]


def flat(lists):
    return [x for one in lists for x in one]


def take_row(r, groups, ref):
    for index, one in enumerate(groups):
        @pl.when(r == index)
        def _():
            ref[...] = join_rows(one)


def give_row(r, refs, value):
    for index, one in enumerate(refs):
        @pl.when(r == index)
        def _():
            one[...] = value


def pack_body(q_ref, k_ref, v_ref, mix_ref, mlp_ref, docs_ref, pack_ref):
    at = 0
    for one in (q_ref, k_ref):
        pack_ref[at : at + one.shape[0], :] = one[...]
        at += one.shape[0]
    pack_ref[at : at + v_ref.shape[1], :] = v_ref[...].T
    at += v_ref.shape[1]
    wb = pack_ref.shape[1]
    extra = pack_ref.shape[0] - at
    rows = []
    for one in (mix_ref, mlp_ref):
        fill = jnp.zeros((1, wb - one.shape[1]), F32)
        rows.append(jnp.concatenate([one[...].astype(F32), fill], axis=1))
    rows.append(docs_ref[...].astype(F32))
    rows.append(jnp.zeros((extra - 2 - docs_ref.shape[0], wb), F32))
    pack_ref[at:, :] = jnp.concatenate(rows, axis=0).astype(BF16)


def pack_two_body(gate_ref, up_ref, pack_ref):
    ff = gate_ref.shape[0]
    pack_ref[:ff, :] = gate_ref[...]
    pack_ref[ff:, :] = up_ref[...]


def project_body(n, piece, where_ref, x_ref, gain_ref, masks_ref, *refs):
    blocks = grouped(refs[:-7], n)
    h1_ref, qk_ref, v_ref, p_ref, wt_ref, gains_ref, z_ref = refs[-7:]
    r = pl.program_id(0)
    heads = qk_ref.shape[1] // (2 * FDIM)
    total = wt_ref.shape[1]
    core = where_ref[n]

    @pl.when(r == 0)
    def _():
        if piece:
            for q, halves in enumerate(blocks):
                for other, half in enumerate(halves):
                    count, _, wb = half.shape
                    tile = jnp.zeros((16, wb), F32)
                    for j in range(count):
                        one = half[j, total : total + 16, :].astype(F32)
                        one = jnp.where(lanes(one.shape) < piece, one, 0.0)
                        tile = tile + (one if j == 0 else pltpu.roll(one, j * piece, 1))
                    side = core if other == 0 else 1 - core
                    at = pl.multiple_of((where_ref[q] * 2 + side) * wb, wb)
                    gains_ref[:, pl.ds(at, wb)] = tile[:8]
        else:
            gains_ref[...] = gain_ref[...]
        x = x_ref[...].astype(F32)
        normed = x * lax.rsqrt(jnp.mean(x * x, axis=-1, keepdims=True) + EPS)
        h1_ref[...] = (normed * gains_ref[0:1, :]).astype(BF16)
        z_ref[...] = jnp.zeros_like(z_ref)

    for index, halves in enumerate(blocks):

        @pl.when(r == index)
        def _():
            for other, half in enumerate(halves):
                count, _, wb = half.shape
                side = core if other == 0 else 1 - core
                for j in range(count):
                    at = j * wb if count * wb == wt_ref.shape[2] else (side * count + j) * wb
                    if not isinstance(at, int):
                        at = pl.multiple_of(at, wb)
                    wt_ref[0, :, pl.ds(at, wb)] = half[j, :total, :]

    h1 = h1_ref[...]
    nqk = qk_ref.shape[1]
    qk = mm(wt_ref[0, :nqk, :], h1, NT).astype(BF16)
    qk_ref[0] = qk
    v = mm(h1, wt_ref[0, nqk:, :], NT).astype(BF16)
    v_ref[0] = v
    tail = masks_ref[1:2, :]
    rows = v.shape[0]
    for pair in range(heads // 2):
        v_pair = v[:, pair * 128 : (pair + 1) * 128]
        both = []
        for j in range(2):
            i = 2 * pair + j
            k = qk[nqk // 2 + i * FDIM : nqk // 2 + (i + 1) * FDIM].astype(F32)
            phi = (features(k) * tail).astype(BF16)
            rhs = jnp.concatenate([v_pair, one_hot_lanes(rows, r * heads + i)], axis=1)
            res = mm(phi, rhs)
            both.append(res[:, :128])
            z_ref[...] += res[:, 128:]
        p_ref[r * (heads // 2) + pair] = own_half(both[0], 0, both[1]).astype(BF16)

    @pl.when(r == pl.num_programs(0) - 1)
    def _():
        p_ref[p_ref.shape[0] - 1] = z_ref[...].astype(BF16)


def project(where, x, gain, masks, blocks, heads, piece):
    n = len(blocks)
    rows, d = x.shape
    nqk, nv = 2 * heads * FDIM, heads * VDIM
    sums = n * heads // 2 + 1
    ins = (where, x, gain, masks, *flat(blocks))
    return call(
        functools.partial(project_body, n, piece),
        (
            sds((rows, d), BF16),
            sds((n, nqk, rows), BF16),
            sds((n, rows, nv), BF16),
            sds((sums, FROWS, 128), BF16),
            sds((n, nqk + nv, d), BF16),
            sds((8, d), F32),
        ),
        ins,
        grid=(n,),
        in_specs=[pl.BlockSpec(memory_space=pltpu.SMEM)] + [whole(x.shape) for x in ins[1:]],
        out_specs=[
            whole((rows, d)),
            by_row((nqk, rows)),
            by_row((rows, nv)),
            whole((sums, FROWS, 128)),
            by_row((nqk + nv, d)),
            whole((8, d)),
        ],
        scratch=[pltpu.VMEM((FROWS, 128), F32)],
        us=7,
        most=K1MOST,
    )


def local_body(qk_ref, v_ref, masks_ref, nd_ref):
    nqk = qk_ref.shape[1]
    heads = nqk // (2 * FDIM)
    rows = v_ref.shape[1]
    mask = doc_mask(masks_ref[...], rows)
    for pair in range(heads // 2):
        v_pair = v_ref[0, :, pair * 128 : (pair + 1) * 128]
        acc = None
        for j in range(2):
            i = 2 * pair + j
            q = qk_ref[0, i * FDIM : (i + 1) * FDIM, :]
            k = qk_ref[0, nqk // 2 + i * FDIM : nqk // 2 + (i + 1) * FDIM, :]
            s1 = mm(q, k, TN) * 0.25 + 1.0
            a = jnp.where(mask, 0.5 * s1 * s1 + 0.5, 0.0).astype(BF16)
            ones = own_half(jnp.ones((rows, 128), BF16), j)
            part = mm(a, jnp.concatenate([own_half(v_pair, j), ones], axis=1))
            acc = part if acc is None else acc + part
        nd_ref[0, pair] = acc


def local(qk, v, masks):
    n, nqk, rows = qk.shape
    heads = nqk // (2 * FDIM)
    return call(
        local_body,
        sds((n, heads // 2, rows, 256), F32),
        (qk, v, masks),
        grid=(n,),
        in_specs=[by_row(qk.shape[1:]), by_row(v.shape[1:]), whole(masks.shape)],
        out_specs=by_row((heads // 2, rows, 256)),
    )


def joined(first, second, flag):
    return first.astype(F32) + second.astype(F32) * flag


def carry_body(nd_ref, qk_ref, masks_ref, one_ref, two_ref, o_ref, on_ref, inv_ref, c_ref):
    r = pl.program_id(0)
    n = pl.num_programs(0)
    nqk = qk_ref.shape[1]
    heads = nqk // (2 * FDIM)
    last = one_ref.shape[0] - 1

    @pl.when(r == 0)
    def _():
        c_ref[last] = joined(one_ref[last], two_ref[last], masks_ref[3:4, 0:128]).astype(BF16)

    flag = masks_ref[3:4, 0:128]
    live = masks_ref[2:3, :]
    for pair in range(heads // 2):
        at = r * (heads // 2) + pair
        c = joined(one_ref[at], two_ref[at], flag).astype(BF16)
        c_ref[at] = c
        acc = nd_ref[0, pair]
        for j in range(2):
            i = 2 * pair + j
            q = qk_ref[0, i * FDIM : (i + 1) * FDIM, :].astype(F32)
            phi = (features(q) * live).astype(BF16)
            z = pick_columns(
                c_ref[last],
                lambda row: row == r * heads + i,
                lambda lane: (lane < VDIM) if j == 0 else (lane >= VDIM),
            ).astype(BF16)
            acc = acc + mm(phi, jnp.concatenate([own_half(c, j), z], axis=1), TN)
        inv = 1.0 / acc[:, 128:]
        on = acc[:, :128] * inv
        cols = slice(pair * 128, (pair + 1) * 128)
        o_ref[0, :, cols] = on.astype(BF16)
        on_ref[0, :, cols] = on
        inv_ref[0, :, cols] = inv


def carry(nd, qk, masks, one, two):
    n, nqk, rows = qk.shape
    heads = nqk // (2 * FDIM)
    nv = heads * VDIM
    return call(
        carry_body,
        (
            sds((n, rows, nv), BF16),
            sds((n, rows, nv), F32),
            sds((n, rows, nv), F32),
            sds(one.shape, BF16),
        ),
        (nd, qk, masks, one, two),
        grid=(n,),
        in_specs=[
            by_row(nd.shape[1:]),
            by_row(qk.shape[1:]),
            whole(masks.shape),
            whole(one.shape),
            whole(two.shape),
        ],
        out_specs=[by_row((rows, nv))] * 3 + [whole(one.shape)],
        most=True,
    )


def middle_body(x_ref, gain_ref, o_ref, w_ref, y1_ref, *h2_refs):
    n, _, width = o_ref.shape
    acc = x_ref[...].astype(F32)
    for r in range(n):
        acc = acc + mm(o_ref[r], w_ref[r * width : (r + 1) * width, :])
    y1_ref[...] = acc
    scale = lax.rsqrt(jnp.mean(acc * acc, axis=-1, keepdims=True) + EPS)
    give_rows(h2_refs, (acc * scale * gain_ref[1:2, :]).astype(BF16))


def give_rows(refs, value):
    at = 0
    for one in refs:
        one[...] = value[at : at + one.shape[0]]
        at += one.shape[0]


def middle(x, o, wo, gain):
    rows, d = x.shape
    res = call(
        middle_body,
        (sds((rows, d), F32), *[sds((rows // 2, d), BF16)] * 2),
        (x, gain, o, wo),
        us=4,
    )
    return res[0], res[1:]


def spread_out_body(w_ref, out_ref, down_ref):
    nb, _, wb = w_ref.shape
    split = out_ref.shape[0]
    for s in range(nb):
        out_ref[:, s * wb : (s + 1) * wb] = w_ref[s, :split, :]
        down_ref[:, s * wb : (s + 1) * wb] = w_ref[s, split:, :]


def spread_out(w, ff):
    nb, total, wb = w.shape
    d = nb * wb
    return call(spread_out_body, (sds((total - ff, d), BF16), sds((ff, d), BF16)), (w,), us=4)


def prepare_body(n, down_ref, *refs):
    cots, out_ref = refs[:n], refs[n]
    for r in range(n):
        out_ref[r] = mm(cots[r][...], down_ref[...], NT).astype(BF16)


def prepare(down, cots):
    n = len(cots)
    return call(
        functools.partial(prepare_body, n),
        sds((n, cots[0].shape[0], down.shape[0]), BF16),
        (down, *cots),
    )


def widen_body(w_ref, wide_ref):
    nb, _, wb = w_ref.shape
    for s in range(nb):
        wide_ref[:, s * wb : (s + 1) * wb] = w_ref[s]


def widen(w):
    nb, total, wb = w.shape
    return call(widen_body, sds((total, nb * wb), BF16), (w,))


def mlp_body(first_ref, second_ref, dhid_ref, w_ref, dh_ref, hid_ref, dg_ref, du_ref):
    ff = hid_ref.shape[1]
    h2 = join_rows((first_ref, second_ref))
    gate_w, up_w = w_ref[0:ff, :], w_ref[ff : 2 * ff, :]
    dhid = dhid_ref[0].astype(F32)
    g = mm(h2, gate_w, NT)
    u = mm(h2, up_w, NT)
    sig = jax.nn.sigmoid(g)
    act = g * sig
    hid_ref[...] = (act * u).astype(BF16)
    dg = (dhid * u * sig * (1.0 + g * (1.0 - sig))).astype(BF16)
    du = (dhid * act).astype(BF16)
    dg_ref[...] = dg
    du_ref[...] = du
    dh_ref[...] = (mm(dg, gate_w) + mm(du, up_w)).astype(BF16)


def mlp(index, h2, dhid, w):
    half, d = h2[0].shape
    rows = 2 * half
    ff = w.shape[0] // 2
    return call(
        mlp_body,
        (sds((rows, d), BF16), *[sds((rows, ff), BF16)] * 3),
        (*h2, dhid, w),
        grid=(1,),
        in_specs=[whole((half, d))] * 2
        + [pl.BlockSpec((1, rows, ff), lambda r: (index, 0, 0)), whole((2 * ff, d))],
        out_specs=[whole((rows, d))] + [whole((rows, ff))] * 3,
    )


def mlp_out_body(n, w_ref, *refs):
    for r in range(n):
        refs[n + r][...] = mm(refs[r][...], w_ref[...]).astype(BF16)


def mlp_out(hid, w):
    n = len(hid)
    return call(
        functools.partial(mlp_out_body, n),
        [sds((hid[0].shape[0], w.shape[1]), BF16)] * n,
        (w, *hid),
    )


def mlp_grads_body(n, *refs):
    h2, cot = grouped(refs[: 2 * n], n), grouped(refs[2 * n : 3 * n], n)
    hid, dg, du = (refs[(3 + k) * n : (4 + k) * n] for k in range(3))
    o_ref, ff = refs[6 * n], hid[0].shape[1]
    nb, _, wb = o_ref.shape
    for k, (left, right) in enumerate(((dg, h2), (du, h2), (hid, cot))):
        acc = None
        for r in range(n):
            part = mm(left[r][...], join_rows(right[r]), TN)
            acc = part if acc is None else acc + part
        acc = acc.astype(BF16)
        for s in range(nb):
            o_ref[s, k * ff : (k + 1) * ff, :] = acc[:, s * wb : (s + 1) * wb]


def mlp_grads(h2, cot, hid, dg, du, nb):
    n = len(h2)
    d, ff = h2[0][0].shape[1], hid[0].shape[1]
    ins = (*flat(h2), *cot, *hid, *dg, *du)
    return call(
        functools.partial(mlp_grads_body, n),
        sds((nb, 3 * ff, d // nb), BF16),
        ins,
        grid=(1,),
        in_specs=[whole(x.shape) for x in ins],
        out_specs=whole((nb, 3 * ff, d // nb)),
        us=9,
    )


def turn_body(n, y1_ref, cot_ref, gain_ref, *refs):
    parts, w_ref = refs[:n], refs[n]
    dy1_ref, dgain_ref, *f_refs = refs[n + 1 : n + 4]
    do_ref = refs[n + 4]
    rows_of = do_ref.shape[2]
    dh2 = parts[0][...].astype(F32)
    for r in range(1, n):
        dh2 = dh2 + parts[r][...].astype(F32)
    y1 = y1_ref[...]
    scale = lax.rsqrt(jnp.mean(y1 * y1, axis=-1, keepdims=True) + EPS)
    normed = y1 * scale
    dgain_ref[...] = jnp.sum(dh2 * normed, axis=0, keepdims=True)
    dn = dh2 * gain_ref[1:2, :]
    inner = jnp.mean(dn * normed, axis=-1, keepdims=True)
    dy1 = cot_ref[...].astype(F32) + scale * (dn - normed * inner)
    dy1_ref[...] = dy1
    f = dy1.astype(BF16)
    give_rows(f_refs, f)
    for r in range(n):
        do_ref[r] = mm(f, w_ref[r * rows_of : (r + 1) * rows_of, :], NT).astype(BF16)


def turn(parts, y1, cot, gain, wo):
    n = len(parts)
    rows, d = y1.shape
    nv = wo.shape[0] // n
    res = call(
        functools.partial(turn_body, n),
        (
            sds((rows, d), F32),
            sds((1, d), F32),
            sds((rows, d), BF16),
            sds((n, rows, nv), BF16),
        ),
        (y1, cot, gain, *parts, wo),
    )
    return res


def back_first_body(do_ref, on_ref, inv_ref, qk_ref, masks_ref, d_ref, p_ref, z_ref):
    r = pl.program_id(0)
    n = pl.num_programs(0)
    nqk = qk_ref.shape[1]
    heads = nqk // (2 * FDIM)
    rows = do_ref.shape[1]

    @pl.when(r == 0)
    def _():
        z_ref[...] = jnp.zeros_like(z_ref)

    live = masks_ref[2:3, :]
    lane = lanes((rows, 128))
    for pair in range(heads // 2):
        cols = slice(pair * 128, (pair + 1) * 128)
        wide = do_ref[0, :, cols].astype(F32) * inv_ref[0, :, cols]
        dnum = wide.astype(BF16)
        prod = -(wide * on_ref[0, :, cols])
        high = prod.astype(BF16)
        low = (prod - high.astype(F32)).astype(BF16)
        both = []
        for j in range(2):
            i = 2 * pair + j
            row = lax.broadcasted_iota(jnp.int32, (128, 128), 0)
            hot = jnp.where((row < VDIM) if j == 0 else (row >= VDIM), 1.0, 0.0).astype(BF16)
            dden = mm(high, hot) + mm(low, hot)
            d_ref[0, i] = own_half(dnum, j, with_pair(dden, j))
            dh = dden.astype(BF16)
            dl = (dden - dh.astype(F32)).astype(BF16)
            zero = jnp.zeros_like(dh)
            spot = r * heads + i
            zext = jnp.where(lane == spot, dh, jnp.where(lane == spot + n * heads, dl, zero))
            q = qk_ref[0, i * FDIM : (i + 1) * FDIM, :].astype(F32)
            phi = (features(q) * live).astype(BF16)
            res = mm(phi, jnp.concatenate([dnum, zext], axis=1))
            both.append(res[:, :128])
            z_ref[...] += res[:, 128:]
        p_ref[r * (heads // 2) + pair] = own_half(both[0], 0, both[1]).astype(BF16)

    @pl.when(r == n - 1)
    def _():
        p_ref[p_ref.shape[0] - 1] = z_ref[...].astype(BF16)


def back_first(do, on, inv, qk, masks):
    n, nqk, rows = qk.shape
    heads = nqk // (2 * FDIM)
    pieces = n * heads // 2 + 1
    return call(
        back_first_body,
        (sds((n, heads, rows, 128), BF16), sds((pieces, FROWS, 128), BF16)),
        (do, on, inv, qk, masks),
        grid=(n,),
        in_specs=[by_row(x.shape[1:]) for x in (do, on, inv, qk)] + [whole(masks.shape)],
        out_specs=[by_row((heads, rows, 128)), whole((pieces, FROWS, 128))],
        scratch=[pltpu.VMEM((FROWS, 128), F32)],
    )


def back_local_body(d_ref, qk_ref, v_ref, masks_ref, c_ref, dq_ref, dk_ref, dv_ref):
    r = pl.program_id(0)
    nqk = qk_ref.shape[1]
    heads = nqk // (2 * FDIM)
    rows = v_ref.shape[1]
    masks = masks_ref[...]
    mask = doc_mask(masks, rows)
    live = masks[2:3, :]
    last = c_ref.shape[0] - 1
    for pair in range(heads // 2):
        cols = slice(pair * 128, (pair + 1) * 128)
        v_pair = v_ref[0, :, cols]
        c = c_ref[r * (heads // 2) + pair]
        dv = None
        for j in range(2):
            i = 2 * pair + j
            q = qk_ref[0, i * FDIM : (i + 1) * FDIM, :]
            k = qk_ref[0, nqk // 2 + i * FDIM : nqk // 2 + (i + 1) * FDIM, :]
            s1 = mm(q, k, TN) * 0.25 + 1.0
            a = jnp.where(mask, 0.5 * s1 * s1 + 0.5, 0.0).astype(BF16)
            d = d_ref[0, i]
            da = mm(d, with_ones(v_pair, j), NT)
            ds = jnp.where(mask, da * s1, 0.0).astype(BF16)
            z = moved_pair(c_ref[last].astype(F32), r * heads + i, j)
            dphi = mm(own_half(c, j, z), d, NT) * live
            back = features_back(q.astype(F32), dphi)
            dq_ref[0, i * FDIM : (i + 1) * FDIM, :] = (mm(k, ds, NT) * 0.25 + back).astype(BF16)
            dk_ref[0, i * FDIM : (i + 1) * FDIM, :] = mm(q, ds) * 0.25
            part = mm(own_half(d, j), a, TN)
            dv = part if dv is None else dv + part
        dv_ref[0, cols, :] = dv


def back_local(d, qk, v, masks, c):
    n, nqk, rows = qk.shape
    heads = nqk // (2 * FDIM)
    nv = heads * VDIM
    return call(
        back_local_body,
        (sds((n, nqk // 2, rows), BF16), sds((n, nqk // 2, rows), F32), sds((n, nv, rows), F32)),
        (d, qk, v, masks, c),
        grid=(n,),
        in_specs=[by_row(x.shape[1:]) for x in (d, qk, v)] + [whole(masks.shape), whole(c.shape)],
        out_specs=[by_row((nqk // 2, rows)), by_row((nqk // 2, rows)), by_row((nv, rows))],
    )


def back_last_body(
    where_ref, dq_ref, dk_ref, dv_ref, qk_ref, v_ref, masks_ref, one_ref, two_ref, h1_ref, wt_ref,
    gain_ref, x_ref, dy1_ref, dgain_mlp_ref, grad_ref, *refs,
):
    *dw_refs, dgain_ref, z_ref, acc_ref, wide_ref = refs
    r = pl.program_id(0)
    n = pl.num_programs(0)
    nqk = qk_ref.shape[1]
    heads = nqk // (2 * FDIM)
    nb, wb = dw_refs[0].shape[1] * len(dw_refs), dw_refs[0].shape[3]
    last = one_ref.shape[0] - 1
    flag = masks_ref[4:5, 0:128]
    tail = masks_ref[1:2, :]

    @pl.when(r == 0)
    def _():
        z_ref[...] = joined(one_ref[last], two_ref[last], flag)
        acc_ref[...] = jnp.zeros_like(acc_ref)

    dks, dvs = [], []
    for pair in range(heads // 2):
        cols = slice(pair * 128, (pair + 1) * 128)
        at = r * (heads // 2) + pair
        dp = joined(one_ref[at], two_ref[at], flag).astype(BF16)
        v_pair = v_ref[0, :, cols]
        dv = dv_ref[0, cols, :]
        for j in range(2):
            i = 2 * pair + j
            k = qk_ref[0, nqk // 2 + i * FDIM : nqk // 2 + (i + 1) * FDIM, :].astype(F32)
            z = moved_pair(z_ref[...], r * heads + i, j)
            dphi = mm(own_half(dp, j, z), with_ones(v_pair, j), NT) * tail
            dk = dk_ref[0, i * FDIM : (i + 1) * FDIM, :] + features_back(k, dphi)
            dks.append(dk.astype(BF16))
            phi = (features(k) * tail).astype(BF16)
            dv = dv + mm(own_half(dp, j), phi, TN)
        dvs.append(dv.astype(BF16))
    d = jnp.concatenate([dq_ref[0]] + dks + dvs, axis=0)
    total = d.shape[0]
    wide_ref[...] = mm(d, h1_ref[...]).astype(BF16)
    give_blocks(where_ref, wide_ref, [one.at[r, :, 0:total, :] for one in dw_refs])
    acc_ref[...] += mm(d, wt_ref[0], TN)

    @pl.when(r == n - 1)
    def _():
        dh1 = acc_ref[...]
        x = x_ref[...].astype(F32)
        scale = lax.rsqrt(jnp.mean(x * x, axis=-1, keepdims=True) + EPS)
        normed = x * scale
        dgain_ref[0:1, :] = jnp.sum(dh1 * normed, axis=0, keepdims=True)
        dgain_ref[1:2, :] = dgain_mlp_ref[...]
        dn = dh1 * gain_ref[0:1, :]
        inner = jnp.mean(dn * normed, axis=-1, keepdims=True)
        grad_ref[...] = dy1_ref[...] + scale * (dn - normed * inner)
        if nb > 1:
            groups, count = dw_refs[0].shape[:2]
            across = groups * nb * wb // dgain_ref.shape[1]
            tiles = nb // across
            for q in range(groups):
                for z in range(count):
                    at = where_ref[q] * tiles + (where_ref[groups + 1] ^ z) * 2 // across
                    both = dgain_ref[:, pl.ds(pl.multiple_of(at * wb, wb), wb)]
                    high = both.astype(BF16).astype(F32)
                    fill = jnp.zeros((dw_refs[0].shape[2] - total - 4, wb), F32)
                    block = jnp.concatenate([high, both - high, fill], axis=0).astype(BF16)
                    for one in dw_refs:
                        one[q, z, total:, :] = block


def give_blocks(where_ref, wide_ref, refs):
    count, _, wb = refs[0].shape
    last = where_ref.shape[0] - 1
    for index, one in enumerate(refs):
        for z in range(count):
            at = 0
            if len(refs) == 2:
                core = where_ref[last - 1]
                side = core if index == 0 else 1 - core
                at = pl.multiple_of(((where_ref[last] ^ z) * 2 + side) * wb, wb)
            one[z] = wide_ref[:, pl.ds(at, wb)]


def back_last(where, dq, dk, dv, qk, v, masks, one, two, h1, w, gain, x, dy1, dgain_mlp, nb):
    n, nqk, rows = qk.shape
    _, total, d = w.shape
    shapes = [(n, 1, total + 16, d)] if nb == 1 else [(n, nb // 2, total + 16, d // nb)] * 2
    ins = (where, dq, dk, dv, qk, v, masks, one, two, h1, w, gain, x, dy1, dgain_mlp)
    return call(
        back_last_body,
        (sds((rows, d), F32), *[sds(shape, BF16) for shape in shapes], sds((2, d), F32)),
        ins,
        grid=(n,),
        in_specs=[pl.BlockSpec(memory_space=pltpu.SMEM)]
        + [by_row(y.shape[1:]) for y in (dq, dk, dv, qk, v)]
        + [whole(y.shape) for y in (masks, one, two, h1)]
        + [by_row(w.shape[1:])]
        + [whole(y.shape) for y in (gain, x, dy1, dgain_mlp)],
        out_specs=[whole((rows, d)), *[whole(shape) for shape in shapes], whole((2, d))],
        scratch=[
            pltpu.VMEM((FROWS, 128), F32),
            pltpu.VMEM((rows, d), F32),
            pltpu.VMEM((total, d), BF16),
        ],
        us=10,
        most=True,
    )


def out_grads_body(n, where_ref, f_ref, *refs):
    o_ref, outs, wide_ref = refs[0], refs[1:-1], refs[-1]
    for r in range(n):
        wide_ref[...] = mm(o_ref[r], f_ref[...], TN).astype(BF16)
        give_blocks(where_ref, wide_ref, [one.at[r] for one in outs])


def out_grads(where, o, f, nb):
    n, _, nv = o.shape
    d = f.shape[1]
    shapes = [(n, 1, nv, d)] if nb == 1 else [(n, nb // 2, nv, d // nb)] * 2
    return call(
        functools.partial(out_grads_body, n),
        [sds(shape, BF16) for shape in shapes],
        (where, f, o),
        scratch=[pltpu.VMEM((nv, d), BF16)],
        smem=1,
        us=3,
    )


def xor_pairs(size, r):
    return [(i, i ^ r) for i in range(size)]


def swap(parts):
    size = lax.axis_size("head")
    return [parts[0]] + [lax.ppermute(parts[r], "head", xor_pairs(size, r)) for r in range(1, size)]


def halves(x):
    return [x[: x.shape[0] // 2], x[x.shape[0] // 2 :]]


def sum_parts(parts):
    total = parts[0].astype(F32)
    for part in parts[1:]:
        total = total + part.astype(F32)
    return total.astype(parts[0].dtype)


def spread(x):
    return [[one] for one in swap([x] * lax.axis_size("head"))]


def spread_halves(pair):
    size = lax.axis_size("head")
    a, b = pair

    def send(x, r):
        return lax.ppermute(x, "head", xor_pairs(size, r))

    if size != 4:
        return [[a, b]] + [[send(a, r), send(b, r)] for r in range(1, size)]
    ax, by = send(a, 1), send(b, 2)
    ay, bx = send(a, 2), send(b, 1)
    return [[a, b], [ax, bx], [ay, by], [send(ax, 2), send(by, 1)]]


def shifted(x, step):
    size = lax.axis_size("seq")
    return lax.ppermute(x, "seq", [(i, i + step) for i in range(size) if 0 <= i + step < size])


def over_z(x):
    count, size = x.shape[0], lax.axis_size("seq")
    if count <= 4:
        parts = [lax.ppermute(x[k], "seq", xor_pairs(size, 2 * k)) for k in range(1, count)]
        total = x[0].astype(F32)
        for part in parts:
            total = total + part.astype(F32)
        return total
    while count > 1:
        count //= 2
        got = lax.ppermute(x[count:], "seq", xor_pairs(size, 2 * count))
        x = (x[:count].astype(F32) + got.astype(F32)).astype(x.dtype)
    return x[0].astype(F32)


def carried(x, labels, step, join, before):
    size, me = lax.axis_size("seq"), lax.axis_index("seq")
    reach = max(size // 4, 1)
    k = 1
    while 2 * k < reach:
        other = jnp.take(labels, jnp.clip(me - step * k, 0, size - 1))
        flag = (other == jnp.take(labels, me)).astype(F32)
        x = join(x, shifted(x, step * k), flag)
        k *= 2
    one = shifted(x, step)
    one, before = lax.optimization_barrier((one, before))
    return one, shifted(one, step * k)


def on_device(
    tokens, doc_ids, query_weight, key_weight, value_weight, out_weight,
    gate_weight, up_weight, down_weight, mix_gain, mlp_gain, cotangent,
):
    n, blocks = lax.axis_size("head"), lax.axis_size("seq")
    here, me = lax.axis_index("head"), lax.axis_index("seq")
    rows, d = tokens.shape[1:]
    wb = d // blocks
    nb = blocks if wb % 128 == 0 else 1
    heads = query_weight.shape[1] // FDIM
    nqkv = 2 * heads * FDIM + heads * VDIM
    nv = heads * VDIM
    ff = gate_weight.shape[1]
    x, cot = tokens[0], cotangent[0]

    piece = mix_gain.shape[0]
    doc_rows = rows // wb
    extra = -(-(2 + doc_rows) // 16) * 16
    pack = call(
        pack_body,
        sds((nqkv + extra, wb), BF16),
        (
            query_weight.T, key_weight.T, value_weight, mix_gain.reshape(1, -1), mlp_gain.reshape(1, -1),
            doc_ids.reshape(doc_rows, wb),
        ),
        us=2,
        most=True,
    )
    out_slices = swap([out_weight] * n)
    pack = lax.all_gather(pack, "seq")
    down_late, pack = lax.optimization_barrier((down_weight, pack))
    second = lax.all_gather(jnp.concatenate([*out_slices, down_late], axis=0), "seq")

    def gathered(w):
        return w if nb == blocks else jnp.transpose(w, (1, 0, 2)).reshape(1, w.shape[1], d)

    def unblocked(w):
        if nb == blocks:
            return w
        w = w.reshape(w.shape[1:-1] + (blocks, wb))
        return jnp.moveaxis(w, -2, 0)

    core = (me % 2).reshape(1)
    where = jnp.concatenate([here ^ jnp.arange(n, dtype=jnp.int32), core, (me // 2).reshape(1)])
    half = blocks // 2
    mine = lax.dynamic_slice_in_dim(pack, core[0] * half, half)
    other = lax.dynamic_slice_in_dim(pack, (1 - core[0]) * half, half)
    mine = swap([mine] * n)
    pairs = [[mine[0], other]]
    pairs += [[one, lax.ppermute(one, "seq", xor_pairs(blocks, 1))] for one in mine[1:]]
    if nb == blocks:
        gain_in = jnp.zeros((8, 128), F32)
    else:
        small = jnp.stack([jnp.stack([one[:, nqkv : nqkv + 2, :piece] for one in pair]) for pair in pairs])
        small = jnp.take(jnp.take(small, here ^ jnp.arange(n), axis=0), core[0] ^ jnp.arange(2), axis=1)
        gain_in = jnp.transpose(small.reshape(n, blocks, 2, piece), (2, 0, 1, 3)).reshape(2, d)
        gain_in = jnp.pad(gain_in.astype(F32), ((0, 6), (0, 0)))
    docs = pack[:, nqkv + 2 : nqkv + 2 + doc_rows].reshape(blocks, rows).astype(F32)
    segs = jnp.take(docs, me, axis=0)
    lasts = docs[:, -1]
    if nb != blocks:
        pairs = [
            [gathered(jnp.where(core[0] == 0, jnp.concatenate(p), jnp.concatenate(p[::-1])))] for p in pairs
        ]
    cot_late, pairs[1:] = lax.optimization_barrier((cot, pairs[1:]))
    wide = call(pack_two_body, sds((2 * ff, wb), BF16), (gate_weight.T, up_weight.T), us=2)

    before = jnp.where(me > 0, jnp.take(lasts, jnp.maximum(me - 1, 0)), -1.0)
    final_label = jnp.take(lasts, me)
    labels_back = jnp.concatenate([jnp.full((1,), -1.0), lasts[:-1]])

    def join(a, b, flag):
        return (a.astype(F32) + b.astype(F32) * flag).astype(BF16)

    def flag_of(labels, step):
        reach = max(blocks // 4, 1)
        k = 1
        while 2 * k < reach:
            k *= 2
        near = jnp.take(labels, jnp.clip(me - step, 0, blocks - 1))
        far = jnp.take(labels, jnp.clip(me - step * (1 + k), 0, blocks - 1))
        return (near == far).astype(F32)

    masks = jnp.stack(
        [
            segs,
            (segs == final_label).astype(F32),
            (segs == before).astype(F32),
            jnp.full((rows,), 1.0) * flag_of(lasts, 1),
            jnp.full((rows,), 1.0) * flag_of(labels_back, -1),
        ]
        + [jnp.zeros_like(segs)] * 3
    )

    h1, qk, v, sums, w_qkv, gains = project(
        where, x, gain_in, masks, pairs, heads, piece if nb == blocks else 0
    )
    cots = swap([cot_late] * n)
    nd = local(qk, v, masks)
    one, two = carried(sums, lasts, 1, join, nd)
    w_out, w_down = spread_out(gathered(second), ff)
    wide, one, w_out = lax.optimization_barrier((wide, one, w_out))
    w_mlp = widen(gathered(lax.all_gather(wide, "seq")))
    dhid = prepare(w_down, cots)
    o, on, inv, c = carry(nd, qk, masks, one, two)
    y1, h2 = middle(x, o, w_out, gains)
    h2s = spread_halves(h2)
    res = [None] * n
    held = h2s[n - 1]
    for r in range(n - 1, -1, -1):
        res[r] = mlp(r, held, dhid, w_mlp)
        if r:
            held, res[r] = lax.optimization_barrier((list(h2s[r - 1]), list(res[r])))
    dparts, hid, dg, du = ([t[k] for t in res] for k in range(4))
    dparts = swap(dparts)
    oparts = mlp_out(hid, w_down)
    dmlp = mlp_grads(h2s, cots, hid, dg, du, nb)
    dparts, oparts, dmlp = lax.optimization_barrier((dparts, oparts, dmlp))
    dy1, dgain_mlp, f, do = turn(dparts, y1, cot, gains, w_out)
    dext, dsums = back_first(do, on, inv, qk, masks)
    dq, dk, dv = back_local(dext, qk, v, masks, c)
    back_one, back_two = carried(dsums, labels_back, -1, join, (dq, dk, dv))

    def split(w):
        if nb == blocks:
            return w
        w = unblocked(w[0][:, 0][None])
        w = jnp.moveaxis(w.reshape((half, 2) + w.shape[1:]), 2, 0)
        w = jnp.take(w, (me // 2) ^ jnp.arange(half), axis=1)
        return [lax.dynamic_index_in_dim(w, bit, 2, keepdims=False) for bit in (core[0], 1 - core[0])]

    def pooled(keep, give):
        got = lax.ppermute(give, "seq", xor_pairs(blocks, 1))
        return [(keep[r].astype(F32) + got[r].astype(F32)).astype(BF16) for r in range(n)]

    dout = sum_parts(swap(pooled(*split(out_grads(where, o, f, nb)))))
    dmlp, back_two, dout = lax.optimization_barrier((dmlp, back_two, dout))
    dmlp = lax.psum_scatter(unblocked(dmlp), "seq", tiled=True)[0].astype(F32)
    grad_tokens, *dqkv, dgains = back_last(
        where, dq, dk, dv, qk, v, masks, back_one, back_two, h1, w_qkv, gains, x, dy1, dgain_mlp, nb
    )
    near = [lax.ppermute(oparts[r], "head", xor_pairs(n, r)) for r in range(1, n - 1)]
    near, dqkv = lax.optimization_barrier((near, dqkv))
    dqkv = pooled(*split(dqkv))
    far = lax.ppermute(oparts[n - 1], "head", xor_pairs(n, n - 1))
    if FAR:
        far, dqkv = lax.optimization_barrier((far, dqkv))
    dqkv = over_z(sum_parts(swap(dqkv)))
    oparts = [oparts[0], *near, far]
    dout = over_z(dout)
    if nb == blocks:
        parts = dqkv[nqkv : nqkv + 2] + dqkv[nqkv + 2 : nqkv + 4]
        total = lax.dynamic_slice_in_dim(parts, me % (wb // piece) * piece, piece, axis=1)
    else:
        total = lax.psum_scatter(dgains, ("head", "seq"), scatter_dimension=1, tiled=True)
    output = y1
    for part in oparts:
        output = output + part.astype(F32)

    kq = heads * FDIM
    return (
        output.astype(BF16)[None],
        grad_tokens[None],
        dqkv[:kq].T,
        dqkv[kq : 2 * kq].T,
        dqkv[2 * kq : nqkv].T,
        dout,
        dmlp[:ff].T,
        dmlp[ff : 2 * ff].T,
        dmlp[2 * ff :],
        total[0],
        total[1],
    )


def solution(mesh):
    placed = (
        P("head", "seq", None),
        P("head", "seq"),
        P("seq", "head"),
        P("seq", "head"),
        P("seq", "head"),
        P("head", "seq"),
        P("seq", "head"),
        P("seq", "head"),
        P("head", "seq"),
        P(("head", "seq")),
        P(("head", "seq")),
        P("head", "seq", None),
    )
    return jax.shard_map(
        on_device,
        mesh=mesh,
        in_specs=placed,
        out_specs=(
            P("head", "seq", None),
            P("head", "seq", None),
            P("seq", "head"),
            P("seq", "head"),
            P("seq", "head"),
            P("head", "seq"),
            P("seq", "head"),
            P("seq", "head"),
            P("head", "seq"),
            P(("head", "seq")),
            P(("head", "seq")),
        ),
        check_vma=False,
    )
```

```python
import functools

import jax
import jax.numpy as jnp
from jax import lax
from jax.experimental import pallas as pl
from jax.experimental.pallas import tpu as pltpu
from jax.sharding import PartitionSpec as P

FDIM = 16
VDIM = 64
EPS = 1e-06
ROOT_HALF = 0.7071067811865476
FROWS = 11 * FDIM
F32 = jnp.float32
BF16 = jnp.bfloat16
VMEM_BYTES = 24 * 1024 * 1024
VMEM_MOST = 56 * 1024 * 1024
K1MOST = True
FAR = False

NN = (((1,), (0,)), ((), ()))
NT = (((1,), (1,)), ((), ()))
TN = (((0,), (0,)), ((), ()))


def mm(a, b, dims=NN):
    return lax.dot_general(a, b, dims, preferred_element_type=F32)


def call(body, outs, ins, grid=None, in_specs=None, out_specs=None, scratch=(), smem=0, us=5, most=False):
    kwargs = {}
    if smem:
        spaces = [pltpu.SMEM] * smem + [pltpu.VMEM] * (len(ins) - smem)
        kwargs = dict(in_specs=[pl.BlockSpec(memory_space=space) for space in spaces])
    if grid is not None:
        kwargs = dict(grid=grid, in_specs=in_specs, out_specs=out_specs)
    return pl.pallas_call(
        body,
        out_shape=outs,
        scratch_shapes=list(scratch),
        compiler_params=pltpu.CompilerParams(vmem_limit_bytes=VMEM_MOST if most else VMEM_BYTES),
        cost_estimate=pl.CostEstimate(flops=0, bytes_accessed=us * 600000, transcendentals=0),
        **kwargs,
    )(*ins)


def sds(shape, dtype):
    return jax.ShapeDtypeStruct(shape, dtype)


def whole(shape):
    return pl.BlockSpec(shape, lambda r: (0,) * len(shape))


def by_row(shape):
    return pl.BlockSpec((1,) + tuple(shape), lambda r: (r,) + (0,) * len(shape))


def coef(d):
    return ROOT_HALF if d in (0, FDIM // 2) else 1.0


def features(w):
    half = w * 0.5
    rows = [half]
    for d in range(FDIM // 2 + 1):
        other = half if d == 0 else pltpu.roll(half, FDIM - d, 0)
        rows.append(half * other * coef(d))
    first = lax.broadcasted_iota(jnp.int32, half.shape, 0) == 0
    rows.append(jnp.where(first, 1.0, 0.0))
    return jnp.concatenate(rows, axis=0)


def features_back(w, grad):
    half = w * 0.5
    total = grad[:FDIM]
    for d in range(FDIM // 2 + 1):
        part = grad[FDIM * (d + 1) : FDIM * (d + 2)]
        if d == 0:
            total = total + part * half * (2.0 * coef(0))
        else:
            near = part * pltpu.roll(half, FDIM - d, 0)
            far = pltpu.roll(part * half, d, 0)
            total = total + (near + far) * coef(d)
    return total * 0.5


def lanes(shape):
    return lax.broadcasted_iota(jnp.int32, shape, len(shape) - 1)


def one_hot_lanes(rows, index):
    lane = lanes((rows, 128))
    hot = jnp.logical_or(lane == index, lane == index + FDIM)
    return jnp.where(hot, 1.0, 0.0).astype(BF16)


def own_half(x, j, other=None):
    left = lanes(x.shape) < VDIM
    keep = left if j == 0 else jnp.logical_not(left)
    return jnp.where(keep, x, jnp.zeros_like(x) if other is None else other)


def pick_columns(z, column, spots):
    row = lax.broadcasted_iota(jnp.int32, (128, 128), 0)
    hot = jnp.where(column(row), 1.0, 0.0) * jnp.where(spots(lanes((128, 128))), 1.0, 0.0)
    return mm(z, hot.astype(BF16))


def doc_mask(masks, rows):
    seg = masks[0:1, :]
    col = jnp.transpose(masks)[:, 0:1]
    causal = lax.broadcasted_iota(jnp.int32, (rows, rows), 0) >= lax.broadcasted_iota(
        jnp.int32, (rows, rows), 1
    )
    return jnp.logical_and(causal, col == seg)


def with_pair(z, j):
    lane = lanes(z.shape)
    base = VDIM if j == 0 else 0
    high = z.astype(BF16)
    low = (z - high.astype(F32)).astype(BF16)
    zero = jnp.zeros_like(high)
    return jnp.where(lane == base, high, jnp.where(lane == base + FDIM, low, zero))


def moved_pair(z, spot, j):
    base = VDIM if j == 0 else 0
    z = pltpu.roll(z, lax.rem(base - spot + 128, 128), 1)
    lane = lanes(z.shape)
    keep = jnp.logical_or(lane == base, lane == base + FDIM)
    return jnp.where(keep, z, 0.0).astype(BF16)


def with_ones(x, j):
    lane = lanes(x.shape)
    base = VDIM if j == 0 else 0
    hot = jnp.where(jnp.logical_or(lane == base, lane == base + FDIM), 1.0, 0.0).astype(x.dtype)
    return own_half(x, j, hot)


def join_rows(refs):
    return refs[0][...] if len(refs) == 1 else jnp.concatenate([one[...] for one in refs], axis=0)


def grouped(refs, n):
    k = len(refs) // n
    return [refs[i * k : (i + 1) * k] for i in range(n)]


def flat(lists):
    return [x for one in lists for x in one]


def take_row(r, groups, ref):
    for index, one in enumerate(groups):
        @pl.when(r == index)
        def _():
            ref[...] = join_rows(one)


def give_row(r, refs, value):
    for index, one in enumerate(refs):
        @pl.when(r == index)
        def _():
            one[...] = value


def pack_body(q_ref, k_ref, v_ref, mix_ref, mlp_ref, docs_ref, pack_ref):
    at = 0
    for one in (q_ref, k_ref):
        pack_ref[at : at + one.shape[0], :] = one[...]
        at += one.shape[0]
    pack_ref[at : at + v_ref.shape[1], :] = v_ref[...].T
    at += v_ref.shape[1]
    wb = pack_ref.shape[1]
    extra = pack_ref.shape[0] - at
    rows = []
    for one in (mix_ref, mlp_ref):
        fill = jnp.zeros((1, wb - one.shape[1]), F32)
        rows.append(jnp.concatenate([one[...].astype(F32), fill], axis=1))
    rows.append(docs_ref[...].astype(F32))
    rows.append(jnp.zeros((extra - 2 - docs_ref.shape[0], wb), F32))
    pack_ref[at:, :] = jnp.concatenate(rows, axis=0).astype(BF16)


def pack_two_body(gate_ref, up_ref, pack_ref):
    ff = gate_ref.shape[0]
    pack_ref[:ff, :] = gate_ref[...]
    pack_ref[ff:, :] = up_ref[...]


def project_body(n, piece, where_ref, x_ref, gain_ref, masks_ref, *refs):
    blocks = grouped(refs[:-7], n)
    h1_ref, qk_ref, v_ref, p_ref, wt_ref, gains_ref, z_ref = refs[-7:]
    r = pl.program_id(0)
    heads = qk_ref.shape[1] // (2 * FDIM)
    total = wt_ref.shape[1]
    core = where_ref[n]

    @pl.when(r == 0)
    def _():
        if piece:
            for q, halves in enumerate(blocks):
                for other, half in enumerate(halves):
                    count, _, wb = half.shape
                    tile = jnp.zeros((16, wb), F32)
                    for j in range(count):
                        one = half[j, total : total + 16, :].astype(F32)
                        one = jnp.where(lanes(one.shape) < piece, one, 0.0)
                        tile = tile + (one if j == 0 else pltpu.roll(one, j * piece, 1))
                    side = core if other == 0 else 1 - core
                    at = pl.multiple_of((where_ref[q] * 2 + side) * wb, wb)
                    gains_ref[:, pl.ds(at, wb)] = tile[:8]
        else:
            gains_ref[...] = gain_ref[...]
        x = x_ref[...].astype(F32)
        normed = x * lax.rsqrt(jnp.mean(x * x, axis=-1, keepdims=True) + EPS)
        h1_ref[...] = (normed * gains_ref[0:1, :]).astype(BF16)
        z_ref[...] = jnp.zeros_like(z_ref)

    for index, halves in enumerate(blocks):

        @pl.when(r == index)
        def _():
            for other, half in enumerate(halves):
                count, _, wb = half.shape
                side = core if other == 0 else 1 - core
                for j in range(count):
                    at = j * wb if count * wb == wt_ref.shape[2] else (side * count + j) * wb
                    if not isinstance(at, int):
                        at = pl.multiple_of(at, wb)
                    wt_ref[0, :, pl.ds(at, wb)] = half[j, :total, :]

    h1 = h1_ref[...]
    nqk = qk_ref.shape[1]
    qk = mm(wt_ref[0, :nqk, :], h1, NT).astype(BF16)
    qk_ref[0] = qk
    v = mm(h1, wt_ref[0, nqk:, :], NT).astype(BF16)
    v_ref[0] = v
    tail = masks_ref[1:2, :]
    rows = v.shape[0]
    for pair in range(heads // 2):
        v_pair = v[:, pair * 128 : (pair + 1) * 128]
        both = []
        for j in range(2):
            i = 2 * pair + j
            k = qk[nqk // 2 + i * FDIM : nqk // 2 + (i + 1) * FDIM].astype(F32)
            phi = (features(k) * tail).astype(BF16)
            rhs = jnp.concatenate([v_pair, one_hot_lanes(rows, r * heads + i)], axis=1)
            res = mm(phi, rhs)
            both.append(res[:, :128])
            z_ref[...] += res[:, 128:]
        p_ref[r * (heads // 2) + pair] = own_half(both[0], 0, both[1]).astype(BF16)

    @pl.when(r == pl.num_programs(0) - 1)
    def _():
        p_ref[p_ref.shape[0] - 1] = z_ref[...].astype(BF16)


def project(where, x, gain, masks, blocks, heads, piece):
    n = len(blocks)
    rows, d = x.shape
    nqk, nv = 2 * heads * FDIM, heads * VDIM
    sums = n * heads // 2 + 1
    ins = (where, x, gain, masks, *flat(blocks))
    return call(
        functools.partial(project_body, n, piece),
        (
            sds((rows, d), BF16),
            sds((n, nqk, rows), BF16),
            sds((n, rows, nv), BF16),
            sds((sums, FROWS, 128), BF16),
            sds((n, nqk + nv, d), BF16),
            sds((8, d), F32),
        ),
        ins,
        grid=(n,),
        in_specs=[pl.BlockSpec(memory_space=pltpu.SMEM)] + [whole(x.shape) for x in ins[1:]],
        out_specs=[
            whole((rows, d)),
            by_row((nqk, rows)),
            by_row((rows, nv)),
            whole((sums, FROWS, 128)),
            by_row((nqk + nv, d)),
            whole((8, d)),
        ],
        scratch=[pltpu.VMEM((FROWS, 128), F32)],
        us=7,
        most=K1MOST,
    )


def local_body(qk_ref, v_ref, masks_ref, nd_ref):
    nqk = qk_ref.shape[1]
    heads = nqk // (2 * FDIM)
    rows = v_ref.shape[1]
    mask = doc_mask(masks_ref[...], rows)
    for pair in range(heads // 2):
        v_pair = v_ref[0, :, pair * 128 : (pair + 1) * 128]
        acc = None
        for j in range(2):
            i = 2 * pair + j
            q = qk_ref[0, i * FDIM : (i + 1) * FDIM, :]
            k = qk_ref[0, nqk // 2 + i * FDIM : nqk // 2 + (i + 1) * FDIM, :]
            s1 = mm(q, k, TN) * 0.25 + 1.0
            a = jnp.where(mask, 0.5 * s1 * s1 + 0.5, 0.0).astype(BF16)
            ones = own_half(jnp.ones((rows, 128), BF16), j)
            part = mm(a, jnp.concatenate([own_half(v_pair, j), ones], axis=1))
            acc = part if acc is None else acc + part
        nd_ref[0, pair] = acc


def local(qk, v, masks):
    n, nqk, rows = qk.shape
    heads = nqk // (2 * FDIM)
    return call(
        local_body,
        sds((n, heads // 2, rows, 256), F32),
        (qk, v, masks),
        grid=(n,),
        in_specs=[by_row(qk.shape[1:]), by_row(v.shape[1:]), whole(masks.shape)],
        out_specs=by_row((heads // 2, rows, 256)),
    )


def joined(first, second, flag):
    return first.astype(F32) + second.astype(F32) * flag


def carry_body(nd_ref, qk_ref, masks_ref, one_ref, two_ref, o_ref, on_ref, inv_ref, c_ref):
    r = pl.program_id(0)
    n = pl.num_programs(0)
    nqk = qk_ref.shape[1]
    heads = nqk // (2 * FDIM)
    last = one_ref.shape[0] - 1

    @pl.when(r == 0)
    def _():
        c_ref[last] = joined(one_ref[last], two_ref[last], masks_ref[3:4, 0:128]).astype(BF16)

    flag = masks_ref[3:4, 0:128]
    live = masks_ref[2:3, :]
    for pair in range(heads // 2):
        at = r * (heads // 2) + pair
        c = joined(one_ref[at], two_ref[at], flag).astype(BF16)
        c_ref[at] = c
        acc = nd_ref[0, pair]
        for j in range(2):
            i = 2 * pair + j
            q = qk_ref[0, i * FDIM : (i + 1) * FDIM, :].astype(F32)
            phi = (features(q) * live).astype(BF16)
            z = pick_columns(
                c_ref[last],
                lambda row: row == r * heads + i,
                lambda lane: (lane < VDIM) if j == 0 else (lane >= VDIM),
            ).astype(BF16)
            acc = acc + mm(phi, jnp.concatenate([own_half(c, j), z], axis=1), TN)
        inv = 1.0 / acc[:, 128:]
        on = acc[:, :128] * inv
        cols = slice(pair * 128, (pair + 1) * 128)
        o_ref[0, :, cols] = on.astype(BF16)
        on_ref[0, :, cols] = on
        inv_ref[0, :, cols] = inv


def carry(nd, qk, masks, one, two):
    n, nqk, rows = qk.shape
    heads = nqk // (2 * FDIM)
    nv = heads * VDIM
    return call(
        carry_body,
        (
            sds((n, rows, nv), BF16),
            sds((n, rows, nv), F32),
            sds((n, rows, nv), F32),
            sds(one.shape, BF16),
        ),
        (nd, qk, masks, one, two),
        grid=(n,),
        in_specs=[
            by_row(nd.shape[1:]),
            by_row(qk.shape[1:]),
            whole(masks.shape),
            whole(one.shape),
            whole(two.shape),
        ],
        out_specs=[by_row((rows, nv))] * 3 + [whole(one.shape)],
        most=True,
    )


def middle_body(x_ref, gain_ref, o_ref, w_ref, y1_ref, *h2_refs):
    n, _, width = o_ref.shape
    acc = x_ref[...].astype(F32)
    for r in range(n):
        acc = acc + mm(o_ref[r], w_ref[r * width : (r + 1) * width, :])
    y1_ref[...] = acc
    scale = lax.rsqrt(jnp.mean(acc * acc, axis=-1, keepdims=True) + EPS)
    give_rows(h2_refs, (acc * scale * gain_ref[1:2, :]).astype(BF16))


def give_rows(refs, value):
    at = 0
    for one in refs:
        one[...] = value[at : at + one.shape[0]]
        at += one.shape[0]


def middle(x, o, wo, gain):
    rows, d = x.shape
    res = call(
        middle_body,
        (sds((rows, d), F32), *[sds((rows // 2, d), BF16)] * 2),
        (x, gain, o, wo),
        us=4,
    )
    return res[0], res[1:]


def spread_out_body(w_ref, out_ref, down_ref):
    nb, _, wb = w_ref.shape
    split = out_ref.shape[0]
    for s in range(nb):
        out_ref[:, s * wb : (s + 1) * wb] = w_ref[s, :split, :]
        down_ref[:, s * wb : (s + 1) * wb] = w_ref[s, split:, :]


def spread_out(w, ff):
    nb, total, wb = w.shape
    d = nb * wb
    return call(spread_out_body, (sds((total - ff, d), BF16), sds((ff, d), BF16)), (w,), us=4)


def prepare_body(n, down_ref, *refs):
    cots, out_ref = refs[:n], refs[n]
    for r in range(n):
        out_ref[r] = mm(cots[r][...], down_ref[...], NT).astype(BF16)


def prepare(down, cots):
    n = len(cots)
    return call(
        functools.partial(prepare_body, n),
        sds((n, cots[0].shape[0], down.shape[0]), BF16),
        (down, *cots),
    )


def widen_body(w_ref, wide_ref):
    nb, _, wb = w_ref.shape
    for s in range(nb):
        wide_ref[:, s * wb : (s + 1) * wb] = w_ref[s]


def widen(w):
    nb, total, wb = w.shape
    return call(widen_body, sds((total, nb * wb), BF16), (w,))


def mlp_body(first_ref, second_ref, dhid_ref, w_ref, dh_ref, hid_ref, dg_ref, du_ref):
    ff = hid_ref.shape[1]
    h2 = join_rows((first_ref, second_ref))
    gate_w, up_w = w_ref[0:ff, :], w_ref[ff : 2 * ff, :]
    dhid = dhid_ref[0].astype(F32)
    g = mm(h2, gate_w, NT)
    u = mm(h2, up_w, NT)
    sig = jax.nn.sigmoid(g)
    act = g * sig
    hid_ref[...] = (act * u).astype(BF16)
    dg = (dhid * u * sig * (1.0 + g * (1.0 - sig))).astype(BF16)
    du = (dhid * act).astype(BF16)
    dg_ref[...] = dg
    du_ref[...] = du
    dh_ref[...] = (mm(dg, gate_w) + mm(du, up_w)).astype(BF16)


def mlp(index, h2, dhid, w):
    half, d = h2[0].shape
    rows = 2 * half
    ff = w.shape[0] // 2
    return call(
        mlp_body,
        (sds((rows, d), BF16), *[sds((rows, ff), BF16)] * 3),
        (*h2, dhid, w),
        grid=(1,),
        in_specs=[whole((half, d))] * 2
        + [pl.BlockSpec((1, rows, ff), lambda r: (index, 0, 0)), whole((2 * ff, d))],
        out_specs=[whole((rows, d))] + [whole((rows, ff))] * 3,
    )


def mlp_out_body(n, w_ref, *refs):
    for r in range(n):
        refs[n + r][...] = mm(refs[r][...], w_ref[...]).astype(BF16)


def mlp_out(hid, w):
    n = len(hid)
    return call(
        functools.partial(mlp_out_body, n),
        [sds((hid[0].shape[0], w.shape[1]), BF16)] * n,
        (w, *hid),
    )


def mlp_grads_body(n, *refs):
    h2, cot = grouped(refs[: 2 * n], n), grouped(refs[2 * n : 3 * n], n)
    hid, dg, du = (refs[(3 + k) * n : (4 + k) * n] for k in range(3))
    o_ref, ff = refs[6 * n], hid[0].shape[1]
    nb, _, wb = o_ref.shape
    for k, (left, right) in enumerate(((dg, h2), (du, h2), (hid, cot))):
        acc = None
        for r in range(n):
            part = mm(left[r][...], join_rows(right[r]), TN)
            acc = part if acc is None else acc + part
        acc = acc.astype(BF16)
        for s in range(nb):
            o_ref[s, k * ff : (k + 1) * ff, :] = acc[:, s * wb : (s + 1) * wb]


def mlp_grads(h2, cot, hid, dg, du, nb):
    n = len(h2)
    d, ff = h2[0][0].shape[1], hid[0].shape[1]
    ins = (*flat(h2), *cot, *hid, *dg, *du)
    return call(
        functools.partial(mlp_grads_body, n),
        sds((nb, 3 * ff, d // nb), BF16),
        ins,
        grid=(1,),
        in_specs=[whole(x.shape) for x in ins],
        out_specs=whole((nb, 3 * ff, d // nb)),
        us=9,
    )


def turn_body(n, y1_ref, cot_ref, gain_ref, *refs):
    parts, w_ref = refs[:n], refs[n]
    dy1_ref, dgain_ref, *f_refs = refs[n + 1 : n + 4]
    do_ref = refs[n + 4]
    rows_of = do_ref.shape[2]
    dh2 = parts[0][...].astype(F32)
    for r in range(1, n):
        dh2 = dh2 + parts[r][...].astype(F32)
    y1 = y1_ref[...]
    scale = lax.rsqrt(jnp.mean(y1 * y1, axis=-1, keepdims=True) + EPS)
    normed = y1 * scale
    dgain_ref[...] = jnp.sum(dh2 * normed, axis=0, keepdims=True)
    dn = dh2 * gain_ref[1:2, :]
    inner = jnp.mean(dn * normed, axis=-1, keepdims=True)
    dy1 = cot_ref[...].astype(F32) + scale * (dn - normed * inner)
    dy1_ref[...] = dy1
    f = dy1.astype(BF16)
    give_rows(f_refs, f)
    for r in range(n):
        do_ref[r] = mm(f, w_ref[r * rows_of : (r + 1) * rows_of, :], NT).astype(BF16)


def turn(parts, y1, cot, gain, wo):
    n = len(parts)
    rows, d = y1.shape
    nv = wo.shape[0] // n
    res = call(
        functools.partial(turn_body, n),
        (
            sds((rows, d), F32),
            sds((1, d), F32),
            sds((rows, d), BF16),
            sds((n, rows, nv), BF16),
        ),
        (y1, cot, gain, *parts, wo),
    )
    return res


def back_first_body(do_ref, on_ref, inv_ref, qk_ref, masks_ref, d_ref, p_ref, z_ref):
    r = pl.program_id(0)
    n = pl.num_programs(0)
    nqk = qk_ref.shape[1]
    heads = nqk // (2 * FDIM)
    rows = do_ref.shape[1]

    @pl.when(r == 0)
    def _():
        z_ref[...] = jnp.zeros_like(z_ref)

    live = masks_ref[2:3, :]
    lane = lanes((rows, 128))
    for pair in range(heads // 2):
        cols = slice(pair * 128, (pair + 1) * 128)
        wide = do_ref[0, :, cols].astype(F32) * inv_ref[0, :, cols]
        dnum = wide.astype(BF16)
        prod = -(wide * on_ref[0, :, cols])
        high = prod.astype(BF16)
        low = (prod - high.astype(F32)).astype(BF16)
        both = []
        for j in range(2):
            i = 2 * pair + j
            row = lax.broadcasted_iota(jnp.int32, (128, 128), 0)
            hot = jnp.where((row < VDIM) if j == 0 else (row >= VDIM), 1.0, 0.0).astype(BF16)
            dden = mm(high, hot) + mm(low, hot)
            d_ref[0, i] = own_half(dnum, j, with_pair(dden, j))
            dh = dden.astype(BF16)
            dl = (dden - dh.astype(F32)).astype(BF16)
            zero = jnp.zeros_like(dh)
            spot = r * heads + i
            zext = jnp.where(lane == spot, dh, jnp.where(lane == spot + n * heads, dl, zero))
            q = qk_ref[0, i * FDIM : (i + 1) * FDIM, :].astype(F32)
            phi = (features(q) * live).astype(BF16)
            res = mm(phi, jnp.concatenate([dnum, zext], axis=1))
            both.append(res[:, :128])
            z_ref[...] += res[:, 128:]
        p_ref[r * (heads // 2) + pair] = own_half(both[0], 0, both[1]).astype(BF16)

    @pl.when(r == n - 1)
    def _():
        p_ref[p_ref.shape[0] - 1] = z_ref[...].astype(BF16)


def back_first(do, on, inv, qk, masks):
    n, nqk, rows = qk.shape
    heads = nqk // (2 * FDIM)
    pieces = n * heads // 2 + 1
    return call(
        back_first_body,
        (sds((n, heads, rows, 128), BF16), sds((pieces, FROWS, 128), BF16)),
        (do, on, inv, qk, masks),
        grid=(n,),
        in_specs=[by_row(x.shape[1:]) for x in (do, on, inv, qk)] + [whole(masks.shape)],
        out_specs=[by_row((heads, rows, 128)), whole((pieces, FROWS, 128))],
        scratch=[pltpu.VMEM((FROWS, 128), F32)],
    )


def back_local_body(d_ref, qk_ref, v_ref, masks_ref, c_ref, dq_ref, dk_ref, dv_ref):
    r = pl.program_id(0)
    nqk = qk_ref.shape[1]
    heads = nqk // (2 * FDIM)
    rows = v_ref.shape[1]
    masks = masks_ref[...]
    mask = doc_mask(masks, rows)
    live = masks[2:3, :]
    last = c_ref.shape[0] - 1
    for pair in range(heads // 2):
        cols = slice(pair * 128, (pair + 1) * 128)
        v_pair = v_ref[0, :, cols]
        c = c_ref[r * (heads // 2) + pair]
        dv = None
        for j in range(2):
            i = 2 * pair + j
            q = qk_ref[0, i * FDIM : (i + 1) * FDIM, :]
            k = qk_ref[0, nqk // 2 + i * FDIM : nqk // 2 + (i + 1) * FDIM, :]
            s1 = mm(q, k, TN) * 0.25 + 1.0
            a = jnp.where(mask, 0.5 * s1 * s1 + 0.5, 0.0).astype(BF16)
            d = d_ref[0, i]
            da = mm(d, with_ones(v_pair, j), NT)
            ds = jnp.where(mask, da * s1, 0.0).astype(BF16)
            z = moved_pair(c_ref[last].astype(F32), r * heads + i, j)
            dphi = mm(own_half(c, j, z), d, NT) * live
            back = features_back(q.astype(F32), dphi)
            dq_ref[0, i * FDIM : (i + 1) * FDIM, :] = (mm(k, ds, NT) * 0.25 + back).astype(BF16)
            dk_ref[0, i * FDIM : (i + 1) * FDIM, :] = mm(q, ds) * 0.25
            part = mm(own_half(d, j), a, TN)
            dv = part if dv is None else dv + part
        dv_ref[0, cols, :] = dv


def back_local(d, qk, v, masks, c):
    n, nqk, rows = qk.shape
    heads = nqk // (2 * FDIM)
    nv = heads * VDIM
    return call(
        back_local_body,
        (sds((n, nqk // 2, rows), BF16), sds((n, nqk // 2, rows), F32), sds((n, nv, rows), F32)),
        (d, qk, v, masks, c),
        grid=(n,),
        in_specs=[by_row(x.shape[1:]) for x in (d, qk, v)] + [whole(masks.shape), whole(c.shape)],
        out_specs=[by_row((nqk // 2, rows)), by_row((nqk // 2, rows)), by_row((nv, rows))],
    )


def back_last_body(
    where_ref, dq_ref, dk_ref, dv_ref, qk_ref, v_ref, masks_ref, one_ref, two_ref, h1_ref, wt_ref,
    gain_ref, x_ref, dy1_ref, dgain_mlp_ref, grad_ref, *refs,
):
    *dw_refs, dgain_ref, z_ref, acc_ref, wide_ref = refs
    r = pl.program_id(0)
    n = pl.num_programs(0)
    nqk = qk_ref.shape[1]
    heads = nqk // (2 * FDIM)
    nb, wb = dw_refs[0].shape[1] * len(dw_refs), dw_refs[0].shape[3]
    last = one_ref.shape[0] - 1
    flag = masks_ref[4:5, 0:128]
    tail = masks_ref[1:2, :]

    @pl.when(r == 0)
    def _():
        z_ref[...] = joined(one_ref[last], two_ref[last], flag)
        acc_ref[...] = jnp.zeros_like(acc_ref)

    dks, dvs = [], []
    for pair in range(heads // 2):
        cols = slice(pair * 128, (pair + 1) * 128)
        at = r * (heads // 2) + pair
        dp = joined(one_ref[at], two_ref[at], flag).astype(BF16)
        v_pair = v_ref[0, :, cols]
        dv = dv_ref[0, cols, :]
        for j in range(2):
            i = 2 * pair + j
            k = qk_ref[0, nqk // 2 + i * FDIM : nqk // 2 + (i + 1) * FDIM, :].astype(F32)
            z = moved_pair(z_ref[...], r * heads + i, j)
            dphi = mm(own_half(dp, j, z), with_ones(v_pair, j), NT) * tail
            dk = dk_ref[0, i * FDIM : (i + 1) * FDIM, :] + features_back(k, dphi)
            dks.append(dk.astype(BF16))
            phi = (features(k) * tail).astype(BF16)
            dv = dv + mm(own_half(dp, j), phi, TN)
        dvs.append(dv.astype(BF16))
    d = jnp.concatenate([dq_ref[0]] + dks + dvs, axis=0)
    total = d.shape[0]
    wide_ref[...] = mm(d, h1_ref[...]).astype(BF16)
    give_blocks(where_ref, wide_ref, [one.at[r, :, 0:total, :] for one in dw_refs])
    acc_ref[...] += mm(d, wt_ref[0], TN)

    @pl.when(r == n - 1)
    def _():
        dh1 = acc_ref[...]
        x = x_ref[...].astype(F32)
        scale = lax.rsqrt(jnp.mean(x * x, axis=-1, keepdims=True) + EPS)
        normed = x * scale
        dgain_ref[0:1, :] = jnp.sum(dh1 * normed, axis=0, keepdims=True)
        dgain_ref[1:2, :] = dgain_mlp_ref[...]
        dn = dh1 * gain_ref[0:1, :]
        inner = jnp.mean(dn * normed, axis=-1, keepdims=True)
        grad_ref[...] = dy1_ref[...] + scale * (dn - normed * inner)
        if nb > 1:
            groups, count = dw_refs[0].shape[:2]
            across = groups * nb * wb // dgain_ref.shape[1]
            tiles = nb // across
            for q in range(groups):
                for z in range(count):
                    at = where_ref[q] * tiles + (where_ref[groups + 1] ^ z) * 2 // across
                    both = dgain_ref[:, pl.ds(pl.multiple_of(at * wb, wb), wb)]
                    high = both.astype(BF16).astype(F32)
                    fill = jnp.zeros((dw_refs[0].shape[2] - total - 4, wb), F32)
                    block = jnp.concatenate([high, both - high, fill], axis=0).astype(BF16)
                    for one in dw_refs:
                        one[q, z, total:, :] = block


def give_blocks(where_ref, wide_ref, refs):
    count, _, wb = refs[0].shape
    last = where_ref.shape[0] - 1
    for index, one in enumerate(refs):
        for z in range(count):
            at = 0
            if len(refs) == 2:
                core = where_ref[last - 1]
                side = core if index == 0 else 1 - core
                at = pl.multiple_of(((where_ref[last] ^ z) * 2 + side) * wb, wb)
            one[z] = wide_ref[:, pl.ds(at, wb)]


def back_last(where, dq, dk, dv, qk, v, masks, one, two, h1, w, gain, x, dy1, dgain_mlp, nb):
    n, nqk, rows = qk.shape
    _, total, d = w.shape
    shapes = [(n, 1, total + 16, d)] if nb == 1 else [(n, nb // 2, total + 16, d // nb)] * 2
    ins = (where, dq, dk, dv, qk, v, masks, one, two, h1, w, gain, x, dy1, dgain_mlp)
    return call(
        back_last_body,
        (sds((rows, d), F32), *[sds(shape, BF16) for shape in shapes], sds((2, d), F32)),
        ins,
        grid=(n,),
        in_specs=[pl.BlockSpec(memory_space=pltpu.SMEM)]
        + [by_row(y.shape[1:]) for y in (dq, dk, dv, qk, v)]
        + [whole(y.shape) for y in (masks, one, two, h1)]
        + [by_row(w.shape[1:])]
        + [whole(y.shape) for y in (gain, x, dy1, dgain_mlp)],
        out_specs=[whole((rows, d)), *[whole(shape) for shape in shapes], whole((2, d))],
        scratch=[
            pltpu.VMEM((FROWS, 128), F32),
            pltpu.VMEM((rows, d), F32),
            pltpu.VMEM((total, d), BF16),
        ],
        us=10,
        most=True,
    )


def out_grads_body(n, where_ref, f_ref, *refs):
    o_ref, outs, wide_ref = refs[0], refs[1:-1], refs[-1]
    for r in range(n):
        wide_ref[...] = mm(o_ref[r], f_ref[...], TN).astype(BF16)
        give_blocks(where_ref, wide_ref, [one.at[r] for one in outs])


def out_grads(where, o, f, nb):
    n, _, nv = o.shape
    d = f.shape[1]
    shapes = [(n, 1, nv, d)] if nb == 1 else [(n, nb // 2, nv, d // nb)] * 2
    return call(
        functools.partial(out_grads_body, n),
        [sds(shape, BF16) for shape in shapes],
        (where, f, o),
        scratch=[pltpu.VMEM((nv, d), BF16)],
        smem=1,
        us=3,
    )


def xor_pairs(size, r):
    return [(i, i ^ r) for i in range(size)]


def swap(parts):
    size = lax.axis_size("head")
    return [parts[0]] + [lax.ppermute(parts[r], "head", xor_pairs(size, r)) for r in range(1, size)]


def halves(x):
    return [x[: x.shape[0] // 2], x[x.shape[0] // 2 :]]


def sum_parts(parts):
    total = parts[0].astype(F32)
    for part in parts[1:]:
        total = total + part.astype(F32)
    return total.astype(parts[0].dtype)


def spread(x):
    return [[one] for one in swap([x] * lax.axis_size("head"))]


def spread_halves(pair):
    size = lax.axis_size("head")
    a, b = pair

    def send(x, r):
        return lax.ppermute(x, "head", xor_pairs(size, r))

    if size != 4:
        return [[a, b]] + [[send(a, r), send(b, r)] for r in range(1, size)]
    ax, by = send(a, 1), send(b, 2)
    ay, bx = send(a, 2), send(b, 1)
    return [[a, b], [ax, bx], [ay, by], [send(ax, 2), send(by, 1)]]


def shifted(x, step):
    size = lax.axis_size("seq")
    return lax.ppermute(x, "seq", [(i, i + step) for i in range(size) if 0 <= i + step < size])


def over_z(x):
    count, size = x.shape[0], lax.axis_size("seq")
    if count <= 4:
        parts = [lax.ppermute(x[k], "seq", xor_pairs(size, 2 * k)) for k in range(1, count)]
        total = x[0].astype(F32)
        for part in parts:
            total = total + part.astype(F32)
        return total
    while count > 1:
        count //= 2
        got = lax.ppermute(x[count:], "seq", xor_pairs(size, 2 * count))
        x = (x[:count].astype(F32) + got.astype(F32)).astype(x.dtype)
    return x[0].astype(F32)


def carried(x, labels, step, join, before):
    size, me = lax.axis_size("seq"), lax.axis_index("seq")
    reach = max(size // 4, 1)
    k = 1
    while 2 * k < reach:
        other = jnp.take(labels, jnp.clip(me - step * k, 0, size - 1))
        flag = (other == jnp.take(labels, me)).astype(F32)
        x = join(x, shifted(x, step * k), flag)
        k *= 2
    one = shifted(x, step)
    one, before = lax.optimization_barrier((one, before))
    return one, shifted(one, step * k)


def on_device(
    tokens, doc_ids, query_weight, key_weight, value_weight, out_weight,
    gate_weight, up_weight, down_weight, mix_gain, mlp_gain, cotangent,
):
    n, blocks = lax.axis_size("head"), lax.axis_size("seq")
    here, me = lax.axis_index("head"), lax.axis_index("seq")
    rows, d = tokens.shape[1:]
    wb = d // blocks
    nb = blocks if wb % 128 == 0 else 1
    heads = query_weight.shape[1] // FDIM
    nqkv = 2 * heads * FDIM + heads * VDIM
    nv = heads * VDIM
    ff = gate_weight.shape[1]
    x, cot = tokens[0], cotangent[0]

    piece = mix_gain.shape[0]
    doc_rows = rows // wb
    extra = -(-(2 + doc_rows) // 16) * 16
    pack = call(
        pack_body,
        sds((nqkv + extra, wb), BF16),
        (
            query_weight.T, key_weight.T, value_weight, mix_gain.reshape(1, -1), mlp_gain.reshape(1, -1),
            doc_ids.reshape(doc_rows, wb),
        ),
        us=2,
        most=True,
    )
    out_slices = swap([out_weight] * n)
    pack = lax.all_gather(pack, "seq")
    near_cots = [lax.ppermute(cot, "head", xor_pairs(n, r)) for r in range(1, n - 1)]
    near_cots, pack = lax.optimization_barrier((near_cots, pack))
    def gathered(w):
        return w if nb == blocks else jnp.transpose(w, (1, 0, 2)).reshape(1, w.shape[1], d)

    def unblocked(w):
        if nb == blocks:
            return w
        w = w.reshape(w.shape[1:-1] + (blocks, wb))
        return jnp.moveaxis(w, -2, 0)

    core = (me % 2).reshape(1)
    where = jnp.concatenate([here ^ jnp.arange(n, dtype=jnp.int32), core, (me // 2).reshape(1)])
    half = blocks // 2
    mine = lax.dynamic_slice_in_dim(pack, core[0] * half, half)
    other = lax.dynamic_slice_in_dim(pack, (1 - core[0]) * half, half)
    down_late, mine = lax.optimization_barrier((down_weight, mine))
    second = lax.all_gather(jnp.concatenate([*out_slices, down_late], axis=0), "seq")

    docs = pack[:, nqkv + 2 : nqkv + 2 + doc_rows].reshape(blocks, rows).astype(F32)
    segs = jnp.take(docs, me, axis=0)
    lasts = docs[:, -1]
    before = jnp.where(me > 0, jnp.take(lasts, jnp.maximum(me - 1, 0)), -1.0)
    final_label = jnp.take(lasts, me)
    labels_back = jnp.concatenate([jnp.full((1,), -1.0), lasts[:-1]])

    def flag_of(labels, step):
        reach = max(blocks // 4, 1)
        k = 1
        while 2 * k < reach:
            k *= 2
        near = jnp.take(labels, jnp.clip(me - step, 0, blocks - 1))
        far = jnp.take(labels, jnp.clip(me - step * (1 + k), 0, blocks - 1))
        return (near == far).astype(F32)

    masks = jnp.stack(
        [
            segs,
            (segs == final_label).astype(F32),
            (segs == before).astype(F32),
            jnp.full((rows,), 1.0) * flag_of(lasts, 1),
            jnp.full((rows,), 1.0) * flag_of(labels_back, -1),
        ]
        + [jnp.zeros_like(segs)] * 3
    )

    mine = swap([mine] * n)
    mine[1], masks = lax.optimization_barrier((mine[1], masks))
    pairs = [[mine[0], other]]
    pairs += [[one, lax.ppermute(one, "seq", xor_pairs(blocks, 1))] for one in mine[1:]]
    if nb == blocks:
        gain_in = jnp.zeros((8, 128), F32)
    else:
        small = jnp.stack([jnp.stack([one[:, nqkv : nqkv + 2, :piece] for one in pair]) for pair in pairs])
        small = jnp.take(jnp.take(small, here ^ jnp.arange(n), axis=0), core[0] ^ jnp.arange(2), axis=1)
        gain_in = jnp.transpose(small.reshape(n, blocks, 2, piece), (2, 0, 1, 3)).reshape(2, d)
        gain_in = jnp.pad(gain_in.astype(F32), ((0, 6), (0, 0)))
    if nb != blocks:
        pairs = [
            [gathered(jnp.where(core[0] == 0, jnp.concatenate(p), jnp.concatenate(p[::-1])))] for p in pairs
        ]
    cot_late, pairs[1:] = lax.optimization_barrier((cot, pairs[1:]))
    wide = call(pack_two_body, sds((2 * ff, wb), BF16), (gate_weight.T, up_weight.T), us=2)

    def join(a, b, flag):
        return (a.astype(F32) + b.astype(F32) * flag).astype(BF16)

    h1, qk, v, sums, w_qkv, gains = project(
        where, x, gain_in, masks, pairs, heads, piece if nb == blocks else 0
    )
    cots = [cot, *near_cots, lax.ppermute(cot_late, "head", xor_pairs(n, n - 1))]
    nd = local(qk, v, masks)
    one, two = carried(sums, lasts, 1, join, nd)
    w_out, w_down = spread_out(gathered(second), ff)
    wide, one, w_out = lax.optimization_barrier((wide, one, w_out))
    w_mlp = widen(gathered(lax.all_gather(wide, "seq")))
    dhid = prepare(w_down, cots)
    o, on, inv, c = carry(nd, qk, masks, one, two)
    y1, h2 = middle(x, o, w_out, gains)
    h2s = spread_halves(h2)
    res = [None] * n
    held = h2s[n - 1]
    for r in range(n - 1, -1, -1):
        res[r] = mlp(r, held, dhid, w_mlp)
        if r:
            held, res[r] = lax.optimization_barrier((list(h2s[r - 1]), list(res[r])))
    dparts, hid, dg, du = ([t[k] for t in res] for k in range(4))
    dparts = swap(dparts)
    oparts = mlp_out(hid, w_down)
    dmlp = mlp_grads(h2s, cots, hid, dg, du, nb)
    dparts, oparts, dmlp = lax.optimization_barrier((dparts, oparts, dmlp))
    dy1, dgain_mlp, f, do = turn(dparts, y1, cot, gains, w_out)
    dext, dsums = back_first(do, on, inv, qk, masks)
    dq, dk, dv = back_local(dext, qk, v, masks, c)
    back_one, back_two = carried(dsums, labels_back, -1, join, (dq, dk, dv))

    def split(w):
        if nb == blocks:
            return w
        w = unblocked(w[0][:, 0][None])
        w = jnp.moveaxis(w.reshape((half, 2) + w.shape[1:]), 2, 0)
        w = jnp.take(w, (me // 2) ^ jnp.arange(half), axis=1)
        return [lax.dynamic_index_in_dim(w, bit, 2, keepdims=False) for bit in (core[0], 1 - core[0])]

    def pooled(keep, give):
        got = lax.ppermute(give, "seq", xor_pairs(blocks, 1))
        return [(keep[r].astype(F32) + got[r].astype(F32)).astype(BF16) for r in range(n)]

    dout = sum_parts(swap(pooled(*split(out_grads(where, o, f, nb)))))
    dmlp, back_two, dout = lax.optimization_barrier((dmlp, back_two, dout))
    dmlp = lax.psum_scatter(unblocked(dmlp), "seq", tiled=True)[0].astype(F32)
    grad_tokens, *dqkv, dgains = back_last(
        where, dq, dk, dv, qk, v, masks, back_one, back_two, h1, w_qkv, gains, x, dy1, dgain_mlp, nb
    )
    near = [lax.ppermute(oparts[r], "head", xor_pairs(n, r)) for r in range(1, n - 1)]
    near, dqkv = lax.optimization_barrier((near, dqkv))
    dqkv = pooled(*split(dqkv))
    far = lax.ppermute(oparts[n - 1], "head", xor_pairs(n, n - 1))
    if FAR:
        far, dqkv = lax.optimization_barrier((far, dqkv))
    dqkv = over_z(sum_parts(swap(dqkv)))
    oparts = [oparts[0], *near, far]
    dout = over_z(dout)
    if nb == blocks:
        parts = dqkv[nqkv : nqkv + 2] + dqkv[nqkv + 2 : nqkv + 4]
        total = lax.dynamic_slice_in_dim(parts, me % (wb // piece) * piece, piece, axis=1)
    else:
        total = lax.psum_scatter(dgains, ("head", "seq"), scatter_dimension=1, tiled=True)
    output = y1
    for part in oparts:
        output = output + part.astype(F32)

    kq = heads * FDIM
    return (
        output.astype(BF16)[None],
        grad_tokens[None],
        dqkv[:kq].T,
        dqkv[kq : 2 * kq].T,
        dqkv[2 * kq : nqkv].T,
        dout,
        dmlp[:ff].T,
        dmlp[ff : 2 * ff].T,
        dmlp[2 * ff :],
        total[0],
        total[1],
    )


def solution(mesh):
    placed = (
        P("head", "seq", None),
        P("head", "seq"),
        P("seq", "head"),
        P("seq", "head"),
        P("seq", "head"),
        P("head", "seq"),
        P("seq", "head"),
        P("seq", "head"),
        P("head", "seq"),
        P(("head", "seq")),
        P(("head", "seq")),
        P("head", "seq", None),
    )
    return jax.shard_map(
        on_device,
        mesh=mesh,
        in_specs=placed,
        out_specs=(
            P("head", "seq", None),
            P("head", "seq", None),
            P("seq", "head"),
            P("seq", "head"),
            P("seq", "head"),
            P("head", "seq"),
            P("seq", "head"),
            P("seq", "head"),
            P("head", "seq"),
            P(("head", "seq")),
            P(("head", "seq")),
        ),
        check_vma=False,
    )
```

```python
import functools

import jax
import jax.numpy as jnp
from jax import lax
from jax.experimental import pallas as pl
from jax.experimental.pallas import tpu as pltpu
from jax.sharding import PartitionSpec as P

FDIM = 16
VDIM = 64
EPS = 1e-06
ROOT_HALF = 0.7071067811865476
FROWS = 11 * FDIM
F32 = jnp.float32
BF16 = jnp.bfloat16
VMEM_BYTES = 24 * 1024 * 1024
VMEM_MOST = 56 * 1024 * 1024
K1MOST = True
FAR = False

NN = (((1,), (0,)), ((), ()))
NT = (((1,), (1,)), ((), ()))
TN = (((0,), (0,)), ((), ()))


def mm(a, b, dims=NN):
    return lax.dot_general(a, b, dims, preferred_element_type=F32)


def call(body, outs, ins, grid=None, in_specs=None, out_specs=None, scratch=(), smem=0, us=5, most=False):
    kwargs = {}
    if smem:
        spaces = [pltpu.SMEM] * smem + [pltpu.VMEM] * (len(ins) - smem)
        kwargs = dict(in_specs=[pl.BlockSpec(memory_space=space) for space in spaces])
    if grid is not None:
        kwargs = dict(grid=grid, in_specs=in_specs, out_specs=out_specs)
    return pl.pallas_call(
        body,
        out_shape=outs,
        scratch_shapes=list(scratch),
        compiler_params=pltpu.CompilerParams(vmem_limit_bytes=VMEM_MOST if most else VMEM_BYTES),
        cost_estimate=pl.CostEstimate(flops=0, bytes_accessed=us * 600000, transcendentals=0),
        **kwargs,
    )(*ins)


def sds(shape, dtype):
    return jax.ShapeDtypeStruct(shape, dtype)


def whole(shape):
    return pl.BlockSpec(shape, lambda r: (0,) * len(shape))


def by_row(shape):
    return pl.BlockSpec((1,) + tuple(shape), lambda r: (r,) + (0,) * len(shape))


def coef(d):
    return ROOT_HALF if d in (0, FDIM // 2) else 1.0


def features(w):
    half = w * 0.5
    rows = [half]
    for d in range(FDIM // 2 + 1):
        other = half if d == 0 else pltpu.roll(half, FDIM - d, 0)
        rows.append(half * other * coef(d))
    first = lax.broadcasted_iota(jnp.int32, half.shape, 0) == 0
    rows.append(jnp.where(first, 1.0, 0.0))
    return jnp.concatenate(rows, axis=0)


def features_back(w, grad):
    half = w * 0.5
    total = grad[:FDIM]
    for d in range(FDIM // 2 + 1):
        part = grad[FDIM * (d + 1) : FDIM * (d + 2)]
        if d == 0:
            total = total + part * half * (2.0 * coef(0))
        else:
            near = part * pltpu.roll(half, FDIM - d, 0)
            far = pltpu.roll(part * half, d, 0)
            total = total + (near + far) * coef(d)
    return total * 0.5


def lanes(shape):
    return lax.broadcasted_iota(jnp.int32, shape, len(shape) - 1)


def one_hot_lanes(rows, index):
    lane = lanes((rows, 128))
    hot = jnp.logical_or(lane == index, lane == index + FDIM)
    return jnp.where(hot, 1.0, 0.0).astype(BF16)


def own_half(x, j, other=None):
    left = lanes(x.shape) < VDIM
    keep = left if j == 0 else jnp.logical_not(left)
    return jnp.where(keep, x, jnp.zeros_like(x) if other is None else other)


def pick_columns(z, column, spots):
    row = lax.broadcasted_iota(jnp.int32, (128, 128), 0)
    hot = jnp.where(column(row), 1.0, 0.0) * jnp.where(spots(lanes((128, 128))), 1.0, 0.0)
    return mm(z, hot.astype(BF16))


def doc_mask(masks, rows):
    seg = masks[0:1, :]
    col = jnp.transpose(masks)[:, 0:1]
    causal = lax.broadcasted_iota(jnp.int32, (rows, rows), 0) >= lax.broadcasted_iota(
        jnp.int32, (rows, rows), 1
    )
    return jnp.logical_and(causal, col == seg)


def with_pair(z, j):
    lane = lanes(z.shape)
    base = VDIM if j == 0 else 0
    high = z.astype(BF16)
    low = (z - high.astype(F32)).astype(BF16)
    zero = jnp.zeros_like(high)
    return jnp.where(lane == base, high, jnp.where(lane == base + FDIM, low, zero))


def moved_pair(z, spot, j):
    base = VDIM if j == 0 else 0
    z = pltpu.roll(z, lax.rem(base - spot + 128, 128), 1)
    lane = lanes(z.shape)
    keep = jnp.logical_or(lane == base, lane == base + FDIM)
    return jnp.where(keep, z, 0.0).astype(BF16)


def with_ones(x, j):
    lane = lanes(x.shape)
    base = VDIM if j == 0 else 0
    hot = jnp.where(jnp.logical_or(lane == base, lane == base + FDIM), 1.0, 0.0).astype(x.dtype)
    return own_half(x, j, hot)


def join_rows(refs):
    return refs[0][...] if len(refs) == 1 else jnp.concatenate([one[...] for one in refs], axis=0)


def grouped(refs, n):
    k = len(refs) // n
    return [refs[i * k : (i + 1) * k] for i in range(n)]


def flat(lists):
    return [x for one in lists for x in one]


def take_row(r, groups, ref):
    for index, one in enumerate(groups):
        @pl.when(r == index)
        def _():
            ref[...] = join_rows(one)


def give_row(r, refs, value):
    for index, one in enumerate(refs):
        @pl.when(r == index)
        def _():
            one[...] = value


def pack_body(q_ref, k_ref, v_ref, mix_ref, mlp_ref, docs_ref, pack_ref):
    at = 0
    for one in (q_ref, k_ref):
        pack_ref[at : at + one.shape[0], :] = one[...]
        at += one.shape[0]
    pack_ref[at : at + v_ref.shape[1], :] = v_ref[...].T
    at += v_ref.shape[1]
    wb = pack_ref.shape[1]
    extra = pack_ref.shape[0] - at
    rows = []
    for one in (mix_ref, mlp_ref):
        fill = jnp.zeros((1, wb - one.shape[1]), F32)
        rows.append(jnp.concatenate([one[...].astype(F32), fill], axis=1))
    rows.append(docs_ref[...].astype(F32))
    rows.append(jnp.zeros((extra - 2 - docs_ref.shape[0], wb), F32))
    pack_ref[at:, :] = jnp.concatenate(rows, axis=0).astype(BF16)


def pack_two_body(gate_ref, up_ref, pack_ref):
    ff = gate_ref.shape[0]
    pack_ref[:ff, :] = gate_ref[...]
    pack_ref[ff:, :] = up_ref[...]


def project_body(n, piece, where_ref, x_ref, gain_ref, masks_ref, *refs):
    blocks = grouped(refs[:-7], n)
    h1_ref, qk_ref, v_ref, p_ref, wt_ref, gains_ref, z_ref = refs[-7:]
    r = pl.program_id(0)
    heads = qk_ref.shape[1] // (2 * FDIM)
    total = wt_ref.shape[1]
    core = where_ref[n]

    @pl.when(r == 0)
    def _():
        if piece:
            for q, halves in enumerate(blocks):
                for other, half in enumerate(halves):
                    count, _, wb = half.shape
                    tile = jnp.zeros((16, wb), F32)
                    for j in range(count):
                        one = half[j, total : total + 16, :].astype(F32)
                        one = jnp.where(lanes(one.shape) < piece, one, 0.0)
                        tile = tile + (one if j == 0 else pltpu.roll(one, j * piece, 1))
                    side = core if other == 0 else 1 - core
                    at = pl.multiple_of((where_ref[q] * 2 + side) * wb, wb)
                    gains_ref[:, pl.ds(at, wb)] = tile[:8]
        else:
            gains_ref[...] = gain_ref[...]
        x = x_ref[...].astype(F32)
        normed = x * lax.rsqrt(jnp.mean(x * x, axis=-1, keepdims=True) + EPS)
        h1_ref[...] = (normed * gains_ref[0:1, :]).astype(BF16)
        z_ref[...] = jnp.zeros_like(z_ref)

    for index, halves in enumerate(blocks):

        @pl.when(r == index)
        def _():
            for other, half in enumerate(halves):
                count, _, wb = half.shape
                side = core if other == 0 else 1 - core
                for j in range(count):
                    at = j * wb if count * wb == wt_ref.shape[2] else (side * count + j) * wb
                    if not isinstance(at, int):
                        at = pl.multiple_of(at, wb)
                    wt_ref[0, :, pl.ds(at, wb)] = half[j, :total, :]

    h1 = h1_ref[...]
    nqk = qk_ref.shape[1]
    qk = mm(wt_ref[0, :nqk, :], h1, NT).astype(BF16)
    qk_ref[0] = qk
    v = mm(h1, wt_ref[0, nqk:, :], NT).astype(BF16)
    v_ref[0] = v
    tail = masks_ref[1:2, :]
    rows = v.shape[0]
    for pair in range(heads // 2):
        v_pair = v[:, pair * 128 : (pair + 1) * 128]
        both = []
        for j in range(2):
            i = 2 * pair + j
            k = qk[nqk // 2 + i * FDIM : nqk // 2 + (i + 1) * FDIM].astype(F32)
            phi = (features(k) * tail).astype(BF16)
            rhs = jnp.concatenate([v_pair, one_hot_lanes(rows, r * heads + i)], axis=1)
            res = mm(phi, rhs)
            both.append(res[:, :128])
            z_ref[...] += res[:, 128:]
        p_ref[r * (heads // 2) + pair] = own_half(both[0], 0, both[1]).astype(BF16)

    @pl.when(r == pl.num_programs(0) - 1)
    def _():
        p_ref[p_ref.shape[0] - 1] = z_ref[...].astype(BF16)


def project(where, x, gain, masks, blocks, heads, piece):
    n = len(blocks)
    rows, d = x.shape
    nqk, nv = 2 * heads * FDIM, heads * VDIM
    sums = n * heads // 2 + 1
    ins = (where, x, gain, masks, *flat(blocks))
    return call(
        functools.partial(project_body, n, piece),
        (
            sds((rows, d), BF16),
            sds((n, nqk, rows), BF16),
            sds((n, rows, nv), BF16),
            sds((sums, FROWS, 128), BF16),
            sds((n, nqk + nv, d), BF16),
            sds((8, d), F32),
        ),
        ins,
        grid=(n,),
        in_specs=[pl.BlockSpec(memory_space=pltpu.SMEM)] + [whole(x.shape) for x in ins[1:]],
        out_specs=[
            whole((rows, d)),
            by_row((nqk, rows)),
            by_row((rows, nv)),
            whole((sums, FROWS, 128)),
            by_row((nqk + nv, d)),
            whole((8, d)),
        ],
        scratch=[pltpu.VMEM((FROWS, 128), F32)],
        us=7,
        most=K1MOST,
    )


def local_body(qk_ref, v_ref, masks_ref, nd_ref):
    nqk = qk_ref.shape[1]
    heads = nqk // (2 * FDIM)
    rows = v_ref.shape[1]
    mask = doc_mask(masks_ref[...], rows)
    for pair in range(heads // 2):
        v_pair = v_ref[0, :, pair * 128 : (pair + 1) * 128]
        acc = None
        for j in range(2):
            i = 2 * pair + j
            q = qk_ref[0, i * FDIM : (i + 1) * FDIM, :]
            k = qk_ref[0, nqk // 2 + i * FDIM : nqk // 2 + (i + 1) * FDIM, :]
            s1 = mm(q, k, TN) * 0.25 + 1.0
            a = jnp.where(mask, 0.5 * s1 * s1 + 0.5, 0.0).astype(BF16)
            ones = own_half(jnp.ones((rows, 128), BF16), j)
            part = mm(a, jnp.concatenate([own_half(v_pair, j), ones], axis=1))
            acc = part if acc is None else acc + part
        nd_ref[0, pair] = acc


def local(qk, v, masks):
    n, nqk, rows = qk.shape
    heads = nqk // (2 * FDIM)
    return call(
        local_body,
        sds((n, heads // 2, rows, 256), F32),
        (qk, v, masks),
        grid=(n,),
        in_specs=[by_row(qk.shape[1:]), by_row(v.shape[1:]), whole(masks.shape)],
        out_specs=by_row((heads // 2, rows, 256)),
    )


def joined(first, second, flag):
    return first.astype(F32) + second.astype(F32) * flag


def carry_body(nd_ref, qk_ref, masks_ref, one_ref, two_ref, o_ref, on_ref, inv_ref, c_ref):
    r = pl.program_id(0)
    n = pl.num_programs(0)
    nqk = qk_ref.shape[1]
    heads = nqk // (2 * FDIM)
    last = one_ref.shape[0] - 1

    @pl.when(r == 0)
    def _():
        c_ref[last] = joined(one_ref[last], two_ref[last], masks_ref[3:4, 0:128]).astype(BF16)

    flag = masks_ref[3:4, 0:128]
    live = masks_ref[2:3, :]
    for pair in range(heads // 2):
        at = r * (heads // 2) + pair
        c = joined(one_ref[at], two_ref[at], flag).astype(BF16)
        c_ref[at] = c
        acc = nd_ref[0, pair]
        for j in range(2):
            i = 2 * pair + j
            q = qk_ref[0, i * FDIM : (i + 1) * FDIM, :].astype(F32)
            phi = (features(q) * live).astype(BF16)
            z = pick_columns(
                c_ref[last],
                lambda row: row == r * heads + i,
                lambda lane: (lane < VDIM) if j == 0 else (lane >= VDIM),
            ).astype(BF16)
            acc = acc + mm(phi, jnp.concatenate([own_half(c, j), z], axis=1), TN)
        inv = 1.0 / acc[:, 128:]
        on = acc[:, :128] * inv
        cols = slice(pair * 128, (pair + 1) * 128)
        o_ref[0, :, cols] = on.astype(BF16)
        on_ref[0, :, cols] = on
        inv_ref[0, :, cols] = inv


def carry(nd, qk, masks, one, two):
    n, nqk, rows = qk.shape
    heads = nqk // (2 * FDIM)
    nv = heads * VDIM
    return call(
        carry_body,
        (
            sds((n, rows, nv), BF16),
            sds((n, rows, nv), F32),
            sds((n, rows, nv), F32),
            sds(one.shape, BF16),
        ),
        (nd, qk, masks, one, two),
        grid=(n,),
        in_specs=[
            by_row(nd.shape[1:]),
            by_row(qk.shape[1:]),
            whole(masks.shape),
            whole(one.shape),
            whole(two.shape),
        ],
        out_specs=[by_row((rows, nv))] * 3 + [whole(one.shape)],
        most=True,
    )


def middle_body(x_ref, gain_ref, o_ref, w_ref, y1_ref, *h2_refs):
    n, _, width = o_ref.shape
    acc = x_ref[...].astype(F32)
    for r in range(n):
        acc = acc + mm(o_ref[r], w_ref[r * width : (r + 1) * width, :])
    y1_ref[...] = acc
    scale = lax.rsqrt(jnp.mean(acc * acc, axis=-1, keepdims=True) + EPS)
    give_rows(h2_refs, (acc * scale * gain_ref[1:2, :]).astype(BF16))


def give_rows(refs, value):
    at = 0
    for one in refs:
        one[...] = value[at : at + one.shape[0]]
        at += one.shape[0]


def middle(x, o, wo, gain):
    rows, d = x.shape
    res = call(
        middle_body,
        (sds((rows, d), F32), *[sds((rows // 2, d), BF16)] * 2),
        (x, gain, o, wo),
        us=4,
    )
    return res[0], res[1:]


def spread_out_body(w_ref, out_ref, down_ref):
    nb, _, wb = w_ref.shape
    split = out_ref.shape[0]
    for s in range(nb):
        out_ref[:, s * wb : (s + 1) * wb] = w_ref[s, :split, :]
        down_ref[:, s * wb : (s + 1) * wb] = w_ref[s, split:, :]


def spread_out(w, ff):
    nb, total, wb = w.shape
    d = nb * wb
    return call(spread_out_body, (sds((total - ff, d), BF16), sds((ff, d), BF16)), (w,), us=4)


def prepare_body(n, down_ref, *refs):
    cots, out_ref = refs[:n], refs[n]
    for r in range(n):
        out_ref[r] = mm(cots[r][...], down_ref[...], NT).astype(BF16)


def prepare(down, cots):
    n = len(cots)
    return call(
        functools.partial(prepare_body, n),
        sds((n, cots[0].shape[0], down.shape[0]), BF16),
        (down, *cots),
    )


def widen_body(w_ref, wide_ref):
    nb, _, wb = w_ref.shape
    for s in range(nb):
        wide_ref[:, s * wb : (s + 1) * wb] = w_ref[s]


def widen(w):
    nb, total, wb = w.shape
    return call(widen_body, sds((total, nb * wb), BF16), (w,))


def mlp_body(first_ref, second_ref, dhid_ref, w_ref, dh_ref, hid_ref, dg_ref, du_ref):
    ff = hid_ref.shape[1]
    h2 = join_rows((first_ref, second_ref))
    gate_w, up_w = w_ref[0:ff, :], w_ref[ff : 2 * ff, :]
    dhid = dhid_ref[0].astype(F32)
    g = mm(h2, gate_w, NT)
    u = mm(h2, up_w, NT)
    sig = jax.nn.sigmoid(g)
    act = g * sig
    hid_ref[...] = (act * u).astype(BF16)
    dg = (dhid * u * sig * (1.0 + g * (1.0 - sig))).astype(BF16)
    du = (dhid * act).astype(BF16)
    dg_ref[...] = dg
    du_ref[...] = du
    dh_ref[...] = (mm(dg, gate_w) + mm(du, up_w)).astype(BF16)


def mlp(index, h2, dhid, w):
    half, d = h2[0].shape
    rows = 2 * half
    ff = w.shape[0] // 2
    return call(
        mlp_body,
        (sds((rows, d), BF16), *[sds((rows, ff), BF16)] * 3),
        (*h2, dhid, w),
        grid=(1,),
        in_specs=[whole((half, d))] * 2
        + [pl.BlockSpec((1, rows, ff), lambda r: (index, 0, 0)), whole((2 * ff, d))],
        out_specs=[whole((rows, d))] + [whole((rows, ff))] * 3,
    )


def mlp_out_body(n, w_ref, *refs):
    for r in range(n):
        refs[n + r][...] = mm(refs[r][...], w_ref[...]).astype(BF16)


def mlp_out(hid, w):
    n = len(hid)
    return call(
        functools.partial(mlp_out_body, n),
        [sds((hid[0].shape[0], w.shape[1]), BF16)] * n,
        (w, *hid),
    )


def mlp_grads_body(n, *refs):
    h2, cot = grouped(refs[: 2 * n], n), grouped(refs[2 * n : 3 * n], n)
    hid, dg, du = (refs[(3 + k) * n : (4 + k) * n] for k in range(3))
    o_ref, ff = refs[6 * n], hid[0].shape[1]
    nb, _, wb = o_ref.shape
    for k, (left, right) in enumerate(((dg, h2), (du, h2), (hid, cot))):
        acc = None
        for r in range(n):
            part = mm(left[r][...], join_rows(right[r]), TN)
            acc = part if acc is None else acc + part
        acc = acc.astype(BF16)
        for s in range(nb):
            o_ref[s, k * ff : (k + 1) * ff, :] = acc[:, s * wb : (s + 1) * wb]


def mlp_grads(h2, cot, hid, dg, du, nb):
    n = len(h2)
    d, ff = h2[0][0].shape[1], hid[0].shape[1]
    ins = (*flat(h2), *cot, *hid, *dg, *du)
    return call(
        functools.partial(mlp_grads_body, n),
        sds((nb, 3 * ff, d // nb), BF16),
        ins,
        grid=(1,),
        in_specs=[whole(x.shape) for x in ins],
        out_specs=whole((nb, 3 * ff, d // nb)),
        us=9,
    )


def turn_body(n, y1_ref, cot_ref, gain_ref, *refs):
    parts, w_ref = refs[:n], refs[n]
    dy1_ref, dgain_ref, *f_refs = refs[n + 1 : n + 4]
    do_ref = refs[n + 4]
    rows_of = do_ref.shape[2]
    dh2 = parts[0][...].astype(F32)
    for r in range(1, n):
        dh2 = dh2 + parts[r][...].astype(F32)
    y1 = y1_ref[...]
    scale = lax.rsqrt(jnp.mean(y1 * y1, axis=-1, keepdims=True) + EPS)
    normed = y1 * scale
    dgain_ref[...] = jnp.sum(dh2 * normed, axis=0, keepdims=True)
    dn = dh2 * gain_ref[1:2, :]
    inner = jnp.mean(dn * normed, axis=-1, keepdims=True)
    dy1 = cot_ref[...].astype(F32) + scale * (dn - normed * inner)
    dy1_ref[...] = dy1
    f = dy1.astype(BF16)
    give_rows(f_refs, f)
    for r in range(n):
        do_ref[r] = mm(f, w_ref[r * rows_of : (r + 1) * rows_of, :], NT).astype(BF16)


def turn(parts, y1, cot, gain, wo):
    n = len(parts)
    rows, d = y1.shape
    nv = wo.shape[0] // n
    res = call(
        functools.partial(turn_body, n),
        (
            sds((rows, d), F32),
            sds((1, d), F32),
            sds((rows, d), BF16),
            sds((n, rows, nv), BF16),
        ),
        (y1, cot, gain, *parts, wo),
    )
    return res


def back_first_body(do_ref, on_ref, inv_ref, qk_ref, masks_ref, d_ref, p_ref, z_ref):
    r = pl.program_id(0)
    n = pl.num_programs(0)
    nqk = qk_ref.shape[1]
    heads = nqk // (2 * FDIM)
    rows = do_ref.shape[1]

    @pl.when(r == 0)
    def _():
        z_ref[...] = jnp.zeros_like(z_ref)

    live = masks_ref[2:3, :]
    lane = lanes((rows, 128))
    for pair in range(heads // 2):
        cols = slice(pair * 128, (pair + 1) * 128)
        wide = do_ref[0, :, cols].astype(F32) * inv_ref[0, :, cols]
        dnum = wide.astype(BF16)
        prod = -(wide * on_ref[0, :, cols])
        high = prod.astype(BF16)
        low = (prod - high.astype(F32)).astype(BF16)
        both = []
        for j in range(2):
            i = 2 * pair + j
            row = lax.broadcasted_iota(jnp.int32, (128, 128), 0)
            hot = jnp.where((row < VDIM) if j == 0 else (row >= VDIM), 1.0, 0.0).astype(BF16)
            dden = mm(high, hot) + mm(low, hot)
            d_ref[0, i] = own_half(dnum, j, with_pair(dden, j))
            dh = dden.astype(BF16)
            dl = (dden - dh.astype(F32)).astype(BF16)
            zero = jnp.zeros_like(dh)
            spot = r * heads + i
            zext = jnp.where(lane == spot, dh, jnp.where(lane == spot + n * heads, dl, zero))
            q = qk_ref[0, i * FDIM : (i + 1) * FDIM, :].astype(F32)
            phi = (features(q) * live).astype(BF16)
            res = mm(phi, jnp.concatenate([dnum, zext], axis=1))
            both.append(res[:, :128])
            z_ref[...] += res[:, 128:]
        p_ref[r * (heads // 2) + pair] = own_half(both[0], 0, both[1]).astype(BF16)

    @pl.when(r == n - 1)
    def _():
        p_ref[p_ref.shape[0] - 1] = z_ref[...].astype(BF16)


def back_first(do, on, inv, qk, masks):
    n, nqk, rows = qk.shape
    heads = nqk // (2 * FDIM)
    pieces = n * heads // 2 + 1
    return call(
        back_first_body,
        (sds((n, heads, rows, 128), BF16), sds((pieces, FROWS, 128), BF16)),
        (do, on, inv, qk, masks),
        grid=(n,),
        in_specs=[by_row(x.shape[1:]) for x in (do, on, inv, qk)] + [whole(masks.shape)],
        out_specs=[by_row((heads, rows, 128)), whole((pieces, FROWS, 128))],
        scratch=[pltpu.VMEM((FROWS, 128), F32)],
    )


def back_local_body(d_ref, qk_ref, v_ref, masks_ref, c_ref, dq_ref, dk_ref, dv_ref):
    r = pl.program_id(0)
    nqk = qk_ref.shape[1]
    heads = nqk // (2 * FDIM)
    rows = v_ref.shape[1]
    masks = masks_ref[...]
    mask = doc_mask(masks, rows)
    live = masks[2:3, :]
    last = c_ref.shape[0] - 1
    for pair in range(heads // 2):
        cols = slice(pair * 128, (pair + 1) * 128)
        v_pair = v_ref[0, :, cols]
        c = c_ref[r * (heads // 2) + pair]
        dv = None
        for j in range(2):
            i = 2 * pair + j
            q = qk_ref[0, i * FDIM : (i + 1) * FDIM, :]
            k = qk_ref[0, nqk // 2 + i * FDIM : nqk // 2 + (i + 1) * FDIM, :]
            s1 = mm(q, k, TN) * 0.25 + 1.0
            a = jnp.where(mask, 0.5 * s1 * s1 + 0.5, 0.0).astype(BF16)
            d = d_ref[0, i]
            da = mm(d, with_ones(v_pair, j), NT)
            ds = jnp.where(mask, da * s1, 0.0).astype(BF16)
            z = moved_pair(c_ref[last].astype(F32), r * heads + i, j)
            dphi = mm(own_half(c, j, z), d, NT) * live
            back = features_back(q.astype(F32), dphi)
            dq_ref[0, i * FDIM : (i + 1) * FDIM, :] = (mm(k, ds, NT) * 0.25 + back).astype(BF16)
            dk_ref[0, i * FDIM : (i + 1) * FDIM, :] = mm(q, ds) * 0.25
            part = mm(own_half(d, j), a, TN)
            dv = part if dv is None else dv + part
        dv_ref[0, cols, :] = dv


def back_local(d, qk, v, masks, c):
    n, nqk, rows = qk.shape
    heads = nqk // (2 * FDIM)
    nv = heads * VDIM
    return call(
        back_local_body,
        (sds((n, nqk // 2, rows), BF16), sds((n, nqk // 2, rows), F32), sds((n, nv, rows), F32)),
        (d, qk, v, masks, c),
        grid=(n,),
        in_specs=[by_row(x.shape[1:]) for x in (d, qk, v)] + [whole(masks.shape), whole(c.shape)],
        out_specs=[by_row((nqk // 2, rows)), by_row((nqk // 2, rows)), by_row((nv, rows))],
    )


def back_last_body(
    where_ref, dq_ref, dk_ref, dv_ref, qk_ref, v_ref, masks_ref, one_ref, two_ref, h1_ref, wt_ref,
    gain_ref, x_ref, dy1_ref, dgain_mlp_ref, grad_ref, *refs,
):
    *dw_refs, dgain_ref, z_ref, acc_ref, wide_ref = refs
    r = pl.program_id(0)
    n = pl.num_programs(0)
    nqk = qk_ref.shape[1]
    heads = nqk // (2 * FDIM)
    nb, wb = dw_refs[0].shape[1] * len(dw_refs), dw_refs[0].shape[3]
    last = one_ref.shape[0] - 1
    flag = masks_ref[4:5, 0:128]
    tail = masks_ref[1:2, :]

    @pl.when(r == 0)
    def _():
        z_ref[...] = joined(one_ref[last], two_ref[last], flag)
        acc_ref[...] = jnp.zeros_like(acc_ref)

    dks, dvs = [], []
    for pair in range(heads // 2):
        cols = slice(pair * 128, (pair + 1) * 128)
        at = r * (heads // 2) + pair
        dp = joined(one_ref[at], two_ref[at], flag).astype(BF16)
        v_pair = v_ref[0, :, cols]
        dv = dv_ref[0, cols, :]
        for j in range(2):
            i = 2 * pair + j
            k = qk_ref[0, nqk // 2 + i * FDIM : nqk // 2 + (i + 1) * FDIM, :].astype(F32)
            z = moved_pair(z_ref[...], r * heads + i, j)
            dphi = mm(own_half(dp, j, z), with_ones(v_pair, j), NT) * tail
            dk = dk_ref[0, i * FDIM : (i + 1) * FDIM, :] + features_back(k, dphi)
            dks.append(dk.astype(BF16))
            phi = (features(k) * tail).astype(BF16)
            dv = dv + mm(own_half(dp, j), phi, TN)
        dvs.append(dv.astype(BF16))
    d = jnp.concatenate([dq_ref[0]] + dks + dvs, axis=0)
    total = d.shape[0]
    wide_ref[...] = mm(d, h1_ref[...]).astype(BF16)
    give_blocks(where_ref, wide_ref, [one.at[r, :, 0:total, :] for one in dw_refs])
    acc_ref[...] += mm(d, wt_ref[0], TN)

    @pl.when(r == n - 1)
    def _():
        dh1 = acc_ref[...]
        x = x_ref[...].astype(F32)
        scale = lax.rsqrt(jnp.mean(x * x, axis=-1, keepdims=True) + EPS)
        normed = x * scale
        dgain_ref[0:1, :] = jnp.sum(dh1 * normed, axis=0, keepdims=True)
        dgain_ref[1:2, :] = dgain_mlp_ref[...]
        dn = dh1 * gain_ref[0:1, :]
        inner = jnp.mean(dn * normed, axis=-1, keepdims=True)
        grad_ref[...] = dy1_ref[...] + scale * (dn - normed * inner)
        if nb > 1:
            groups, count = dw_refs[0].shape[:2]
            across = groups * nb * wb // dgain_ref.shape[1]
            tiles = nb // across
            for q in range(groups):
                for z in range(count):
                    at = where_ref[q] * tiles + (where_ref[groups + 1] ^ z) * 2 // across
                    both = dgain_ref[:, pl.ds(pl.multiple_of(at * wb, wb), wb)]
                    high = both.astype(BF16).astype(F32)
                    fill = jnp.zeros((dw_refs[0].shape[2] - total - 4, wb), F32)
                    block = jnp.concatenate([high, both - high, fill], axis=0).astype(BF16)
                    for one in dw_refs:
                        one[q, z, total:, :] = block


def give_blocks(where_ref, wide_ref, refs):
    count, _, wb = refs[0].shape
    last = where_ref.shape[0] - 1
    for index, one in enumerate(refs):
        for z in range(count):
            at = 0
            if len(refs) == 2:
                core = where_ref[last - 1]
                side = core if index == 0 else 1 - core
                at = pl.multiple_of(((where_ref[last] ^ z) * 2 + side) * wb, wb)
            one[z] = wide_ref[:, pl.ds(at, wb)]


def back_last(where, dq, dk, dv, qk, v, masks, one, two, h1, w, gain, x, dy1, dgain_mlp, nb):
    n, nqk, rows = qk.shape
    _, total, d = w.shape
    shapes = [(n, 1, total + 16, d)] if nb == 1 else [(n, nb // 2, total + 16, d // nb)] * 2
    ins = (where, dq, dk, dv, qk, v, masks, one, two, h1, w, gain, x, dy1, dgain_mlp)
    return call(
        back_last_body,
        (sds((rows, d), F32), *[sds(shape, BF16) for shape in shapes], sds((2, d), F32)),
        ins,
        grid=(n,),
        in_specs=[pl.BlockSpec(memory_space=pltpu.SMEM)]
        + [by_row(y.shape[1:]) for y in (dq, dk, dv, qk, v)]
        + [whole(y.shape) for y in (masks, one, two, h1)]
        + [by_row(w.shape[1:])]
        + [whole(y.shape) for y in (gain, x, dy1, dgain_mlp)],
        out_specs=[whole((rows, d)), *[whole(shape) for shape in shapes], whole((2, d))],
        scratch=[
            pltpu.VMEM((FROWS, 128), F32),
            pltpu.VMEM((rows, d), F32),
            pltpu.VMEM((total, d), BF16),
        ],
        us=10,
        most=True,
    )


def out_grads_body(n, where_ref, f_ref, *refs):
    o_ref, outs, wide_ref = refs[0], refs[1:-1], refs[-1]
    for r in range(n):
        wide_ref[...] = mm(o_ref[r], f_ref[...], TN).astype(BF16)
        give_blocks(where_ref, wide_ref, [one.at[r] for one in outs])


def out_grads(where, o, f, nb):
    n, _, nv = o.shape
    d = f.shape[1]
    shapes = [(n, 1, nv, d)] if nb == 1 else [(n, nb // 2, nv, d // nb)] * 2
    return call(
        functools.partial(out_grads_body, n),
        [sds(shape, BF16) for shape in shapes],
        (where, f, o),
        scratch=[pltpu.VMEM((nv, d), BF16)],
        smem=1,
        us=3,
    )


def xor_pairs(size, r):
    return [(i, i ^ r) for i in range(size)]


def swap(parts):
    size = lax.axis_size("head")
    return [parts[0]] + [lax.ppermute(parts[r], "head", xor_pairs(size, r)) for r in range(1, size)]


def halves(x):
    return [x[: x.shape[0] // 2], x[x.shape[0] // 2 :]]


def sum_parts(parts):
    total = parts[0].astype(F32)
    for part in parts[1:]:
        total = total + part.astype(F32)
    return total.astype(parts[0].dtype)


def spread(x):
    return [[one] for one in swap([x] * lax.axis_size("head"))]


def spread_halves(pair):
    size = lax.axis_size("head")
    a, b = pair

    def send(x, r):
        return lax.ppermute(x, "head", xor_pairs(size, r))

    if size != 4:
        return [[a, b]] + [[send(a, r), send(b, r)] for r in range(1, size)]
    ax, by = send(a, 1), send(b, 2)
    ay, bx = send(a, 2), send(b, 1)
    return [[a, b], [ax, bx], [ay, by], [send(ax, 2), send(by, 1)]]


def shifted(x, step):
    size = lax.axis_size("seq")
    return lax.ppermute(x, "seq", [(i, i + step) for i in range(size) if 0 <= i + step < size])


def over_z(x):
    count, size = x.shape[0], lax.axis_size("seq")
    if count <= 4:
        parts = [lax.ppermute(x[k], "seq", xor_pairs(size, 2 * k)) for k in range(1, count)]
        total = x[0].astype(F32)
        for part in parts:
            total = total + part.astype(F32)
        return total
    while count > 1:
        count //= 2
        got = lax.ppermute(x[count:], "seq", xor_pairs(size, 2 * count))
        x = (x[:count].astype(F32) + got.astype(F32)).astype(x.dtype)
    return x[0].astype(F32)


def carried(x, labels, step, join, before):
    size, me = lax.axis_size("seq"), lax.axis_index("seq")
    reach = max(size // 4, 1)
    k = 1
    while 2 * k < reach:
        other = jnp.take(labels, jnp.clip(me - step * k, 0, size - 1))
        flag = (other == jnp.take(labels, me)).astype(F32)
        x = join(x, shifted(x, step * k), flag)
        k *= 2
    one = shifted(x, step)
    one, before = lax.optimization_barrier((one, before))
    return one, shifted(one, step * k)


def on_device(
    tokens, doc_ids, query_weight, key_weight, value_weight, out_weight,
    gate_weight, up_weight, down_weight, mix_gain, mlp_gain, cotangent,
):
    n, blocks = lax.axis_size("head"), lax.axis_size("seq")
    here, me = lax.axis_index("head"), lax.axis_index("seq")
    rows, d = tokens.shape[1:]
    wb = d // blocks
    nb = blocks if wb % 128 == 0 else 1
    heads = query_weight.shape[1] // FDIM
    nqkv = 2 * heads * FDIM + heads * VDIM
    nv = heads * VDIM
    ff = gate_weight.shape[1]
    x, cot = tokens[0], cotangent[0]

    piece = mix_gain.shape[0]
    doc_rows = rows // wb
    extra = -(-(2 + doc_rows) // 16) * 16
    pack = call(
        pack_body,
        sds((nqkv + extra, wb), BF16),
        (
            query_weight.T, key_weight.T, value_weight, mix_gain.reshape(1, -1), mlp_gain.reshape(1, -1),
            doc_ids.reshape(doc_rows, wb),
        ),
        us=2,
        most=True,
    )
    out_slices = swap([out_weight] * n)
    pack = lax.all_gather(pack, "seq")
    near_cots = [lax.ppermute(cot, "head", xor_pairs(n, r)) for r in range(1, n - 1)]
    near_cots, pack = lax.optimization_barrier((near_cots, pack))
    def gathered(w):
        return w if nb == blocks else jnp.transpose(w, (1, 0, 2)).reshape(1, w.shape[1], d)

    def unblocked(w):
        if nb == blocks:
            return w
        w = w.reshape(w.shape[1:-1] + (blocks, wb))
        return jnp.moveaxis(w, -2, 0)

    core = (me % 2).reshape(1)
    where = jnp.concatenate([here ^ jnp.arange(n, dtype=jnp.int32), core, (me // 2).reshape(1)])
    half = blocks // 2
    mine = lax.dynamic_slice_in_dim(pack, core[0] * half, half)
    other = lax.dynamic_slice_in_dim(pack, (1 - core[0]) * half, half)
    down_late, mine = lax.optimization_barrier((down_weight, mine))
    second = lax.all_gather(jnp.concatenate([*out_slices, down_late], axis=0), "seq")

    docs = pack[:, nqkv + 2 : nqkv + 2 + doc_rows].reshape(blocks, rows).astype(F32)
    segs = jnp.take(docs, me, axis=0)
    lasts = docs[:, -1]
    before = jnp.where(me > 0, jnp.take(lasts, jnp.maximum(me - 1, 0)), -1.0)
    final_label = jnp.take(lasts, me)
    labels_back = jnp.concatenate([jnp.full((1,), -1.0), lasts[:-1]])

    def flag_of(labels, step):
        reach = max(blocks // 4, 1)
        k = 1
        while 2 * k < reach:
            k *= 2
        near = jnp.take(labels, jnp.clip(me - step, 0, blocks - 1))
        far = jnp.take(labels, jnp.clip(me - step * (1 + k), 0, blocks - 1))
        return (near == far).astype(F32)

    masks = jnp.stack(
        [
            segs,
            (segs == final_label).astype(F32),
            (segs == before).astype(F32),
            jnp.full((rows,), 1.0) * flag_of(lasts, 1),
            jnp.full((rows,), 1.0) * flag_of(labels_back, -1),
        ]
        + [jnp.zeros_like(segs)] * 3
    )

    mine = swap([mine] * n)
    mine[1], masks = lax.optimization_barrier((mine[1], masks))
    pairs = [[mine[0], other]]
    pairs += [[one, lax.ppermute(one, "seq", xor_pairs(blocks, 1))] for one in mine[1:]]
    if nb == blocks:
        gain_in = jnp.zeros((8, 128), F32)
    else:
        small = jnp.stack([jnp.stack([one[:, nqkv : nqkv + 2, :piece] for one in pair]) for pair in pairs])
        small = jnp.take(jnp.take(small, here ^ jnp.arange(n), axis=0), core[0] ^ jnp.arange(2), axis=1)
        gain_in = jnp.transpose(small.reshape(n, blocks, 2, piece), (2, 0, 1, 3)).reshape(2, d)
        gain_in = jnp.pad(gain_in.astype(F32), ((0, 6), (0, 0)))
    if nb != blocks:
        pairs = [
            [gathered(jnp.where(core[0] == 0, jnp.concatenate(p), jnp.concatenate(p[::-1])))] for p in pairs
        ]
    cot_late, pairs[1:] = lax.optimization_barrier((cot, pairs[1:]))
    wide = call(pack_two_body, sds((2 * ff, wb), BF16), (gate_weight.T, up_weight.T), us=2)

    def join(a, b, flag):
        return (a.astype(F32) + b.astype(F32) * flag).astype(BF16)

    h1, qk, v, sums, w_qkv, gains = project(
        where, x, gain_in, masks, pairs, heads, piece if nb == blocks else 0
    )
    cots = [cot, *near_cots, lax.ppermute(cot_late, "head", xor_pairs(n, n - 1))]
    nd = local(qk, v, masks)
    one, two = carried(sums, lasts, 1, join, nd)
    w_out, w_down = spread_out(gathered(second), ff)
    wide, one = lax.optimization_barrier((wide, one))
    w_mlp = widen(gathered(lax.all_gather(wide, "seq")))
    dhid = prepare(w_down, cots)
    o, on, inv, c = carry(nd, qk, masks, one, two)
    y1, h2 = middle(x, o, w_out, gains)
    h2s = spread_halves(h2)
    res = [None] * n
    held = h2s[n - 1]
    for r in range(n - 1, -1, -1):
        res[r] = mlp(r, held, dhid, w_mlp)
        if r:
            held, res[r] = lax.optimization_barrier((list(h2s[r - 1]), list(res[r])))
    dparts, hid, dg, du = ([t[k] for t in res] for k in range(4))
    dparts = swap(dparts)
    oparts = mlp_out(hid, w_down)
    dparts, oparts = lax.optimization_barrier((dparts, oparts))
    dy1, dgain_mlp, f, do = turn(dparts, y1, cot, gains, w_out)
    dext, dsums = back_first(do, on, inv, qk, masks)
    hid_late, dg, du, dsums = lax.optimization_barrier((hid, dg, du, dsums))
    dmlp = mlp_grads(h2s, cots, hid_late, dg, du, nb)
    dq, dk, dv = back_local(dext, qk, v, masks, c)
    back_one, back_two = carried(dsums, labels_back, -1, join, (dq, dk, dv))

    def split(w):
        if nb == blocks:
            return w
        w = unblocked(w[0][:, 0][None])
        w = jnp.moveaxis(w.reshape((half, 2) + w.shape[1:]), 2, 0)
        w = jnp.take(w, (me // 2) ^ jnp.arange(half), axis=1)
        return [lax.dynamic_index_in_dim(w, bit, 2, keepdims=False) for bit in (core[0], 1 - core[0])]

    def pooled(keep, give):
        got = lax.ppermute(give, "seq", xor_pairs(blocks, 1))
        return [(keep[r].astype(F32) + got[r].astype(F32)).astype(BF16) for r in range(n)]

    dout = sum_parts(swap(pooled(*split(out_grads(where, o, f, nb)))))
    dmlp, back_two, dout = lax.optimization_barrier((dmlp, back_two, dout))
    dmlp = lax.psum_scatter(unblocked(dmlp), "seq", tiled=True)[0].astype(F32)
    grad_tokens, *dqkv, dgains = back_last(
        where, dq, dk, dv, qk, v, masks, back_one, back_two, h1, w_qkv, gains, x, dy1, dgain_mlp, nb
    )
    near = [lax.ppermute(oparts[r], "head", xor_pairs(n, r)) for r in range(1, n - 1)]
    near, dqkv = lax.optimization_barrier((near, dqkv))
    dqkv = pooled(*split(dqkv))
    far = lax.ppermute(oparts[n - 1], "head", xor_pairs(n, n - 1))
    if FAR:
        far, dqkv = lax.optimization_barrier((far, dqkv))
    dqkv = over_z(sum_parts(swap(dqkv)))
    oparts = [oparts[0], *near, far]
    dout = over_z(dout)
    if nb == blocks:
        parts = dqkv[nqkv : nqkv + 2] + dqkv[nqkv + 2 : nqkv + 4]
        total = lax.dynamic_slice_in_dim(parts, me % (wb // piece) * piece, piece, axis=1)
    else:
        total = lax.psum_scatter(dgains, ("head", "seq"), scatter_dimension=1, tiled=True)
    output = y1
    for part in oparts:
        output = output + part.astype(F32)

    kq = heads * FDIM
    return (
        output.astype(BF16)[None],
        grad_tokens[None],
        dqkv[:kq].T,
        dqkv[kq : 2 * kq].T,
        dqkv[2 * kq : nqkv].T,
        dout,
        dmlp[:ff].T,
        dmlp[ff : 2 * ff].T,
        dmlp[2 * ff :],
        total[0],
        total[1],
    )


def solution(mesh):
    placed = (
        P("head", "seq", None),
        P("head", "seq"),
        P("seq", "head"),
        P("seq", "head"),
        P("seq", "head"),
        P("head", "seq"),
        P("seq", "head"),
        P("seq", "head"),
        P("head", "seq"),
        P(("head", "seq")),
        P(("head", "seq")),
        P("head", "seq", None),
    )
    return jax.shard_map(
        on_device,
        mesh=mesh,
        in_specs=placed,
        out_specs=(
            P("head", "seq", None),
            P("head", "seq", None),
            P("seq", "head"),
            P("seq", "head"),
            P("seq", "head"),
            P("head", "seq"),
            P("seq", "head"),
            P("seq", "head"),
            P("head", "seq"),
            P(("head", "seq")),
            P(("head", "seq")),
        ),
        check_vma=False,
    )
```

```python
import functools

import jax
import jax.numpy as jnp
from jax import lax
from jax.experimental import pallas as pl
from jax.experimental.pallas import tpu as pltpu
from jax.sharding import PartitionSpec as P

FDIM = 16
VDIM = 64
EPS = 1e-06
ROOT_HALF = 0.7071067811865476
FROWS = 11 * FDIM
F32 = jnp.float32
BF16 = jnp.bfloat16
VMEM_BYTES = 24 * 1024 * 1024
VMEM_MOST = 56 * 1024 * 1024
K1MOST = True
FAR = False

NN = (((1,), (0,)), ((), ()))
NT = (((1,), (1,)), ((), ()))
TN = (((0,), (0,)), ((), ()))


def mm(a, b, dims=NN):
    return lax.dot_general(a, b, dims, preferred_element_type=F32)


def call(body, outs, ins, grid=None, in_specs=None, out_specs=None, scratch=(), smem=0, us=5, most=False):
    kwargs = {}
    if smem:
        spaces = [pltpu.SMEM] * smem + [pltpu.VMEM] * (len(ins) - smem)
        kwargs = dict(in_specs=[pl.BlockSpec(memory_space=space) for space in spaces])
    if grid is not None:
        kwargs = dict(grid=grid, in_specs=in_specs, out_specs=out_specs)
    return pl.pallas_call(
        body,
        out_shape=outs,
        scratch_shapes=list(scratch),
        compiler_params=pltpu.CompilerParams(vmem_limit_bytes=VMEM_MOST if most else VMEM_BYTES),
        cost_estimate=pl.CostEstimate(flops=0, bytes_accessed=us * 600000, transcendentals=0),
        **kwargs,
    )(*ins)


def sds(shape, dtype):
    return jax.ShapeDtypeStruct(shape, dtype)


def whole(shape):
    return pl.BlockSpec(shape, lambda r: (0,) * len(shape))


def by_row(shape):
    return pl.BlockSpec((1,) + tuple(shape), lambda r: (r,) + (0,) * len(shape))


def coef(d):
    return ROOT_HALF if d in (0, FDIM // 2) else 1.0


def features(w):
    half = w * 0.5
    rows = [half]
    for d in range(FDIM // 2 + 1):
        other = half if d == 0 else pltpu.roll(half, FDIM - d, 0)
        rows.append(half * other * coef(d))
    first = lax.broadcasted_iota(jnp.int32, half.shape, 0) == 0
    rows.append(jnp.where(first, 1.0, 0.0))
    return jnp.concatenate(rows, axis=0)


def features_back(w, grad):
    half = w * 0.5
    total = grad[:FDIM]
    for d in range(FDIM // 2 + 1):
        part = grad[FDIM * (d + 1) : FDIM * (d + 2)]
        if d == 0:
            total = total + part * half * (2.0 * coef(0))
        else:
            near = part * pltpu.roll(half, FDIM - d, 0)
            far = pltpu.roll(part * half, d, 0)
            total = total + (near + far) * coef(d)
    return total * 0.5


def lanes(shape):
    return lax.broadcasted_iota(jnp.int32, shape, len(shape) - 1)


def one_hot_lanes(rows, index):
    lane = lanes((rows, 128))
    hot = jnp.logical_or(lane == index, lane == index + FDIM)
    return jnp.where(hot, 1.0, 0.0).astype(BF16)


def own_half(x, j, other=None):
    left = lanes(x.shape) < VDIM
    keep = left if j == 0 else jnp.logical_not(left)
    return jnp.where(keep, x, jnp.zeros_like(x) if other is None else other)


def pick_columns(z, column, spots):
    row = lax.broadcasted_iota(jnp.int32, (128, 128), 0)
    hot = jnp.where(column(row), 1.0, 0.0) * jnp.where(spots(lanes((128, 128))), 1.0, 0.0)
    return mm(z, hot.astype(BF16))


def doc_mask(masks, rows):
    seg = masks[0:1, :]
    col = jnp.transpose(masks)[:, 0:1]
    causal = lax.broadcasted_iota(jnp.int32, (rows, rows), 0) >= lax.broadcasted_iota(
        jnp.int32, (rows, rows), 1
    )
    return jnp.logical_and(causal, col == seg)


def with_pair(z, j):
    lane = lanes(z.shape)
    base = VDIM if j == 0 else 0
    high = z.astype(BF16)
    low = (z - high.astype(F32)).astype(BF16)
    zero = jnp.zeros_like(high)
    return jnp.where(lane == base, high, jnp.where(lane == base + FDIM, low, zero))


def moved_pair(z, spot, j):
    base = VDIM if j == 0 else 0
    z = pltpu.roll(z, lax.rem(base - spot + 128, 128), 1)
    lane = lanes(z.shape)
    keep = jnp.logical_or(lane == base, lane == base + FDIM)
    return jnp.where(keep, z, 0.0).astype(BF16)


def with_ones(x, j):
    lane = lanes(x.shape)
    base = VDIM if j == 0 else 0
    hot = jnp.where(jnp.logical_or(lane == base, lane == base + FDIM), 1.0, 0.0).astype(x.dtype)
    return own_half(x, j, hot)


def join_rows(refs):
    return refs[0][...] if len(refs) == 1 else jnp.concatenate([one[...] for one in refs], axis=0)


def grouped(refs, n):
    k = len(refs) // n
    return [refs[i * k : (i + 1) * k] for i in range(n)]


def flat(lists):
    return [x for one in lists for x in one]


def take_row(r, groups, ref):
    for index, one in enumerate(groups):
        @pl.when(r == index)
        def _():
            ref[...] = join_rows(one)


def give_row(r, refs, value):
    for index, one in enumerate(refs):
        @pl.when(r == index)
        def _():
            one[...] = value


def pack_body(q_ref, k_ref, v_ref, mix_ref, mlp_ref, docs_ref, pack_ref):
    at = 0
    for one in (q_ref, k_ref):
        pack_ref[at : at + one.shape[0], :] = one[...]
        at += one.shape[0]
    pack_ref[at : at + v_ref.shape[1], :] = v_ref[...].T
    at += v_ref.shape[1]
    wb = pack_ref.shape[1]
    extra = pack_ref.shape[0] - at
    rows = []
    for one in (mix_ref, mlp_ref):
        fill = jnp.zeros((1, wb - one.shape[1]), F32)
        rows.append(jnp.concatenate([one[...].astype(F32), fill], axis=1))
    rows.append(docs_ref[...].astype(F32))
    rows.append(jnp.zeros((extra - 2 - docs_ref.shape[0], wb), F32))
    pack_ref[at:, :] = jnp.concatenate(rows, axis=0).astype(BF16)


def pack_two_body(gate_ref, up_ref, pack_ref):
    ff = gate_ref.shape[0]
    pack_ref[:ff, :] = gate_ref[...]
    pack_ref[ff:, :] = up_ref[...]


def project_body(n, piece, where_ref, x_ref, gain_ref, masks_ref, *refs):
    blocks = grouped(refs[:-7], n)
    h1_ref, qk_ref, v_ref, p_ref, wt_ref, gains_ref, z_ref = refs[-7:]
    r = pl.program_id(0)
    heads = qk_ref.shape[1] // (2 * FDIM)
    total = wt_ref.shape[1]
    core = where_ref[n]

    @pl.when(r == 0)
    def _():
        if piece:
            for q, halves in enumerate(blocks):
                for other, half in enumerate(halves):
                    count, _, wb = half.shape
                    tile = jnp.zeros((16, wb), F32)
                    for j in range(count):
                        one = half[j, total : total + 16, :].astype(F32)
                        one = jnp.where(lanes(one.shape) < piece, one, 0.0)
                        tile = tile + (one if j == 0 else pltpu.roll(one, j * piece, 1))
                    side = core if other == 0 else 1 - core
                    at = pl.multiple_of((where_ref[q] * 2 + side) * wb, wb)
                    gains_ref[:, pl.ds(at, wb)] = tile[:8]
        else:
            gains_ref[...] = gain_ref[...]
        x = x_ref[...].astype(F32)
        normed = x * lax.rsqrt(jnp.mean(x * x, axis=-1, keepdims=True) + EPS)
        h1_ref[...] = (normed * gains_ref[0:1, :]).astype(BF16)
        z_ref[...] = jnp.zeros_like(z_ref)

    for index, halves in enumerate(blocks):

        @pl.when(r == index)
        def _():
            for other, half in enumerate(halves):
                count, _, wb = half.shape
                side = core if other == 0 else 1 - core
                for j in range(count):
                    at = j * wb if count * wb == wt_ref.shape[2] else (side * count + j) * wb
                    if not isinstance(at, int):
                        at = pl.multiple_of(at, wb)
                    wt_ref[0, :, pl.ds(at, wb)] = half[j, :total, :]

    h1 = h1_ref[...]
    nqk = qk_ref.shape[1]
    qk = mm(wt_ref[0, :nqk, :], h1, NT).astype(BF16)
    qk_ref[0] = qk
    v = mm(h1, wt_ref[0, nqk:, :], NT).astype(BF16)
    v_ref[0] = v
    tail = masks_ref[1:2, :]
    rows = v.shape[0]
    for pair in range(heads // 2):
        v_pair = v[:, pair * 128 : (pair + 1) * 128]
        both = []
        for j in range(2):
            i = 2 * pair + j
            k = qk[nqk // 2 + i * FDIM : nqk // 2 + (i + 1) * FDIM].astype(F32)
            phi = (features(k) * tail).astype(BF16)
            rhs = jnp.concatenate([v_pair, one_hot_lanes(rows, r * heads + i)], axis=1)
            res = mm(phi, rhs)
            both.append(res[:, :128])
            z_ref[...] += res[:, 128:]
        p_ref[r * (heads // 2) + pair] = own_half(both[0], 0, both[1]).astype(BF16)

    @pl.when(r == pl.num_programs(0) - 1)
    def _():
        p_ref[p_ref.shape[0] - 1] = z_ref[...].astype(BF16)


def project(where, x, gain, masks, blocks, heads, piece):
    n = len(blocks)
    rows, d = x.shape
    nqk, nv = 2 * heads * FDIM, heads * VDIM
    sums = n * heads // 2 + 1
    ins = (where, x, gain, masks, *flat(blocks))
    return call(
        functools.partial(project_body, n, piece),
        (
            sds((rows, d), BF16),
            sds((n, nqk, rows), BF16),
            sds((n, rows, nv), BF16),
            sds((sums, FROWS, 128), BF16),
            sds((n, nqk + nv, d), BF16),
            sds((8, d), F32),
        ),
        ins,
        grid=(n,),
        in_specs=[pl.BlockSpec(memory_space=pltpu.SMEM)] + [whole(x.shape) for x in ins[1:]],
        out_specs=[
            whole((rows, d)),
            by_row((nqk, rows)),
            by_row((rows, nv)),
            whole((sums, FROWS, 128)),
            by_row((nqk + nv, d)),
            whole((8, d)),
        ],
        scratch=[pltpu.VMEM((FROWS, 128), F32)],
        us=7,
        most=K1MOST,
    )


def local_body(qk_ref, v_ref, masks_ref, nd_ref):
    nqk = qk_ref.shape[1]
    heads = nqk // (2 * FDIM)
    rows = v_ref.shape[1]
    mask = doc_mask(masks_ref[...], rows)
    for pair in range(heads // 2):
        v_pair = v_ref[0, :, pair * 128 : (pair + 1) * 128]
        acc = None
        for j in range(2):
            i = 2 * pair + j
            q = qk_ref[0, i * FDIM : (i + 1) * FDIM, :]
            k = qk_ref[0, nqk // 2 + i * FDIM : nqk // 2 + (i + 1) * FDIM, :]
            s1 = mm(q, k, TN) * 0.25 + 1.0
            a = jnp.where(mask, 0.5 * s1 * s1 + 0.5, 0.0).astype(BF16)
            ones = own_half(jnp.ones((rows, 128), BF16), j)
            part = mm(a, jnp.concatenate([own_half(v_pair, j), ones], axis=1))
            acc = part if acc is None else acc + part
        nd_ref[0, pair] = acc


def local(qk, v, masks):
    n, nqk, rows = qk.shape
    heads = nqk // (2 * FDIM)
    return call(
        local_body,
        sds((n, heads // 2, rows, 256), F32),
        (qk, v, masks),
        grid=(n,),
        in_specs=[by_row(qk.shape[1:]), by_row(v.shape[1:]), whole(masks.shape)],
        out_specs=by_row((heads // 2, rows, 256)),
    )


def joined(first, second, flag):
    return first.astype(F32) + second.astype(F32) * flag


def carry_body(nd_ref, qk_ref, masks_ref, one_ref, two_ref, o_ref, on_ref, inv_ref, c_ref):
    r = pl.program_id(0)
    n = pl.num_programs(0)
    nqk = qk_ref.shape[1]
    heads = nqk // (2 * FDIM)
    last = one_ref.shape[0] - 1

    @pl.when(r == 0)
    def _():
        c_ref[last] = joined(one_ref[last], two_ref[last], masks_ref[3:4, 0:128]).astype(BF16)

    flag = masks_ref[3:4, 0:128]
    live = masks_ref[2:3, :]
    for pair in range(heads // 2):
        at = r * (heads // 2) + pair
        c = joined(one_ref[at], two_ref[at], flag).astype(BF16)
        c_ref[at] = c
        acc = nd_ref[0, pair]
        for j in range(2):
            i = 2 * pair + j
            q = qk_ref[0, i * FDIM : (i + 1) * FDIM, :].astype(F32)
            phi = (features(q) * live).astype(BF16)
            z = pick_columns(
                c_ref[last],
                lambda row: row == r * heads + i,
                lambda lane: (lane < VDIM) if j == 0 else (lane >= VDIM),
            ).astype(BF16)
            acc = acc + mm(phi, jnp.concatenate([own_half(c, j), z], axis=1), TN)
        inv = 1.0 / acc[:, 128:]
        on = acc[:, :128] * inv
        cols = slice(pair * 128, (pair + 1) * 128)
        o_ref[0, :, cols] = on.astype(BF16)
        on_ref[0, :, cols] = on
        inv_ref[0, :, cols] = inv


def carry(nd, qk, masks, one, two):
    n, nqk, rows = qk.shape
    heads = nqk // (2 * FDIM)
    nv = heads * VDIM
    return call(
        carry_body,
        (
            sds((n, rows, nv), BF16),
            sds((n, rows, nv), F32),
            sds((n, rows, nv), F32),
            sds(one.shape, BF16),
        ),
        (nd, qk, masks, one, two),
        grid=(n,),
        in_specs=[
            by_row(nd.shape[1:]),
            by_row(qk.shape[1:]),
            whole(masks.shape),
            whole(one.shape),
            whole(two.shape),
        ],
        out_specs=[by_row((rows, nv))] * 3 + [whole(one.shape)],
        most=True,
    )


def middle_body(x_ref, gain_ref, o_ref, w_ref, y1_ref, *h2_refs):
    n, _, width = o_ref.shape
    acc = x_ref[...].astype(F32)
    for r in range(n):
        acc = acc + mm(o_ref[r], w_ref[r * width : (r + 1) * width, :])
    y1_ref[...] = acc
    scale = lax.rsqrt(jnp.mean(acc * acc, axis=-1, keepdims=True) + EPS)
    give_rows(h2_refs, (acc * scale * gain_ref[1:2, :]).astype(BF16))


def give_rows(refs, value):
    at = 0
    for one in refs:
        one[...] = value[at : at + one.shape[0]]
        at += one.shape[0]


def middle(x, o, wo, gain):
    rows, d = x.shape
    res = call(
        middle_body,
        (sds((rows, d), F32), *[sds((rows // 2, d), BF16)] * 2),
        (x, gain, o, wo),
        us=4,
    )
    return res[0], res[1:]


def spread_out_body(w_ref, out_ref, down_ref):
    nb, _, wb = w_ref.shape
    split = out_ref.shape[0]
    for s in range(nb):
        out_ref[:, s * wb : (s + 1) * wb] = w_ref[s, :split, :]
        down_ref[:, s * wb : (s + 1) * wb] = w_ref[s, split:, :]


def spread_out(w, ff):
    nb, total, wb = w.shape
    d = nb * wb
    return call(spread_out_body, (sds((total - ff, d), BF16), sds((ff, d), BF16)), (w,), us=4)


def prepare_body(n, down_ref, *refs):
    cots, out_ref = refs[:n], refs[n]
    for r in range(n):
        out_ref[r] = mm(cots[r][...], down_ref[...], NT).astype(BF16)


def prepare(down, cots):
    n = len(cots)
    return call(
        functools.partial(prepare_body, n),
        sds((n, cots[0].shape[0], down.shape[0]), BF16),
        (down, *cots),
    )


def widen_body(w_ref, wide_ref):
    nb, _, wb = w_ref.shape
    for s in range(nb):
        wide_ref[:, s * wb : (s + 1) * wb] = w_ref[s]


def widen(w):
    nb, total, wb = w.shape
    return call(widen_body, sds((total, nb * wb), BF16), (w,))


def mlp_body(first_ref, second_ref, dhid_ref, w_ref, dh_ref, hid_ref, dg_ref, du_ref):
    ff = hid_ref.shape[1]
    h2 = join_rows((first_ref, second_ref))
    gate_w, up_w = w_ref[0:ff, :], w_ref[ff : 2 * ff, :]
    dhid = dhid_ref[0].astype(F32)
    g = mm(h2, gate_w, NT)
    u = mm(h2, up_w, NT)
    sig = jax.nn.sigmoid(g)
    act = g * sig
    hid_ref[...] = (act * u).astype(BF16)
    dg = (dhid * u * sig * (1.0 + g * (1.0 - sig))).astype(BF16)
    du = (dhid * act).astype(BF16)
    dg_ref[...] = dg
    du_ref[...] = du
    dh_ref[...] = (mm(dg, gate_w) + mm(du, up_w)).astype(BF16)


def mlp(index, h2, dhid, w):
    half, d = h2[0].shape
    rows = 2 * half
    ff = w.shape[0] // 2
    return call(
        mlp_body,
        (sds((rows, d), BF16), *[sds((rows, ff), BF16)] * 3),
        (*h2, dhid, w),
        grid=(1,),
        in_specs=[whole((half, d))] * 2
        + [pl.BlockSpec((1, rows, ff), lambda r: (index, 0, 0)), whole((2 * ff, d))],
        out_specs=[whole((rows, d))] + [whole((rows, ff))] * 3,
    )


def mlp_out_body(n, w_ref, *refs):
    for r in range(n):
        refs[n + r][...] = mm(refs[r][...], w_ref[...]).astype(BF16)


def mlp_out(hid, w):
    n = len(hid)
    return call(
        functools.partial(mlp_out_body, n),
        [sds((hid[0].shape[0], w.shape[1]), BF16)] * n,
        (w, *hid),
    )


def down_grads_body(n, *refs):
    hid, cot, o_ref = refs[:n], refs[n : 2 * n], refs[2 * n]
    nb, _, wb = o_ref.shape
    acc = None
    for r in range(n):
        part = mm(hid[r][...], cot[r][...], TN)
        acc = part if acc is None else acc + part
    for s in range(nb):
        o_ref[s] = acc[:, s * wb : (s + 1) * wb].astype(BF16)


def down_grads(hid, cot, nb):
    n = len(hid)
    ff, d = hid[0].shape[1], cot[0].shape[1]
    return call(
        functools.partial(down_grads_body, n), sds((nb, ff, d // nb), BF16), (*hid, *cot), us=3
    )


def mlp_grads_body(n, *refs):
    h2 = grouped(refs[: 2 * n], n)
    dg, du, down_ref, o_ref = refs[2 * n : 3 * n], refs[3 * n : 4 * n], refs[4 * n], refs[4 * n + 1]
    nb, ff, wb = down_ref.shape
    for k, left in enumerate((dg, du)):
        acc = None
        for r in range(n):
            part = mm(left[r][...], join_rows(h2[r]), TN)
            acc = part if acc is None else acc + part
        acc = acc.astype(BF16)
        for s in range(nb):
            o_ref[s, k * ff : (k + 1) * ff, :] = acc[:, s * wb : (s + 1) * wb]
    for s in range(nb):
        o_ref[s, 2 * ff :, :] = down_ref[s]


def mlp_grads(h2, dg, du, down):
    n = len(h2)
    nb, ff, wb = down.shape
    return call(
        functools.partial(mlp_grads_body, n),
        sds((nb, 3 * ff, wb), BF16),
        (*flat(h2), *dg, *du, down),
        us=6,
    )


def turn_body(n, y1_ref, cot_ref, gain_ref, *refs):
    parts, w_ref = refs[:n], refs[n]
    dy1_ref, dgain_ref, *f_refs = refs[n + 1 : n + 4]
    do_ref = refs[n + 4]
    rows_of = do_ref.shape[2]
    dh2 = parts[0][...].astype(F32)
    for r in range(1, n):
        dh2 = dh2 + parts[r][...].astype(F32)
    y1 = y1_ref[...]
    scale = lax.rsqrt(jnp.mean(y1 * y1, axis=-1, keepdims=True) + EPS)
    normed = y1 * scale
    dgain_ref[...] = jnp.sum(dh2 * normed, axis=0, keepdims=True)
    dn = dh2 * gain_ref[1:2, :]
    inner = jnp.mean(dn * normed, axis=-1, keepdims=True)
    dy1 = cot_ref[...].astype(F32) + scale * (dn - normed * inner)
    dy1_ref[...] = dy1
    f = dy1.astype(BF16)
    give_rows(f_refs, f)
    for r in range(n):
        do_ref[r] = mm(f, w_ref[r * rows_of : (r + 1) * rows_of, :], NT).astype(BF16)


def turn(parts, y1, cot, gain, wo):
    n = len(parts)
    rows, d = y1.shape
    nv = wo.shape[0] // n
    res = call(
        functools.partial(turn_body, n),
        (
            sds((rows, d), F32),
            sds((1, d), F32),
            sds((rows, d), BF16),
            sds((n, rows, nv), BF16),
        ),
        (y1, cot, gain, *parts, wo),
    )
    return res


def back_first_body(do_ref, on_ref, inv_ref, qk_ref, masks_ref, d_ref, p_ref, z_ref):
    r = pl.program_id(0)
    n = pl.num_programs(0)
    nqk = qk_ref.shape[1]
    heads = nqk // (2 * FDIM)
    rows = do_ref.shape[1]

    @pl.when(r == 0)
    def _():
        z_ref[...] = jnp.zeros_like(z_ref)

    live = masks_ref[2:3, :]
    lane = lanes((rows, 128))
    for pair in range(heads // 2):
        cols = slice(pair * 128, (pair + 1) * 128)
        wide = do_ref[0, :, cols].astype(F32) * inv_ref[0, :, cols]
        dnum = wide.astype(BF16)
        prod = -(wide * on_ref[0, :, cols])
        high = prod.astype(BF16)
        low = (prod - high.astype(F32)).astype(BF16)
        both = []
        for j in range(2):
            i = 2 * pair + j
            row = lax.broadcasted_iota(jnp.int32, (128, 128), 0)
            hot = jnp.where((row < VDIM) if j == 0 else (row >= VDIM), 1.0, 0.0).astype(BF16)
            dden = mm(high, hot) + mm(low, hot)
            d_ref[0, i] = own_half(dnum, j, with_pair(dden, j))
            dh = dden.astype(BF16)
            dl = (dden - dh.astype(F32)).astype(BF16)
            zero = jnp.zeros_like(dh)
            spot = r * heads + i
            zext = jnp.where(lane == spot, dh, jnp.where(lane == spot + n * heads, dl, zero))
            q = qk_ref[0, i * FDIM : (i + 1) * FDIM, :].astype(F32)
            phi = (features(q) * live).astype(BF16)
            res = mm(phi, jnp.concatenate([dnum, zext], axis=1))
            both.append(res[:, :128])
            z_ref[...] += res[:, 128:]
        p_ref[r * (heads // 2) + pair] = own_half(both[0], 0, both[1]).astype(BF16)

    @pl.when(r == n - 1)
    def _():
        p_ref[p_ref.shape[0] - 1] = z_ref[...].astype(BF16)


def back_first(do, on, inv, qk, masks):
    n, nqk, rows = qk.shape
    heads = nqk // (2 * FDIM)
    pieces = n * heads // 2 + 1
    return call(
        back_first_body,
        (sds((n, heads, rows, 128), BF16), sds((pieces, FROWS, 128), BF16)),
        (do, on, inv, qk, masks),
        grid=(n,),
        in_specs=[by_row(x.shape[1:]) for x in (do, on, inv, qk)] + [whole(masks.shape)],
        out_specs=[by_row((heads, rows, 128)), whole((pieces, FROWS, 128))],
        scratch=[pltpu.VMEM((FROWS, 128), F32)],
    )


def back_local_body(d_ref, qk_ref, v_ref, masks_ref, c_ref, dq_ref, dk_ref, dv_ref):
    r = pl.program_id(0)
    nqk = qk_ref.shape[1]
    heads = nqk // (2 * FDIM)
    rows = v_ref.shape[1]
    masks = masks_ref[...]
    mask = doc_mask(masks, rows)
    live = masks[2:3, :]
    last = c_ref.shape[0] - 1
    for pair in range(heads // 2):
        cols = slice(pair * 128, (pair + 1) * 128)
        v_pair = v_ref[0, :, cols]
        c = c_ref[r * (heads // 2) + pair]
        dv = None
        for j in range(2):
            i = 2 * pair + j
            q = qk_ref[0, i * FDIM : (i + 1) * FDIM, :]
            k = qk_ref[0, nqk // 2 + i * FDIM : nqk // 2 + (i + 1) * FDIM, :]
            s1 = mm(q, k, TN) * 0.25 + 1.0
            a = jnp.where(mask, 0.5 * s1 * s1 + 0.5, 0.0).astype(BF16)
            d = d_ref[0, i]
            da = mm(d, with_ones(v_pair, j), NT)
            ds = jnp.where(mask, da * s1, 0.0).astype(BF16)
            z = moved_pair(c_ref[last].astype(F32), r * heads + i, j)
            dphi = mm(own_half(c, j, z), d, NT) * live
            back = features_back(q.astype(F32), dphi)
            dq_ref[0, i * FDIM : (i + 1) * FDIM, :] = (mm(k, ds, NT) * 0.25 + back).astype(BF16)
            dk_ref[0, i * FDIM : (i + 1) * FDIM, :] = mm(q, ds) * 0.25
            part = mm(own_half(d, j), a, TN)
            dv = part if dv is None else dv + part
        dv_ref[0, cols, :] = dv


def back_local(d, qk, v, masks, c):
    n, nqk, rows = qk.shape
    heads = nqk // (2 * FDIM)
    nv = heads * VDIM
    return call(
        back_local_body,
        (sds((n, nqk // 2, rows), BF16), sds((n, nqk // 2, rows), F32), sds((n, nv, rows), F32)),
        (d, qk, v, masks, c),
        grid=(n,),
        in_specs=[by_row(x.shape[1:]) for x in (d, qk, v)] + [whole(masks.shape), whole(c.shape)],
        out_specs=[by_row((nqk // 2, rows)), by_row((nqk // 2, rows)), by_row((nv, rows))],
    )


def back_last_body(
    where_ref, dq_ref, dk_ref, dv_ref, qk_ref, v_ref, masks_ref, one_ref, two_ref, h1_ref, wt_ref,
    gain_ref, x_ref, dy1_ref, dgain_mlp_ref, grad_ref, *refs,
):
    *dw_refs, dgain_ref, z_ref, acc_ref, wide_ref = refs
    r = pl.program_id(0)
    n = pl.num_programs(0)
    nqk = qk_ref.shape[1]
    heads = nqk // (2 * FDIM)
    nb, wb = dw_refs[0].shape[1] * len(dw_refs), dw_refs[0].shape[3]
    last = one_ref.shape[0] - 1
    flag = masks_ref[4:5, 0:128]
    tail = masks_ref[1:2, :]

    @pl.when(r == 0)
    def _():
        z_ref[...] = joined(one_ref[last], two_ref[last], flag)
        acc_ref[...] = jnp.zeros_like(acc_ref)

    dks, dvs = [], []
    for pair in range(heads // 2):
        cols = slice(pair * 128, (pair + 1) * 128)
        at = r * (heads // 2) + pair
        dp = joined(one_ref[at], two_ref[at], flag).astype(BF16)
        v_pair = v_ref[0, :, cols]
        dv = dv_ref[0, cols, :]
        for j in range(2):
            i = 2 * pair + j
            k = qk_ref[0, nqk // 2 + i * FDIM : nqk // 2 + (i + 1) * FDIM, :].astype(F32)
            z = moved_pair(z_ref[...], r * heads + i, j)
            dphi = mm(own_half(dp, j, z), with_ones(v_pair, j), NT) * tail
            dk = dk_ref[0, i * FDIM : (i + 1) * FDIM, :] + features_back(k, dphi)
            dks.append(dk.astype(BF16))
            phi = (features(k) * tail).astype(BF16)
            dv = dv + mm(own_half(dp, j), phi, TN)
        dvs.append(dv.astype(BF16))
    d = jnp.concatenate([dq_ref[0]] + dks + dvs, axis=0)
    total = d.shape[0]
    wide_ref[...] = mm(d, h1_ref[...]).astype(BF16)
    give_blocks(where_ref, wide_ref, [one.at[r, :, 0:total, :] for one in dw_refs])
    acc_ref[...] += mm(d, wt_ref[0], TN)

    @pl.when(r == n - 1)
    def _():
        dh1 = acc_ref[...]
        x = x_ref[...].astype(F32)
        scale = lax.rsqrt(jnp.mean(x * x, axis=-1, keepdims=True) + EPS)
        normed = x * scale
        dgain_ref[0:1, :] = jnp.sum(dh1 * normed, axis=0, keepdims=True)
        dgain_ref[1:2, :] = dgain_mlp_ref[...]
        dn = dh1 * gain_ref[0:1, :]
        inner = jnp.mean(dn * normed, axis=-1, keepdims=True)
        grad_ref[...] = dy1_ref[...] + scale * (dn - normed * inner)
        if nb > 1:
            groups, count = dw_refs[0].shape[:2]
            across = groups * nb * wb // dgain_ref.shape[1]
            tiles = nb // across
            for q in range(groups):
                for z in range(count):
                    at = where_ref[q] * tiles + (where_ref[groups + 1] ^ z) * 2 // across
                    both = dgain_ref[:, pl.ds(pl.multiple_of(at * wb, wb), wb)]
                    high = both.astype(BF16).astype(F32)
                    fill = jnp.zeros((dw_refs[0].shape[2] - total - 4, wb), F32)
                    block = jnp.concatenate([high, both - high, fill], axis=0).astype(BF16)
                    for one in dw_refs:
                        one[q, z, total:, :] = block


def give_blocks(where_ref, wide_ref, refs):
    count, _, wb = refs[0].shape
    last = where_ref.shape[0] - 1
    for index, one in enumerate(refs):
        for z in range(count):
            at = 0
            if len(refs) == 2:
                core = where_ref[last - 1]
                side = core if index == 0 else 1 - core
                at = pl.multiple_of(((where_ref[last] ^ z) * 2 + side) * wb, wb)
            one[z] = wide_ref[:, pl.ds(at, wb)]


def back_last(where, dq, dk, dv, qk, v, masks, one, two, h1, w, gain, x, dy1, dgain_mlp, nb):
    n, nqk, rows = qk.shape
    _, total, d = w.shape
    shapes = [(n, 1, total + 16, d)] if nb == 1 else [(n, nb // 2, total + 16, d // nb)] * 2
    ins = (where, dq, dk, dv, qk, v, masks, one, two, h1, w, gain, x, dy1, dgain_mlp)
    return call(
        back_last_body,
        (sds((rows, d), F32), *[sds(shape, BF16) for shape in shapes], sds((2, d), F32)),
        ins,
        grid=(n,),
        in_specs=[pl.BlockSpec(memory_space=pltpu.SMEM)]
        + [by_row(y.shape[1:]) for y in (dq, dk, dv, qk, v)]
        + [whole(y.shape) for y in (masks, one, two, h1)]
        + [by_row(w.shape[1:])]
        + [whole(y.shape) for y in (gain, x, dy1, dgain_mlp)],
        out_specs=[whole((rows, d)), *[whole(shape) for shape in shapes], whole((2, d))],
        scratch=[
            pltpu.VMEM((FROWS, 128), F32),
            pltpu.VMEM((rows, d), F32),
            pltpu.VMEM((total, d), BF16),
        ],
        us=10,
        most=True,
    )


def out_grads_body(n, where_ref, f_ref, *refs):
    o_ref, outs, wide_ref = refs[0], refs[1:-1], refs[-1]
    for r in range(n):
        wide_ref[...] = mm(o_ref[r], f_ref[...], TN).astype(BF16)
        give_blocks(where_ref, wide_ref, [one.at[r] for one in outs])


def out_grads(where, o, f, nb):
    n, _, nv = o.shape
    d = f.shape[1]
    shapes = [(n, 1, nv, d)] if nb == 1 else [(n, nb // 2, nv, d // nb)] * 2
    return call(
        functools.partial(out_grads_body, n),
        [sds(shape, BF16) for shape in shapes],
        (where, f, o),
        scratch=[pltpu.VMEM((nv, d), BF16)],
        smem=1,
        us=3,
    )


def xor_pairs(size, r):
    return [(i, i ^ r) for i in range(size)]


def swap(parts):
    size = lax.axis_size("head")
    return [parts[0]] + [lax.ppermute(parts[r], "head", xor_pairs(size, r)) for r in range(1, size)]


def halves(x):
    return [x[: x.shape[0] // 2], x[x.shape[0] // 2 :]]


def sum_parts(parts):
    total = parts[0].astype(F32)
    for part in parts[1:]:
        total = total + part.astype(F32)
    return total.astype(parts[0].dtype)


def spread(x):
    return [[one] for one in swap([x] * lax.axis_size("head"))]


def spread_halves(pair):
    size = lax.axis_size("head")
    a, b = pair

    def send(x, r):
        return lax.ppermute(x, "head", xor_pairs(size, r))

    if size != 4:
        return [[a, b]] + [[send(a, r), send(b, r)] for r in range(1, size)]
    ax, by = send(a, 1), send(b, 2)
    ay, bx = send(a, 2), send(b, 1)
    return [[a, b], [ax, bx], [ay, by], [send(ax, 2), send(by, 1)]]


def shifted(x, step):
    size = lax.axis_size("seq")
    return lax.ppermute(x, "seq", [(i, i + step) for i in range(size) if 0 <= i + step < size])


def over_z(x):
    count, size = x.shape[0], lax.axis_size("seq")
    if count <= 4:
        parts = [lax.ppermute(x[k], "seq", xor_pairs(size, 2 * k)) for k in range(1, count)]
        total = x[0].astype(F32)
        for part in parts:
            total = total + part.astype(F32)
        return total
    while count > 1:
        count //= 2
        got = lax.ppermute(x[count:], "seq", xor_pairs(size, 2 * count))
        x = (x[:count].astype(F32) + got.astype(F32)).astype(x.dtype)
    return x[0].astype(F32)


def carried(x, labels, step, join, before):
    size, me = lax.axis_size("seq"), lax.axis_index("seq")
    reach = max(size // 4, 1)
    k = 1
    while 2 * k < reach:
        other = jnp.take(labels, jnp.clip(me - step * k, 0, size - 1))
        flag = (other == jnp.take(labels, me)).astype(F32)
        x = join(x, shifted(x, step * k), flag)
        k *= 2
    one = shifted(x, step)
    one, before = lax.optimization_barrier((one, before))
    return one, shifted(one, step * k)


def on_device(
    tokens, doc_ids, query_weight, key_weight, value_weight, out_weight,
    gate_weight, up_weight, down_weight, mix_gain, mlp_gain, cotangent,
):
    n, blocks = lax.axis_size("head"), lax.axis_size("seq")
    here, me = lax.axis_index("head"), lax.axis_index("seq")
    rows, d = tokens.shape[1:]
    wb = d // blocks
    nb = blocks if wb % 128 == 0 else 1
    heads = query_weight.shape[1] // FDIM
    nqkv = 2 * heads * FDIM + heads * VDIM
    nv = heads * VDIM
    ff = gate_weight.shape[1]
    x, cot = tokens[0], cotangent[0]

    piece = mix_gain.shape[0]
    doc_rows = rows // wb
    extra = -(-(2 + doc_rows) // 16) * 16
    pack = call(
        pack_body,
        sds((nqkv + extra, wb), BF16),
        (
            query_weight.T, key_weight.T, value_weight, mix_gain.reshape(1, -1), mlp_gain.reshape(1, -1),
            doc_ids.reshape(doc_rows, wb),
        ),
        us=2,
        most=True,
    )
    out_slices = swap([out_weight] * n)
    pack = lax.all_gather(pack, "seq")
    near_cots = [lax.ppermute(cot, "head", xor_pairs(n, r)) for r in range(1, n - 1)]
    near_cots, pack = lax.optimization_barrier((near_cots, pack))
    def gathered(w):
        return w if nb == blocks else jnp.transpose(w, (1, 0, 2)).reshape(1, w.shape[1], d)

    def unblocked(w):
        if nb == blocks:
            return w
        w = w.reshape(w.shape[1:-1] + (blocks, wb))
        return jnp.moveaxis(w, -2, 0)

    core = (me % 2).reshape(1)
    where = jnp.concatenate([here ^ jnp.arange(n, dtype=jnp.int32), core, (me // 2).reshape(1)])
    half = blocks // 2
    mine = lax.dynamic_slice_in_dim(pack, core[0] * half, half)
    other = lax.dynamic_slice_in_dim(pack, (1 - core[0]) * half, half)
    down_late, mine = lax.optimization_barrier((down_weight, mine))
    second = lax.all_gather(jnp.concatenate([*out_slices, down_late], axis=0), "seq")

    docs = pack[:, nqkv + 2 : nqkv + 2 + doc_rows].reshape(blocks, rows).astype(F32)
    segs = jnp.take(docs, me, axis=0)
    lasts = docs[:, -1]
    before = jnp.where(me > 0, jnp.take(lasts, jnp.maximum(me - 1, 0)), -1.0)
    final_label = jnp.take(lasts, me)
    labels_back = jnp.concatenate([jnp.full((1,), -1.0), lasts[:-1]])

    def flag_of(labels, step):
        reach = max(blocks // 4, 1)
        k = 1
        while 2 * k < reach:
            k *= 2
        near = jnp.take(labels, jnp.clip(me - step, 0, blocks - 1))
        far = jnp.take(labels, jnp.clip(me - step * (1 + k), 0, blocks - 1))
        return (near == far).astype(F32)

    masks = jnp.stack(
        [
            segs,
            (segs == final_label).astype(F32),
            (segs == before).astype(F32),
            jnp.full((rows,), 1.0) * flag_of(lasts, 1),
            jnp.full((rows,), 1.0) * flag_of(labels_back, -1),
        ]
        + [jnp.zeros_like(segs)] * 3
    )

    mine = swap([mine] * n)
    mine[1], masks = lax.optimization_barrier((mine[1], masks))
    pairs = [[mine[0], other]]
    pairs += [[one, lax.ppermute(one, "seq", xor_pairs(blocks, 1))] for one in mine[1:]]
    if nb == blocks:
        gain_in = jnp.zeros((8, 128), F32)
    else:
        small = jnp.stack([jnp.stack([one[:, nqkv : nqkv + 2, :piece] for one in pair]) for pair in pairs])
        small = jnp.take(jnp.take(small, here ^ jnp.arange(n), axis=0), core[0] ^ jnp.arange(2), axis=1)
        gain_in = jnp.transpose(small.reshape(n, blocks, 2, piece), (2, 0, 1, 3)).reshape(2, d)
        gain_in = jnp.pad(gain_in.astype(F32), ((0, 6), (0, 0)))
    if nb != blocks:
        pairs = [
            [gathered(jnp.where(core[0] == 0, jnp.concatenate(p), jnp.concatenate(p[::-1])))] for p in pairs
        ]
    cot_late, pairs[1:] = lax.optimization_barrier((cot, pairs[1:]))
    wide = call(pack_two_body, sds((2 * ff, wb), BF16), (gate_weight.T, up_weight.T), us=2)

    def join(a, b, flag):
        return (a.astype(F32) + b.astype(F32) * flag).astype(BF16)

    h1, qk, v, sums, w_qkv, gains = project(
        where, x, gain_in, masks, pairs, heads, piece if nb == blocks else 0
    )
    cots = [cot, *near_cots, lax.ppermute(cot_late, "head", xor_pairs(n, n - 1))]
    nd = local(qk, v, masks)
    one, two = carried(sums, lasts, 1, join, nd)
    w_out, w_down = spread_out(gathered(second), ff)
    wide, one = lax.optimization_barrier((wide, one))
    w_mlp = widen(gathered(lax.all_gather(wide, "seq")))
    dhid = prepare(w_down, cots)
    o, on, inv, c = carry(nd, qk, masks, one, two)
    y1, h2 = middle(x, o, w_out, gains)
    h2s = spread_halves(h2)
    res = [None] * n
    held = h2s[n - 1]
    for r in range(n - 1, -1, -1):
        res[r] = mlp(r, held, dhid, w_mlp)
        if r:
            held, res[r] = lax.optimization_barrier((list(h2s[r - 1]), list(res[r])))
    dparts, hid, dg, du = ([t[k] for t in res] for k in range(4))
    dparts = swap(dparts)
    oparts = mlp_out(hid, w_down)
    ddown = down_grads(hid, cots, nb)
    dparts, oparts, ddown = lax.optimization_barrier((dparts, oparts, ddown))
    dy1, dgain_mlp, f, do = turn(dparts, y1, cot, gains, w_out)
    dext, dsums = back_first(do, on, inv, qk, masks)
    dg, du, dsums = lax.optimization_barrier((dg, du, dsums))
    dmlp = mlp_grads(h2s, dg, du, ddown)
    dq, dk, dv = back_local(dext, qk, v, masks, c)
    back_one, back_two = carried(dsums, labels_back, -1, join, (dq, dk, dv))

    def split(w):
        if nb == blocks:
            return w
        w = unblocked(w[0][:, 0][None])
        w = jnp.moveaxis(w.reshape((half, 2) + w.shape[1:]), 2, 0)
        w = jnp.take(w, (me // 2) ^ jnp.arange(half), axis=1)
        return [lax.dynamic_index_in_dim(w, bit, 2, keepdims=False) for bit in (core[0], 1 - core[0])]

    def pooled(keep, give):
        got = lax.ppermute(give, "seq", xor_pairs(blocks, 1))
        return [(keep[r].astype(F32) + got[r].astype(F32)).astype(BF16) for r in range(n)]

    dout = sum_parts(swap(pooled(*split(out_grads(where, o, f, nb)))))
    dmlp, back_two, dout = lax.optimization_barrier((dmlp, back_two, dout))
    dmlp = lax.psum_scatter(unblocked(dmlp), "seq", tiled=True)[0].astype(F32)
    grad_tokens, *dqkv, dgains = back_last(
        where, dq, dk, dv, qk, v, masks, back_one, back_two, h1, w_qkv, gains, x, dy1, dgain_mlp, nb
    )
    near = [lax.ppermute(oparts[r], "head", xor_pairs(n, r)) for r in range(1, n - 1)]
    near, dqkv = lax.optimization_barrier((near, dqkv))
    dqkv = pooled(*split(dqkv))
    far = lax.ppermute(oparts[n - 1], "head", xor_pairs(n, n - 1))
    if FAR:
        far, dqkv = lax.optimization_barrier((far, dqkv))
    dqkv = over_z(sum_parts(swap(dqkv)))
    oparts = [oparts[0], *near, far]
    dout = over_z(dout)
    if nb == blocks:
        parts = dqkv[nqkv : nqkv + 2] + dqkv[nqkv + 2 : nqkv + 4]
        total = lax.dynamic_slice_in_dim(parts, me % (wb // piece) * piece, piece, axis=1)
    else:
        total = lax.psum_scatter(dgains, ("head", "seq"), scatter_dimension=1, tiled=True)
    output = y1
    for part in oparts:
        output = output + part.astype(F32)

    kq = heads * FDIM
    return (
        output.astype(BF16)[None],
        grad_tokens[None],
        dqkv[:kq].T,
        dqkv[kq : 2 * kq].T,
        dqkv[2 * kq : nqkv].T,
        dout,
        dmlp[:ff].T,
        dmlp[ff : 2 * ff].T,
        dmlp[2 * ff :],
        total[0],
        total[1],
    )


def solution(mesh):
    placed = (
        P("head", "seq", None),
        P("head", "seq"),
        P("seq", "head"),
        P("seq", "head"),
        P("seq", "head"),
        P("head", "seq"),
        P("seq", "head"),
        P("seq", "head"),
        P("head", "seq"),
        P(("head", "seq")),
        P(("head", "seq")),
        P("head", "seq", None),
    )
    return jax.shard_map(
        on_device,
        mesh=mesh,
        in_specs=placed,
        out_specs=(
            P("head", "seq", None),
            P("head", "seq", None),
            P("seq", "head"),
            P("seq", "head"),
            P("seq", "head"),
            P("head", "seq"),
            P("seq", "head"),
            P("seq", "head"),
            P("head", "seq"),
            P(("head", "seq")),
            P(("head", "seq")),
        ),
        check_vma=False,
    )
```
